512 devices in a mesh: space: 64 (over z, y), dp: 8 (over x, core).
Axes of the slice: x: 4, y: 4, z: 16, core: 2. Of those that a mesh axis runs over, the one named last changes fastest.
Arguments:
- features: bfloat16 [8, 256, 4096], P('dp', 'space'), may hold values from -6 to 6
- sources: int32 [8, 256, 27], P('dp', 'space'), may hold values from 0 to 255, as said below
- voxels: int32 [8, 256, 1728], P('dp', 'space'), may hold values from 0 to 64, as said below
- cotangent: bfloat16 [8, 256, 4096], P('dp', 'space'), may hold values from -6 to 6
- weight_one: bfloat16 [27, 64, 64], replicated, may hold values from -0.15625 to 0.15625
- weight_two: bfloat16 [27, 64, 64], replicated, may hold values from -0.15625 to 0.15625
Outputs:
- conv_out: bfloat16 [8, 256, 4096], P('dp', 'space')
- grad_input: bfloat16 [8, 256, 4096], P('dp', 'space')
- grad_one: float32 [27, 64, 64], replicated
- grad_two: float32 [27, 64, 64], replicated
The draws below stay inside these ranges and needn't reach their ends.
Inputs may be any that keep to these rules, and one draw needn't show every extreme that they name: `sources`: block b lies in slab b // 4. Each source block lies in the reader's own slab, or among the last 2 blocks of the slab before, or among the first 2 blocks of the slab after; every such boundary block is read by the neighbouring slab. Offset 27 // 2 reads the block itself. `voxels`: offset 27 // 2 maps every voxel to itself; the value 64 marks a voxel with no neighbour at that offset.
All inputs are finite; a program needn't handle non-finite values.
Results may differ from the reference program's by a relative error of at most 0.009.
Values may be sent and summed in bfloat16 or wider, within the bound.
A program may use at most 64 MiB of HBM per device.

```python
import jax
import jax.numpy as jnp

C = 64
V = 64
K = 27
HALO = 2
BLK = 4
BLOCKS = 256
SCENES = 8


def draw_sources(key, part):
    key = jax.random.fold_in(key, 11)
    slabs = BLOCKS // BLK
    keys = jax.random.split(key, 3)
    block_ids = jnp.arange(BLOCKS, dtype=jnp.int32)
    place = (block_ids % BLK)[None, :, None]
    slab = (block_ids // BLK)[None, :, None]
    offsets = jnp.arange(K, dtype=jnp.int32)[None, None, :]
    jitter = jax.random.randint(keys[0], (SCENES, BLOCKS, K), -3, 4)
    coin = jax.random.randint(keys[1], (SCENES, BLOCKS, K), 0, 3)
    pick = jax.random.randint(keys[2], (SCENES, BLOCKS, K), 0, HALO)
    near = jnp.clip(place + jitter, 0, BLK - 1) + slab * BLK
    left_ok = (place < HALO) & (slab > 0)
    right_ok = (place >= BLK - HALO) & (slab < slabs - 1)
    left_src = (slab - 1) * BLK + BLK - HALO + jnp.where(offsets == 0, place, pick)
    right_src = (slab + 1) * BLK + jnp.where(offsets == K - 1, place - (BLK - HALO), pick)
    use_left = left_ok & ((coin == 0) | (offsets == 0))
    use_right = right_ok & ((coin == 0) | (offsets == K - 1))
    chosen = jnp.where(use_left, left_src, jnp.where(use_right, right_src, near))
    chosen = jnp.where(offsets == K // 2, slab * BLK + place, chosen)
    return chosen.astype(jnp.int32)


def draw_voxels(key, part):
    key = jax.random.fold_in(key, 12)
    raw = jax.random.randint(key, (SCENES, BLOCKS, K, V), 0, V + V // 2)
    raw = jnp.minimum(raw, V)
    centre = jnp.arange(V, dtype=jnp.int32)[None, None, None, :]
    offsets = jnp.arange(K, dtype=jnp.int32)[None, None, :, None]
    chosen = jnp.where(offsets == K // 2, centre, raw)
    return chosen.reshape(SCENES, BLOCKS, K * V).astype(jnp.int32)


def level_of(stream_key, shape, cuts, low, largest):
    gain = 1.0
    for position, parts in cuts:
        draws = jax.random.uniform(jax.random.fold_in(jax.random.fold_in(stream_key, 6), position), (parts,), jnp.float32, low / len(cuts), largest / len(cuts))
        gain = gain * jnp.repeat(jnp.exp(draws), shape[position] // parts).reshape((-1,) + (1,) * (len(shape) - 1 - position))
    return gain


def scatter_about(rng, dims, deviation, limit, shards=(), held_as=jnp.bfloat16):
    factor_of = level_of(rng, dims, shards, -0.22, 0.18) if shards else 1.0
    values = jax.random.normal(rng, dims, jnp.float32) * deviation * factor_of
    return jnp.minimum(jnp.maximum(values, -limit), limit).astype(held_as)


def setup_inputs(seed: int = 0) -> dict:
    key_of = jax.random.split(jax.random.key(seed), 7)
    return {
        "features": scatter_about(key_of[0], (SCENES, BLOCKS, V * C), 1.0, 6.0, ((0, 8), (1, 64))),
        "sources": draw_sources(jax.random.fold_in(key_of[6], 71), 0),
        "voxels": draw_voxels(jax.random.fold_in(key_of[6], 71), 0),
        "cotangent": scatter_about(key_of[3], (SCENES, BLOCKS, V * C), 1.0, 6.0, ((0, 8), (1, 64))),
        "weight_one": scatter_about(key_of[4], (K, C, C), (K * C) ** -0.5, 0.15625),
        "weight_two": scatter_about(key_of[5], (K, C, C), (K * C) ** -0.5, 0.15625),
    }


def pad_table(field, count):
    shaped = field.reshape(count, V, C)
    shaped = jnp.pad(shaped, ((0, 0), (0, 1), (0, 0)))
    return shaped.reshape(count * (V + 1), C)


def strip_table(table, count):
    return table.reshape(count, V + 1, C)[:, :V].reshape(count * V, C)


def conv_forward(table, rows, weight):
    picked = jnp.take(table, rows, axis=0).astype(jnp.float32)
    return jnp.einsum("knc,kcd->nd", picked, weight.astype(jnp.float32))


def conv_backward(table, rows, weight, grad):
    picked = jnp.take(table, rows, axis=0).astype(jnp.float32)
    grad_wide = grad.astype(jnp.float32)
    wgrads = jnp.einsum("knc,nd->kcd", picked, grad_wide)
    back = jnp.einsum("nd,kcd->knc", grad_wide, weight.astype(jnp.float32))
    start = jnp.zeros((table.shape[0], C), jnp.float32)
    accum = start.at[rows.reshape(-1)].add(back.reshape(-1, C))
    return wgrads, accum


def slope(pre):
    sig = jax.nn.sigmoid(pre)
    return sig * (1.0 + pre * (1.0 - sig))


def one_scene(feat, sources, voxels, cotangent, weight_one, weight_two):
    vox = voxels.reshape(BLOCKS, K, V)
    rows = sources[:, :, None] * (V + 1) + vox
    rows = jnp.transpose(rows, (1, 0, 2)).reshape(K, BLOCKS * V).astype(jnp.int32)
    table_in = pad_table(feat, BLOCKS)
    pre = conv_forward(table_in, rows, weight_one)
    hidden = jax.nn.silu(pre).astype(jnp.bfloat16)
    table_hidden = pad_table(hidden, BLOCKS)
    conv_out = conv_forward(table_hidden, rows, weight_two).astype(jnp.bfloat16)
    grad_out = cotangent.reshape(BLOCKS * V, C)
    part_two, back_hidden = conv_backward(table_hidden, rows, weight_two, grad_out)
    grad_hidden = strip_table(back_hidden, BLOCKS)
    grad_pre = (grad_hidden * slope(pre)).astype(jnp.bfloat16)
    part_one, back_in = conv_backward(table_in, rows, weight_one, grad_pre)
    grad_input = strip_table(back_in, BLOCKS).astype(jnp.bfloat16)
    return conv_out.reshape(BLOCKS, V * C), grad_input.reshape(BLOCKS, V * C), part_one, part_two


def reference(features, sources, voxels, cotangent, weight_one, weight_two):
    outs = []
    grads = []
    total_one = jnp.zeros((K, C, C), jnp.float32)
    total_two = jnp.zeros((K, C, C), jnp.float32)
    for scene in range(SCENES):
        conv_out, grad_input, part_one, part_two = one_scene(features[scene], sources[scene], voxels[scene], cotangent[scene], weight_one, weight_two)
        outs.append(conv_out)
        grads.append(grad_input)
        total_one = total_one + part_one
        total_two = total_two + part_two
    factor = float(SCENES * BLOCKS * V) ** -0.5
    return jnp.stack(outs), jnp.stack(grads), total_one * factor, total_two * factor
```

```python
import functools

import jax
import jax.numpy as jnp
from jax import lax
from jax.experimental import pallas as pl
from jax.experimental.pallas import tpu as pltpu
from jax.sharding import PartitionSpec as P

C = 64
V = 64
K = 27
HALO = 2
Y = 4
ZPAR = 2
TILE = 16
TILES = K * C * C // (TILE * 2 * C)
MESH = pl.DeviceIdType.MESH
BF16 = jnp.bfloat16
F32 = jnp.float32


def mxu(a, b, dims=((1,), (0,))):
    return lax.dot_general(a, b, (dims, ((), ())), preferred_element_type=F32)


def step_kernel(
    sizes,
    feat_ref,
    cot_ref,
    rows_ref,
    w1_ref,
    w2_ref,
    conv_ref,
    gin_ref,
    sums_ref,
    hots,
    picked1,
    picked2,
    back,
    w1t,
    w2t,
    halo_in,
    halo_mid,
    rim_out,
    rim_in,
    hidden,
    parts,
    got1,
    mid,
    got2,
    got3,
    whole2,
    halo_send,
    halo_recv,
    group_send,
    group_recv,
):
    space, dp, planes, deep = sizes
    n = feat_ref.shape[1]
    half = n // 2
    t1 = parts.shape[1] // dp
    t2 = mid.shape[1] // planes
    s = lax.axis_index("space")
    d = lax.axis_index("dp")
    y = s % Y
    z = s // Y
    plane = (z % ZPAR) * Y + y
    depth = z // ZPAR

    def at_dp(i):
        return (s, i)

    def at_plane(i):
        return (((z // ZPAR) * ZPAR + i // Y) * Y + i % Y, d)

    def at_depth(i):
        return ((i * ZPAR + z % ZPAR) * Y + y, d)

    before = ((s + space - 1) % space, d)
    after = ((s + 1) % space, d)

    barrier = pltpu.get_barrier_semaphore()
    partners = [before, after]
    for group, me, at in ((dp, d, at_dp), (planes, plane, at_plane), (deep, depth, at_depth)):
        partners += [at((me + j) % group) for j in range(1, group)]
    for partner in partners:
        pl.semaphore_signal(barrier, inc=1, device_id=partner, device_id_type=MESH)

    def remote(src, dst, send, recv, target):
        return pltpu.make_async_remote_copy(
            src_ref=src, dst_ref=dst, send_sem=send, recv_sem=recv, device_id=target, device_id_type=MESH
        )

    spot = lax.broadcasted_iota(jnp.int32, (2 * n, n), 0)

    def build(k, carry):
        row = rows_ref[k]
        hot = jnp.where(spot == row, 1.0, 0.0).astype(BF16)
        hots[:, pl.ds(pl.multiple_of(k * n, n), n)] = hot
        return carry

    lax.fori_loop(0, K, build, 0)

    group_of = 9

    def spread(w_ref, grad):
        for g in range(0, K, group_of):
            out = mxu(w_ref[g * C : (g + group_of) * C, :], grad).astype(BF16)
            for k in range(group_of):
                back[:, (g + k) * n : (g + k + 1) * n] = out[k * C : (k + 1) * C, :]

    def scattered(lo, hi):
        def some(g, total):
            lanes = pl.ds(pl.multiple_of(g * group_of * n, group_of * n), group_of * n)
            return total + mxu(back[:, lanes], hots[lo:hi, lanes], ((1,), (1,)))

        return lax.fori_loop(0, K // group_of, some, jnp.zeros((C, hi - lo), F32))

    def pick_own(table, picked):
        def one(g, carry):
            for i in range(group_of):
                k = g * group_of + i
                lanes = pl.ds(pl.multiple_of(k * n, n), n)
                picked[k] = mxu(table, hots[0:n, lanes]).astype(BF16)
            return carry

        lax.fori_loop(0, K // group_of, one, 0)

    def pick_halo(table, picked):
        def one(g, carry):
            for i in range(group_of):
                k = g * group_of + i
                lanes = pl.ds(pl.multiple_of(k * n, n), n)
                more = mxu(table, hots[n : 2 * n, lanes])
                picked[k] = (picked[k].astype(F32) + more).astype(BF16)
            return carry

        lax.fori_loop(0, K // group_of, one, 0)

    def convolved(wt, picked):
        return mxu(wt[...], picked[...].reshape(K * C, n))

    def weight_parts(which, picked, grad):
        zero = jnp.zeros((C, n), BF16)
        pair = jnp.concatenate(
            [jnp.concatenate([grad, zero], axis=1), jnp.concatenate([zero, grad], axis=1)], axis=0
        )
        for g in range(0, K, group_of):
            both = jnp.concatenate(
                [picked[g : g + group_of, 0 : C // 2, :], picked[g : g + group_of, C // 2 : C, :]], axis=2
            ).reshape(group_of * C // 2, 2 * n)
            out = mxu(both, pair, ((1,), (1,))).astype(BF16)
            tiles = group_of * C // 2 // TILE
            parts[which, g * 2 : g * 2 + tiles] = out.reshape(tiles, TILE, 2 * C)

    def to_neighbours(slot, low, high, into):
        copies = [
            remote(low, into.at[1], halo_send.at[slot, 0], halo_recv.at[slot, 1], before),
            remote(high, into.at[0], halo_send.at[slot, 1], halo_recv.at[slot, 0], after),
        ]
        for copy in copies:
            copy.start()
        return copies

    def arrive(copies):
        for copy in copies:
            copy.wait_recv()

    def to_group(stage, which, group, me, at, src_of, dst):
        copies = []
        for j in range(1, group):
            other = (me + j) % group
            copy = remote(
                src_of(other),
                dst,
                group_send.at[stage, which, j - 1],
                group_recv.at[stage, which, j - 1],
                at(other),
            )
            copy.start()
            copies.append(copy)
        return copies

    feat = feat_ref[...]
    cot = cot_ref[...]
    w1t[...] = w1_ref[...].T
    w2t[...] = w2_ref[...].T
    for which in range(2):
        parts[which, TILES:] = jnp.zeros((parts.shape[1] - TILES, TILE, 2 * C), BF16)
        mid[which, t1:] = jnp.zeros((mid.shape[1] - t1, TILE, 2 * C), BF16)
    spread(w2_ref, cot)
    rim = scattered(n, 2 * n).astype(BF16)
    for i in range(2):
        rim_out[0, i] = rim[:, i * half : (i + 1) * half]

    pl.semaphore_wait(barrier, len(partners))

    sent = []
    feat_copies = to_neighbours(0, feat_ref.at[:, 0:half], feat_ref.at[:, half:n], halo_in)
    rim_copies = to_neighbours(1, rim_out.at[0, 0], rim_out.at[0, 1], rim_in.at[0])
    sent += feat_copies + rim_copies

    pick_own(feat, picked1)
    grad_hidden = scattered(0, n)

    arrive(feat_copies)
    pick_halo(jnp.concatenate([halo_in[0], halo_in[1]], axis=1), picked1)
    pre = convolved(w1t, picked1)
    sig = 1.0 / (1.0 + jnp.exp(-pre))
    hid = (pre * sig).astype(BF16)
    hidden[...] = hid
    hid_copies = to_neighbours(2, hidden.at[:, 0:half], hidden.at[:, half:n], halo_mid)
    sent += hid_copies

    arrive(rim_copies)
    rims = jnp.concatenate([rim_in[0, 0], rim_in[0, 1]], axis=1).astype(F32)
    grad_pre = ((grad_hidden + rims) * (sig * (1.0 + pre * (1.0 - sig)))).astype(BF16)
    weight_parts(0, picked1, grad_pre)

    def scatter_reduce_1(which):
        return to_group(
            0,
            which,
            dp,
            d,
            at_dp,
            lambda other: parts.at[which, pl.ds(other * t1, t1)],
            got1.at[which, d],
        )

    def scatter_reduce_2(which, copies):
        arrive(copies)
        got1[which, d] = parts[which, pl.ds(d * t1, t1)]
        total = got1[which, 0].astype(F32)
        for i in range(1, dp):
            total = total + got1[which, i].astype(F32)
        mid[which, 0:t1] = total.astype(BF16)
        return to_group(
            1,
            which,
            planes,
            plane,
            at_plane,
            lambda other: mid.at[which, pl.ds(other * t2, t2)],
            got2.at[which, plane],
        )

    def reduce_3(which, copies):
        arrive(copies)
        got2[which, plane] = mid[which, pl.ds(plane * t2, t2)]
        total = got2[which, 0].astype(F32)
        for i in range(1, planes):
            total = total + got2[which, i].astype(F32)
        got3[which, depth] = total.astype(BF16)
        return to_group(2, which, deep, depth, at_depth, lambda other: got3.at[which, depth], got3.at[which, depth])

    def gather_2(which, copies):
        arrive(copies)
        total = got3[which, 0].astype(F32)
        for i in range(1, deep):
            total = total + got3[which, i].astype(F32)
        mine = pl.ds(plane * t2, t2)
        whole2[which, mine] = total.astype(BF16)
        return to_group(
            3, which, planes, plane, at_plane, lambda other: whole2.at[which, mine], whole2.at[which, mine]
        )

    def gather_1(which, copies):
        arrive(copies)
        mine = whole2.at[which, 0:t1]
        sums_ref[which, d] = whole2[which, 0:t1]
        return to_group(4, which, dp, d, at_dp, lambda other: mine, sums_ref.at[which, d])

    one = scatter_reduce_1(0)
    sent += one

    pick_own(hid, picked2)
    arrive(hid_copies)
    pick_halo(jnp.concatenate([halo_mid[0], halo_mid[1]], axis=1), picked2)
    weight_parts(1, picked2, cot)
    two = scatter_reduce_1(1)
    sent += two

    spread(w1_ref, grad_pre)
    rim = scattered(n, 2 * n).astype(BF16)
    for i in range(2):
        rim_out[1, i] = rim[:, i * half : (i + 1) * half]
    last_copies = to_neighbours(3, rim_out.at[1, 0], rim_out.at[1, 1], rim_in.at[1])
    sent += last_copies

    one = scatter_reduce_2(0, one)
    sent += one
    conv_ref[...] = convolved(w2t, picked2).astype(BF16)
    two = scatter_reduce_2(1, two)
    sent += two
    one = reduce_3(0, one)
    sent += one
    grad_in = scattered(0, n)
    two = reduce_3(1, two)
    sent += two
    arrive(last_copies)
    rims = jnp.concatenate([rim_in[1, 0], rim_in[1, 1]], axis=1).astype(F32)
    gin_ref[...] = (grad_in + rims).astype(BF16)

    one = gather_2(0, one)
    sent += one
    two = gather_2(1, two)
    sent += two
    one = gather_1(0, one)
    sent += one
    two = gather_1(1, two)
    sent += two
    arrive(one)
    arrive(two)
    for copy in sent:
        copy.wait_send()


def per_device(sizes, features, sources, voxels, cotangent, weight_one, weight_two):
    space, dp, planes, deep = sizes
    blocks = features.shape[1]
    n = blocks * V
    half = n // 2
    me = lax.axis_index("space")
    source_ids = sources[0]
    owner = source_ids // blocks
    place = source_ids % blocks
    slot = jnp.where(owner == me, place, jnp.where(owner < me, place + HALO, blocks + HALO + place))
    vox = voxels[0].reshape(blocks, K, V)
    rows = jnp.where(vox == V, -1, slot[:, :, None] * V + vox)
    rows = jnp.transpose(rows, (1, 0, 2)).reshape(K, 1, n)
    feat = features[0].reshape(n, C).T
    cot = cotangent[0].reshape(n, C).T
    t1 = -(-TILES // dp)
    t2 = -(-t1 // planes)
    scratch = [
        pltpu.VMEM((2 * n, K * n), BF16),
        pltpu.VMEM((K, C, n), BF16),
        pltpu.VMEM((K, C, n), BF16),
        pltpu.VMEM((C, K * n), BF16),
        pltpu.VMEM((C, K * C), BF16),
        pltpu.VMEM((C, K * C), BF16),
        pltpu.VMEM((2, C, half), BF16),
        pltpu.VMEM((2, C, half), BF16),
        pltpu.VMEM((2, 2, C, half), BF16),
        pltpu.VMEM((2, 2, C, half), BF16),
        pltpu.VMEM((C, n), BF16),
        pltpu.VMEM((2, dp * t1, TILE, 2 * C), BF16),
        pltpu.VMEM((2, dp, t1, TILE, 2 * C), BF16),
        pltpu.VMEM((2, planes * t2, TILE, 2 * C), BF16),
        pltpu.VMEM((2, planes, t2, TILE, 2 * C), BF16),
        pltpu.VMEM((2, deep, t2, TILE, 2 * C), BF16),
        pltpu.VMEM((2, planes * t2, TILE, 2 * C), BF16),
        pltpu.SemaphoreType.DMA((4, 2)),
        pltpu.SemaphoreType.DMA((4, 2)),
        pltpu.SemaphoreType.DMA((5, 2, max(dp, planes, deep) - 1)),
        pltpu.SemaphoreType.DMA((5, 2, max(dp, planes, deep) - 1)),
    ]
    conv, gin, sums = pl.pallas_call(
        functools.partial(step_kernel, sizes),
        out_shape=(
            jax.ShapeDtypeStruct((C, n), BF16),
            jax.ShapeDtypeStruct((C, n), BF16),
            jax.ShapeDtypeStruct((2, dp, t1, TILE, 2 * C), BF16),
        ),
        in_specs=[pl.BlockSpec(memory_space=pltpu.VMEM)] * 5,
        out_specs=(pl.BlockSpec(memory_space=pltpu.VMEM),) * 3,
        scratch_shapes=scratch,
        compiler_params=pltpu.CompilerParams(
            collective_id=0, has_side_effects=True, vmem_limit_bytes=48 * 1024 * 1024
        ),
        name="step",
    )(feat, cot, rows, weight_one.reshape(K * C, C), weight_two.reshape(K * C, C))
    factor = float(dp * space * n) ** (-0.5)
    sums = sums.reshape(2, dp * t1 * TILE, 2, C)[:, : K * C // 2].reshape(2, K, C // 2, 2, C)
    grads = jnp.transpose(sums, (0, 1, 3, 2, 4)).reshape(2, K, C, C).astype(F32) * factor
    conv = conv.T.reshape(1, blocks, V * C)
    gin = gin.T.reshape(1, blocks, V * C)
    return conv, gin, grads[0], grads[1]


def solution(mesh):
    space, dp = mesh.shape["space"], mesh.shape["dp"]
    sizes = (space, dp, ZPAR * Y, space // (ZPAR * Y))
    wide = P("dp", "space", None)
    return jax.shard_map(
        functools.partial(per_device, sizes),
        mesh=mesh,
        in_specs=(wide, wide, wide, wide, P(), P()),
        out_specs=(wide, wide, P(), P()),
        check_vma=False,
    )
```

```python
import functools

import jax
import jax.numpy as jnp
from jax import lax
from jax.experimental import pallas as pl
from jax.experimental.pallas import tpu as pltpu
from jax.sharding import PartitionSpec as P

C = 64
V = 64
K = 27
HALO = 2
Y = 4
ZPAR = 2
CORES = 2
TILE = 16
TILES = K * C * C // (TILE * 2 * C)
MESH = pl.DeviceIdType.MESH
BF16 = jnp.bfloat16
F32 = jnp.float32


def mxu(a, b, dims=((1,), (0,))):
    return lax.dot_general(a, b, (dims, ((), ())), preferred_element_type=F32)


def step_kernel(
    sizes,
    feat_ref,
    cot_ref,
    rows_ref,
    w1_hbm,
    w2_hbm,
    conv_ref,
    gin_ref,
    sum1_ref,
    sum2_ref,
    hots,
    picked1,
    picked2,
    back,
    w1_ref,
    w2_ref,
    w1t,
    w2t,
    halo_in,
    halo_mid,
    rim_out,
    rim_in,
    hidden,
    parts,
    got1,
    mid,
    got2,
    got3,
    load_sem,
    halo_send,
    halo_recv,
    pair_send,
    pair_recv,
    group_send,
    group_recv,
    deep_send,
    deep_recv,
    relay,
):
    n_x, n_y, n_z = sizes
    deep = n_z // ZPAR
    space = n_y * n_z
    n = feat_ref.shape[1]
    half = n // 2
    s = lax.axis_index("space")
    d = lax.axis_index("dp")
    x, core = d // CORES, d % CORES
    z, y = s // n_y, s % n_y
    z_par, depth = z % ZPAR, z // ZPAR
    pad = TILES // CORES

    def at(dx=0, dy=0, dz=0, core=core):
        return (((z + dz) % n_z) * n_y + (y + dy) % n_y, ((x + dx) % n_x) * CORES + core)

    before = ((s + space - 1) % space, d)
    after = ((s + 1) % space, d)
    twin = at(core=1 - core)
    x_pair = [at(dx=1), at(dx=n_x - 1)]
    y_pair = [at(dy=1), at(dy=n_y - 1)]

    def z_pair(step):
        return [at(dz=step), at(dz=n_z - step)]

    other_z = (((z // ZPAR) * ZPAR + 1 - z_par) * n_y + y, d)

    def signal(sem, devices):
        for device in devices:
            pl.semaphore_signal(sem, inc=1, device_id=device, device_id_type=MESH)

    barrier = pltpu.get_barrier_semaphore()
    near = [before, after, twin] + x_pair + y_pair + z_pair(1)
    signal(barrier, near)

    z_steps = []
    while 2 ** len(z_steps) < n_z // 2:
        z_steps.append(2 ** len(z_steps))

    def relay_signal(i):
        if i == 0:
            signal(relay.at[0], x_pair)
        elif i <= 2:
            signal(relay.at[i], y_pair)
        else:
            signal(relay.at[i], [other_z])
        if i < len(z_steps):
            signal(relay.at[4 + i], z_pair(z_steps[i]))

    def relay_wait(i):
        pl.semaphore_wait(relay.at[i], 2 if i <= 2 else 1)
        if i < len(z_steps) - 1:
            pl.semaphore_wait(relay.at[4 + i], 2)

    def relay_end():
        pl.semaphore_wait(relay.at[4 + len(z_steps) - 1], 2)

    def remote(src, dst, send, recv, target):
        return pltpu.make_async_remote_copy(
            src_ref=src, dst_ref=dst, send_sem=send, recv_sem=recv, device_id=target, device_id_type=MESH
        )

    loads = [
        pltpu.make_async_copy(w2_hbm, w2_ref, load_sem.at[0]),
        pltpu.make_async_copy(w1_hbm, w1_ref, load_sem.at[1]),
    ]
    for load in loads:
        load.start()

    spot = lax.broadcasted_iota(jnp.int32, (n, n), 0).astype(F32).astype(BF16)
    one_hot = jnp.ones((n, n), BF16)
    no_hot = jnp.zeros((n, n), BF16)

    def build(k, carry):
        row = rows_ref[k].astype(F32)
        lanes = pl.ds(pl.multiple_of(k * n, n), n)
        hots[0:n, lanes] = jnp.where(spot == row.astype(BF16), one_hot, no_hot)
        hots[n : 2 * n, lanes] = jnp.where(spot == (row - n).astype(BF16), one_hot, no_hot)
        return carry

    lax.fori_loop(0, K, build, 0)

    group_of = 9

    def spread(w_ref, grad):
        for g in range(0, K, group_of):
            out = mxu(w_ref[g * C : (g + group_of) * C, :], grad).astype(BF16)
            for k in range(group_of):
                back[:, (g + k) * n : (g + k + 1) * n] = out[k * C : (k + 1) * C, :]

    def scattered(lo, hi):
        def some(g, total):
            lanes = pl.ds(pl.multiple_of(g * group_of * n, group_of * n), group_of * n)
            return total + mxu(back[:, lanes], hots[lo:hi, lanes], ((1,), (1,)))

        return lax.fori_loop(0, K // group_of, some, jnp.zeros((C, hi - lo), F32))

    def pick_own(table, picked):
        def one(g, carry):
            for i in range(group_of):
                k = g * group_of + i
                lanes = pl.ds(pl.multiple_of(k * n, n), n)
                picked[k] = mxu(table, hots[0:n, lanes]).astype(BF16)
            return carry

        lax.fori_loop(0, K // group_of, one, 0)

    def pick_halo(table, picked):
        def one(g, carry):
            for i in range(group_of):
                k = g * group_of + i
                lanes = pl.ds(pl.multiple_of(k * n, n), n)
                more = mxu(table, hots[n : 2 * n, lanes])
                picked[k] = (picked[k].astype(F32) + more).astype(BF16)
            return carry

        lax.fori_loop(0, K // group_of, one, 0)

    def convolved(wt, picked):
        return mxu(wt[...], picked[...].reshape(K * C, n))

    def weight_parts(which, picked, grad):
        zero = jnp.zeros((C, n), BF16)
        pair = jnp.concatenate(
            [jnp.concatenate([grad, zero], axis=1), jnp.concatenate([zero, grad], axis=1)], axis=0
        )
        for g in range(0, K, group_of):
            both = jnp.concatenate(
                [picked[g : g + group_of, 0 : C // 2, :], picked[g : g + group_of, C // 2 : C, :]], axis=2
            ).reshape(group_of * C // 2, 2 * n)
            out = mxu(both, pair, ((1,), (1,))).astype(BF16)
            tiles = group_of * C // 2 // TILE
            out = out.reshape(tiles, TILE, 2 * C)
            first = g * C // 2 // TILE
            cut = min(max(pad - first, 0), tiles)
            if cut > 0:
                parts[which, 0, first : first + cut] = out[:cut]
            if cut < tiles:
                parts[which, 1, first + cut - pad : first + tiles - pad] = out[cut:]

    def to_neighbours(slot, low, high, into):
        copies = [
            remote(low, into.at[1], halo_send.at[slot, 0], halo_recv.at[slot, 1], before),
            remote(high, into.at[0], halo_send.at[slot, 1], halo_recv.at[slot, 0], after),
        ]
        for copy in copies:
            copy.start()
        return copies

    def arrive(copies):
        for copy in copies:
            copy.wait_recv()

    offsets = [
        (dx, dy, dz) for dx in range(n_x) for dy in range(n_y) for dz in range(ZPAR) if (dx, dy, dz) != (0, 0, 0)
    ]
    offsets.sort(key=lambda o: -(min(o[0], n_x - o[0]) + min(o[1], n_y - o[1]) + o[2]))

    def member(x, y, z):
        return (z * n_y + y) * n_x + x

    me = member(x, y, z_par)

    def to_twin(stage, which, src, dst):
        copy = remote(src, dst, pair_send.at[stage, which], pair_recv.at[stage, which], twin)
        copy.start()
        return [copy]

    def to_members(stage, which, src_of, dst):
        copies = []
        for i, (dx, dy, dz) in enumerate(offsets):
            xx, yy, zz = (x + dx) % n_x, (y + dy) % n_y, (z_par + dz) % ZPAR
            target = (((z // ZPAR) * ZPAR + zz) * n_y + yy, xx * CORES + core)
            copy = remote(
                src_of(member(xx, yy, zz)), dst, group_send.at[stage, which, i], group_recv.at[stage, which, i], target
            )
            copy.start()
            copies.append(copy)
        return copies

    def to_depths(which, src, dst):
        copies = []
        for j in [j for i in range(deep // 2, 0, -1) for j in sorted({i, deep - i})]:
            target = at(dz=j * ZPAR)
            copy = remote(src, dst, deep_send.at[which, j - 1], deep_recv.at[which, j - 1], target)
            copy.start()
            copies.append(copy)
        return copies

    feat = feat_ref[...]
    cot = cot_ref[...]
    for which in range(2):
        mid[which, pad] = jnp.zeros((TILE, 2 * C), BF16)
    loads[0].wait()
    spread(w2_ref, cot)
    pl.semaphore_wait(barrier, len(near))
    relay_signal(0)
    feat_copies = to_neighbours(0, feat_ref.at[:, 0:half], feat_ref.at[:, half:n], halo_in)
    rim = scattered(n, 2 * n).astype(BF16)
    for i in range(2):
        rim_out[0, i] = rim[:, i * half : (i + 1) * half]
    rim_copies = to_neighbours(1, rim_out.at[0, 0], rim_out.at[0, 1], rim_in.at[0])
    sent = feat_copies + rim_copies
    relay_wait(0)
    relay_signal(1)

    pick_own(feat, picked1)
    relay_wait(1)
    relay_signal(2)
    loads[1].wait()
    w1t[...] = w1_ref[...].T
    w2t[...] = w2_ref[...].T

    arrive(feat_copies)
    pick_halo(jnp.concatenate([halo_in[0], halo_in[1]], axis=1), picked1)
    pre = convolved(w1t, picked1)
    sig = 1.0 / (1.0 + jnp.exp(-pre))
    hid = (pre * sig).astype(BF16)
    hidden[...] = hid
    hid_copies = to_neighbours(2, hidden.at[:, 0:half], hidden.at[:, half:n], halo_mid)
    sent += hid_copies
    relay_wait(2)
    relay_signal(3)

    grad_hidden = scattered(0, n)
    arrive(rim_copies)
    rims = jnp.concatenate([rim_in[0, 0], rim_in[0, 1]], axis=1).astype(F32)
    grad_pre = ((grad_hidden + rims) * (sig * (1.0 + pre * (1.0 - sig)))).astype(BF16)
    weight_parts(0, picked1, grad_pre)

    def reduce_pair(which):
        return to_twin(0, which, parts.at[which, 1 - core], got1.at[which])

    def scatter_reduce(which, copies):
        arrive(copies)
        mid[which, 0:pad] = (parts[which, core].astype(F32) + got1[which].astype(F32)).astype(BF16)
        got2[which, me] = mid[which, jnp.minimum(me, pad)]
        return to_members(0, which, lambda other: mid.at[which, jnp.minimum(other, pad)], got2.at[which, me])

    def added(ref, which, count):
        totals = [ref[which, i].astype(F32) for i in range(count)]
        while len(totals) > 1:
            totals = [a + b for a, b in zip(totals[::2], totals[1::2])]
        return totals[0].astype(BF16)

    def reduce_deep(which, copies):
        arrive(copies)
        got3[which, depth] = added(got2, which, len(offsets) + 1)
        mine = got3.at[which, depth]
        return to_depths(which, mine, mine)

    def gather_members(which, copies, out):
        arrive(copies)
        out[core, me] = added(got3, which, deep)
        mine = out.at[core, me]
        return to_members(1, which, lambda other: mine, mine)

    def gather_pair(which, copies, out):
        arrive(copies)
        mine = out.at[core, 0:pad]
        return to_twin(1, which, mine, mine)

    one = reduce_pair(0)
    sent += one

    pick_own(hid, picked2)
    relay_wait(3)
    one = scatter_reduce(0, one)
    sent += one
    arrive(hid_copies)
    pick_halo(jnp.concatenate([halo_mid[0], halo_mid[1]], axis=1), picked2)
    weight_parts(1, picked2, cot)
    two = reduce_pair(1)
    sent += two

    spread(w1_ref, grad_pre)
    rim = scattered(n, 2 * n).astype(BF16)
    for i in range(2):
        rim_out[1, i] = rim[:, i * half : (i + 1) * half]
    last_copies = to_neighbours(3, rim_out.at[1, 0], rim_out.at[1, 1], rim_in.at[1])
    sent += last_copies
    two = scatter_reduce(1, two)
    sent += two
    relay_end()
    one = reduce_deep(0, one)
    sent += one

    conv_ref[...] = convolved(w2t, picked2).astype(BF16)
    grad_in = scattered(0, n)
    arrive(last_copies)
    rims = jnp.concatenate([rim_in[1, 0], rim_in[1, 1]], axis=1).astype(F32)
    gin_ref[...] = (grad_in + rims).astype(BF16)

    two = reduce_deep(1, two)
    sent += two
    one = gather_members(0, one, sum1_ref)
    sent += one
    two = gather_members(1, two, sum2_ref)
    sent += two
    one = gather_pair(0, one, sum1_ref)
    sent += one
    two = gather_pair(1, two, sum2_ref)
    sent += two
    arrive(one)
    arrive(two)
    for copy in sent:
        copy.wait_send()


def per_device(sizes, features, sources, voxels, cotangent, weight_one, weight_two):
    n_x, n_y, n_z = sizes
    members = n_x * n_y * ZPAR
    deep = n_z // ZPAR
    blocks = features.shape[1]
    n = blocks * V
    half = n // 2
    me = lax.axis_index("space")
    source_ids = sources[0]
    owner = source_ids // blocks
    place = source_ids % blocks
    slot = jnp.where(owner == me, place, jnp.where(owner < me, place + HALO, blocks + HALO + place))
    vox = voxels[0].reshape(blocks, K, V)
    rows = jnp.where(vox == V, -1, slot[:, :, None] * V + vox)
    rows = jnp.transpose(rows, (1, 0, 2)).reshape(K, 1, n)
    feat = features[0].reshape(n, C).T
    cot = cotangent[0].reshape(n, C).T
    pad = TILES // CORES
    scratch = [
        pltpu.VMEM((2 * n, K * n), BF16),
        pltpu.VMEM((K, C, n), BF16),
        pltpu.VMEM((K, C, n), BF16),
        pltpu.VMEM((C, K * n), BF16),
        pltpu.VMEM((K * C, C), BF16),
        pltpu.VMEM((K * C, C), BF16),
        pltpu.VMEM((C, K * C), BF16),
        pltpu.VMEM((C, K * C), BF16),
        pltpu.VMEM((2, C, half), BF16),
        pltpu.VMEM((2, C, half), BF16),
        pltpu.VMEM((2, 2, C, half), BF16),
        pltpu.VMEM((2, 2, C, half), BF16),
        pltpu.VMEM((C, n), BF16),
        pltpu.VMEM((2, CORES, pad, TILE, 2 * C), BF16),
        pltpu.VMEM((2, pad, TILE, 2 * C), BF16),
        pltpu.VMEM((2, pad + 1, TILE, 2 * C), BF16),
        pltpu.VMEM((2, members, TILE, 2 * C), BF16),
        pltpu.VMEM((2, deep, TILE, 2 * C), BF16),
        pltpu.SemaphoreType.DMA((2,)),
        pltpu.SemaphoreType.DMA((4, 2)),
        pltpu.SemaphoreType.DMA((4, 2)),
        pltpu.SemaphoreType.DMA((2, 2)),
        pltpu.SemaphoreType.DMA((2, 2)),
        pltpu.SemaphoreType.DMA((2, 2, members - 1)),
        pltpu.SemaphoreType.DMA((2, 2, members - 1)),
        pltpu.SemaphoreType.DMA((2, deep - 1)),
        pltpu.SemaphoreType.DMA((2, deep - 1)),
        pltpu.SemaphoreType.REGULAR((8,)),
    ]
    total = jax.ShapeDtypeStruct((CORES, members, TILE, 2 * C), BF16)
    vmem = pl.BlockSpec(memory_space=pltpu.VMEM)
    hbm = pl.BlockSpec(memory_space=pl.ANY)
    conv, gin, sum1, sum2 = pl.pallas_call(
        functools.partial(step_kernel, sizes),
        out_shape=(jax.ShapeDtypeStruct((C, n), BF16), jax.ShapeDtypeStruct((C, n), BF16), total, total),
        in_specs=[vmem, vmem, vmem, hbm, hbm],
        out_specs=(vmem,) * 4,
        scratch_shapes=scratch,
        compiler_params=pltpu.CompilerParams(
            collective_id=0, has_side_effects=True, vmem_limit_bytes=48 * 1024 * 1024
        ),
        name="step",
    )(feat, cot, rows, weight_one.reshape(K * C, C), weight_two.reshape(K * C, C))
    factor = float(n_x * CORES * n_y * n_z * n) ** (-0.5)

    def whole(tiles):
        pairs = tiles[:, :pad].reshape(K, C // 2, 2, C)
        return jnp.transpose(pairs, (0, 2, 1, 3)).reshape(K, C, C).astype(F32) * factor

    conv = conv.T.reshape(1, blocks, V * C)
    gin = gin.T.reshape(1, blocks, V * C)
    return conv, gin, whole(sum1), whole(sum2)


def solution(mesh):
    space, dp = mesh.shape["space"], mesh.shape["dp"]
    sizes = (dp // CORES, Y, space // Y)
    wide = P("dp", "space", None)
    return jax.shard_map(
        functools.partial(per_device, sizes),
        mesh=mesh,
        in_specs=(wide, wide, wide, wide, P(), P()),
        out_specs=(wide, wide, P(), P()),
        check_vma=False,
    )
```

```python
import functools

import jax
import jax.numpy as jnp
from jax import lax
from jax.experimental import pallas as pl
from jax.experimental.pallas import tpu as pltpu
from jax.sharding import PartitionSpec as P

C = 64
V = 64
K = 27
HALO = 2
Y = 4
ZPAR = 2
CORES = 2
TILE = 16
TILES = K * C * C // (TILE * 2 * C)
MESH = pl.DeviceIdType.MESH
BF16 = jnp.bfloat16
F32 = jnp.float32


def mxu(a, b, dims=((1,), (0,))):
    return lax.dot_general(a, b, (dims, ((), ())), preferred_element_type=F32)


def step_kernel(
    sizes,
    x_hbm,
    ct_hbm,
    src_hbm,
    vox_hbm,
    w1_hbm,
    w2_hbm,
    conv_ref,
    gin_ref,
    grad1_ref,
    grad2_ref,
    x_ref,
    ct_ref,
    src_ref,
    vox_ref,
    w1_ref,
    w2_ref,
    slots,
    pair_rows,
    wide_rows,
    turn,
    flat,
    table1,
    table2,
    feat_ref,
    picked1,
    picked2,
    back,
    w1t,
    w2t,
    halo_in,
    halo_mid,
    rim_out,
    rim_in,
    hidden,
    parts,
    got1,
    mid,
    got2,
    got3,
    sums,
    load_sem,
    halo_send,
    halo_recv,
    pair_send,
    pair_recv,
    group_send,
    group_recv,
    deep_send,
    deep_recv,
    relay,
):
    n_x, n_y, n_z = sizes
    deep = n_z // ZPAR
    space = n_y * n_z
    blocks = x_ref.shape[0]
    n = feat_ref.shape[1]
    half = n // 2
    s = lax.axis_index("space")
    d = lax.axis_index("dp")
    x, core = d // CORES, d % CORES
    z, y = s // n_y, s % n_y
    z_par, depth = z % ZPAR, z // ZPAR
    pad = TILES // CORES
    per = sums.shape[2] // (n_x * n_y * ZPAR)

    def at(dx=0, dy=0, dz=0, core=core):
        return (((z + dz) % n_z) * n_y + (y + dy) % n_y, ((x + dx) % n_x) * CORES + core)

    before = ((s + space - 1) % space, d)
    after = ((s + 1) % space, d)
    twin = at(core=1 - core)
    x_pair = [at(dx=1), at(dx=n_x - 1)]
    y_pair = [at(dy=1), at(dy=n_y - 1)]

    def z_pair(step):
        return [at(dz=step), at(dz=n_z - step)]

    other_z = (((z // ZPAR) * ZPAR + 1 - z_par) * n_y + y, d)

    def signal(sem, devices):
        for device in devices:
            pl.semaphore_signal(sem, inc=1, device_id=device, device_id_type=MESH)

    barrier = pltpu.get_barrier_semaphore()
    near = [before, after, twin] + x_pair + y_pair + z_pair(1)
    signal(barrier, near)

    z_steps = []
    while 2 ** len(z_steps) < n_z // 2:
        z_steps.append(2 ** len(z_steps))

    def relay_signal(i):
        if i == 0:
            signal(relay.at[0], x_pair)
        elif i <= 2:
            signal(relay.at[i], y_pair)
        else:
            signal(relay.at[i], [other_z])
        if i < len(z_steps):
            signal(relay.at[4 + i], z_pair(z_steps[i]))

    def relay_wait(i):
        pl.semaphore_wait(relay.at[i], 2 if i <= 2 else 1)
        if i < len(z_steps) - 1:
            pl.semaphore_wait(relay.at[4 + i], 2)

    def relay_end():
        pl.semaphore_wait(relay.at[4 + len(z_steps) - 1], 2)

    def remote(src, dst, send, recv, target):
        return pltpu.make_async_remote_copy(
            src_ref=src, dst_ref=dst, send_sem=send, recv_sem=recv, device_id=target, device_id_type=MESH
        )

    loads = {}
    for i, (name, src, dst) in enumerate(
        (
            ("vox", vox_hbm, vox_ref),
            ("src", src_hbm, src_ref),
            ("x", x_hbm, x_ref),
            ("ct", ct_hbm, ct_ref),
            ("w2", w2_hbm, w2_ref),
            ("w1", w1_hbm, w1_ref),
        )
    ):
        loads[name] = pltpu.make_async_copy(src, dst, load_sem.at[i])
        loads[name].start()

    def iota(shape, dim):
        return lax.broadcasted_iota(jnp.int32, shape, dim)

    pairs = V // 2
    old = iota((n, n), 0)
    parity, rest = old // (n // 2), old % (n // 2)
    order = jnp.where(rest // pairs * V + rest % pairs * 2 + parity == iota((n, n), 1), 1.0, 0.0).astype(BF16)

    def to_channels(ref):
        wide = ref[...].astype(F32)
        for j in range(pairs):
            turn[j * blocks : (j + 1) * blocks, :] = wide[:, j * 2 * C : (j + 1) * 2 * C]
        rows = jnp.concatenate([turn[pl.ds(b, pairs, stride=blocks), :] for b in range(blocks)], axis=0)
        lanes = rows.T
        both = jnp.concatenate([lanes[:C], lanes[C:]], axis=1).astype(BF16)
        return mxu(both, order).astype(BF16)

    def from_channels(value, out_ref):
        both = mxu(value, order, ((1,), (1,)))
        rows = jnp.concatenate([both[:, : n // 2], both[:, n // 2 :]], axis=0).T
        turn[...] = rows
        for j in range(pairs):
            flat[:, j * 2 * C : (j + 1) * 2 * C] = turn[pl.ds(j, blocks, stride=pairs), :]
        out_ref[...] = flat[...].astype(BF16)

    low_row = iota((1, 2 * V), 1) < V
    shift = blocks.bit_length() - 1

    def make_rows():
        for k in range(K):
            for b in range(blocks):
                source = src_ref[b, k]
                owner, place = source >> shift, source & (blocks - 1)
                slots[k * blocks + b] = jnp.where(
                    owner == s, place, jnp.where(owner < s, place + HALO, blocks + HALO + place)
                )
            start = k // 2 * 2 * V
            if start + 2 * V <= K * V:
                here = vox_ref[:, start : start + 2 * V]
            else:
                here = jnp.concatenate([vox_ref[:, start : start + V]] * 2, axis=1)
            there = pltpu.roll(here, V, 1)
            first, second = (here, there) if k % 2 == 0 else (there, here)
            for p in range(blocks // 2):
                row = jnp.where(low_row, first[2 * p : 2 * p + 1], second[2 * p + 1 : 2 * p + 2])
                none = row >= V
                base = jnp.where(low_row, slots[k * blocks + 2 * p] * V, slots[k * blocks + 2 * p + 1] * V)
                lanes = slice(p * 2 * V, (p + 1) * 2 * V)
                pair_rows[k, :, lanes] = jnp.where(none, -1, row + jnp.where(low_row, 0, V)).astype(F32)
                wide_rows[k, :, lanes] = jnp.where(none, -1, row + base).astype(F32)

    group_of = 9
    spot = iota((n, n), 0).astype(F32).astype(BF16)
    spot_pair = iota((2 * V, 2 * V), 0).astype(F32).astype(BF16)

    def hot(where, row):
        return jnp.where(where == row.astype(BF16), jnp.ones_like(where), jnp.zeros_like(where))

    def spread(w_ref, grad):
        for g in range(0, K, group_of):
            out = mxu(w_ref[g * C : (g + group_of) * C, :], grad).astype(BF16)
            back[g : g + group_of] = out.reshape(group_of, C, n)

    def scattered(lo):
        def some(g, total):
            for i in range(group_of):
                k = g * group_of + i
                total = total + mxu(back[k], hot(spot, wide_rows[k] - lo), ((1,), (1,)))
            return total

        return lax.fori_loop(0, K // group_of, some, jnp.zeros((C, n), F32))

    low16 = iota((C, 2 * V), 1).astype(F32).astype(BF16) < V
    low32 = iota((C, 2 * V), 1) < V

    def fill(table, value, first):
        value = value.astype(F32)
        turned = pltpu.roll(value, V, 1)
        table[first] = jnp.where(low32, value, turned).astype(BF16)
        table[first + 1] = jnp.where(low32, turned, value).astype(BF16)

    def fill_own(table, value):
        for p in range(blocks // 2):
            fill(table, value[:, p * 2 * V : (p + 1) * 2 * V], 2 * p)

    def fill_halo(table, ref):
        for i in range(2):
            fill(table, ref[i], blocks + 2 * i)

    def pick(table, picked):
        def one(g, carry):
            for i in range(group_of):
                k = g * group_of + i
                for p in range(blocks // 2):
                    lanes = slice(p * 2 * V, (p + 1) * 2 * V)
                    both = jnp.where(
                        low16, table[slots[k * blocks + 2 * p]], table[slots[k * blocks + 2 * p + 1]]
                    )
                    picked[k, :, lanes] = mxu(both, hot(spot_pair, pair_rows[k, :, lanes])).astype(BF16)
            return carry

        lax.fori_loop(0, K // group_of, one, 0)

    def convolved(wt, picked):
        return mxu(wt[...], picked[...].reshape(K * C, n))

    def weight_parts(which, picked, grad):
        zero = jnp.zeros((C, n), BF16)
        pair = jnp.concatenate(
            [jnp.concatenate([grad, zero], axis=1), jnp.concatenate([zero, grad], axis=1)], axis=0
        )
        for g in range(0, K, group_of):
            both = jnp.concatenate(
                [picked[g : g + group_of, 0 : C // 2, :], picked[g : g + group_of, C // 2 : C, :]], axis=2
            ).reshape(group_of * C // 2, 2 * n)
            out = mxu(both, pair, ((1,), (1,))).astype(BF16)
            tiles = group_of * C // 2 // TILE
            out = out.reshape(tiles, TILE, 2 * C)
            first = g * C // 2 // TILE
            cut = min(max(pad - first, 0), tiles)
            if cut > 0:
                parts[which, 0, first : first + cut] = out[:cut]
            if cut < tiles:
                parts[which, 1, first + cut - pad : first + tiles - pad] = out[cut:]

    def to_neighbours(slot, low, high, into):
        copies = [
            remote(low, into.at[1], halo_send.at[slot, 0], halo_recv.at[slot, 1], before),
            remote(high, into.at[0], halo_send.at[slot, 1], halo_recv.at[slot, 0], after),
        ]
        for copy in copies:
            copy.start()
        return copies

    def arrive(copies):
        for copy in copies:
            copy.wait_recv()

    offsets = [
        (dx, dy, dz) for dx in range(n_x) for dy in range(n_y) for dz in range(ZPAR) if (dx, dy, dz) != (0, 0, 0)
    ]
    offsets.sort(key=lambda o: -(min(o[0], n_x - o[0]) + min(o[1], n_y - o[1]) + o[2]))

    def member(x, y, z):
        return (z * n_y + y) * n_x + x

    me = member(x, y, z_par)

    def to_twin(stage, which, src, dst):
        copy = remote(src, dst, pair_send.at[stage, which], pair_recv.at[stage, which], twin)
        copy.start()
        return [copy]

    def to_members(stage, which, src_of, dst):
        copies = []
        for i, (dx, dy, dz) in enumerate(offsets):
            xx, yy, zz = (x + dx) % n_x, (y + dy) % n_y, (z_par + dz) % ZPAR
            target = (((z // ZPAR) * ZPAR + zz) * n_y + yy, xx * CORES + core)
            copy = remote(
                src_of(member(xx, yy, zz)), dst, group_send.at[stage, which, i], group_recv.at[stage, which, i], target
            )
            copy.start()
            copies.append(copy)
        return copies

    def to_depths(which, src, dst):
        copies = []
        for j in [j for i in range(deep // 2, 0, -1) for j in sorted({i, deep - i})]:
            target = at(dz=j * ZPAR)
            copy = remote(src, dst, deep_send.at[which, j - 1], deep_recv.at[which, j - 1], target)
            copy.start()
            copies.append(copy)
        return copies

    for which in range(2):
        mid[which, pad:] = jnp.zeros((mid.shape[1] - pad, TILE, 2 * C), BF16)
    loads["x"].wait()
    feat = to_channels(x_ref)
    feat_ref[...] = feat
    pl.semaphore_wait(barrier, len(near))
    feat_copies = to_neighbours(0, feat_ref.at[:, 0:half], feat_ref.at[:, half:n], halo_in)
    relay_signal(0)
    sent = list(feat_copies)

    loads["vox"].wait()
    loads["src"].wait()
    make_rows()
    loads["ct"].wait()
    cot = to_channels(ct_ref)
    loads["w2"].wait()
    spread(w2_ref, cot)
    rim = scattered(n).astype(BF16)
    for i in range(2):
        rim_out[0, i] = rim[:, i * half : (i + 1) * half]
    rim_copies = to_neighbours(1, rim_out.at[0, 0], rim_out.at[0, 1], rim_in.at[0])
    sent += rim_copies
    relay_wait(0)
    relay_signal(1)
    loads["w1"].wait()
    w1t[...] = w1_ref[...].T
    fill_own(table1, feat)

    arrive(feat_copies)
    fill_halo(table1, halo_in)
    pick(table1, picked1)
    pre = convolved(w1t, picked1)
    sig = 1.0 / (1.0 + jnp.exp(-pre))
    hid = (pre * sig).astype(BF16)
    hidden[...] = hid
    hid_copies = to_neighbours(2, hidden.at[:, 0:half], hidden.at[:, half:n], halo_mid)
    sent += hid_copies
    relay_wait(1)
    relay_signal(2)

    grad_hidden = scattered(0)
    arrive(rim_copies)
    rims = jnp.concatenate([rim_in[0, 0], rim_in[0, 1]], axis=1).astype(F32)
    grad_pre = ((grad_hidden + rims) * (sig * (1.0 + pre * (1.0 - sig)))).astype(BF16)
    weight_parts(0, picked1, grad_pre)

    def mine_of(which):
        return sums.at[which, core, pl.ds(me * per, per)]

    def reduce_pair(which):
        return to_twin(0, which, parts.at[which, 1 - core], got1.at[which])

    def scatter_reduce(which, copies):
        arrive(copies)
        mid[which, 0:pad] = (parts[which, core].astype(F32) + got1[which].astype(F32)).astype(BF16)
        got2[which, me] = mid[which, pl.ds(me * per, per)]
        return to_members(0, which, lambda other: mid.at[which, pl.ds(other * per, per)], got2.at[which, me])

    def added(ref, which, count):
        totals = [ref[which, i].astype(F32) for i in range(count)]
        while len(totals) > 1:
            totals = [a + b for a, b in zip(totals[::2], totals[1::2])]
        return totals[0].astype(BF16)

    def reduce_deep(which, copies):
        arrive(copies)
        got3[which, depth] = added(got2, which, len(offsets) + 1)
        mine = got3.at[which, depth]
        return to_depths(which, mine, mine)

    def gather_members(which, copies):
        arrive(copies)
        sums[which, core, pl.ds(me * per, per)] = added(got3, which, deep)
        mine = mine_of(which)
        return to_members(1, which, lambda other: mine, mine)

    def gather_pair(which, copies):
        arrive(copies)
        mine = sums.at[which, core, 0:pad]
        return to_twin(1, which, mine, mine)

    factor = float(n_x * CORES * space * n) ** (-0.5)

    def lay_out(which, side, out):
        for i in range(pad):
            tile = side * pad + i
            k = tile // 2
            value = sums[which, side, i].astype(F32) * factor
            top = pl.multiple_of(tile % 2 * TILE, TILE)
            out[k, pl.ds(top, TILE), :] = value[:, :C]
            out[k, pl.ds(top + C // 2, TILE), :] = value[:, C:]

    def drain(copies):
        for copy in copies:
            copy.wait_send()

    one = reduce_pair(0)
    sent += one
    fill_own(table2, hid)
    relay_wait(2)
    relay_signal(3)
    w2t[...] = w2_ref[...].T
    relay_wait(3)
    one = scatter_reduce(0, one)
    sent += one
    arrive(hid_copies)
    fill_halo(table2, halo_mid)
    pick(table2, picked2)
    weight_parts(1, picked2, cot)
    two = reduce_pair(1)
    sent += two

    spread(w1_ref, grad_pre)
    two = scatter_reduce(1, two)
    sent += two
    rim = scattered(n).astype(BF16)
    for i in range(2):
        rim_out[1, i] = rim[:, i * half : (i + 1) * half]
    last_copies = to_neighbours(3, rim_out.at[1, 0], rim_out.at[1, 1], rim_in.at[1])
    sent += last_copies
    from_channels(convolved(w2t, picked2).astype(BF16), conv_ref)

    relay_end()
    one = reduce_deep(0, one)
    sent += one
    grad_in = scattered(0)
    two = reduce_deep(1, two)
    sent += two
    arrive(last_copies)
    rims = jnp.concatenate([rim_in[1, 0], rim_in[1, 1]], axis=1).astype(F32)
    from_channels((grad_in + rims).astype(BF16), gin_ref)
    drain(sent)

    one = gather_members(0, one)
    sent = list(one)
    two = gather_members(1, two)
    sent += two
    one = gather_pair(0, one)
    sent += one
    lay_out(0, core, grad1_ref)
    arrive(one)
    lay_out(0, 1 - core, grad1_ref)
    two = gather_pair(1, two)
    drain(sent)
    lay_out(1, core, grad2_ref)
    arrive(two)
    lay_out(1, 1 - core, grad2_ref)
    drain(two)


def put_kernel(*refs):
    count = len(refs) // 2
    sem = refs[-1]
    copies = []
    for i, (src, dst) in enumerate(zip(refs[:count], refs[count:-1])):
        size = src.shape[0]
        cuts = 3 if size == K else 1
        for c in range(cuts):
            part = pl.ds(c * size // cuts, size // cuts)
            copies.append(pltpu.make_async_copy(src.at[part], dst.at[part], sem.at[i, c]))
    for copy in copies:
        copy.start()
    for copy in copies:
        copy.wait()


def per_device(sizes, features, sources, voxels, cotangent, weight_one, weight_two):
    n_x, n_y, n_z = sizes
    members = n_x * n_y * ZPAR
    deep = n_z // ZPAR
    blocks = features.shape[1]
    n = blocks * V
    half = n // 2
    pad = TILES // CORES
    per = -(-pad // members)
    slots = blocks + 2 * HALO
    scratch = [
        pltpu.VMEM((blocks, V * C), BF16),
        pltpu.VMEM((blocks, V * C), BF16),
        pltpu.SMEM((blocks, K), jnp.int32),
        pltpu.VMEM((blocks, K * V), jnp.int32),
        pltpu.VMEM((K * C, C), BF16),
        pltpu.VMEM((K * C, C), BF16),
        pltpu.SMEM((K * blocks,), jnp.int32),
        pltpu.VMEM((K, 1, n), F32),
        pltpu.VMEM((K, 1, n), F32),
        pltpu.VMEM((n // 2, 2 * C), F32),
        pltpu.VMEM((blocks, V * C), F32),
        pltpu.VMEM((slots, C, 2 * V), BF16),
        pltpu.VMEM((slots, C, 2 * V), BF16),
        pltpu.VMEM((C, n), BF16),
        pltpu.VMEM((K, C, n), BF16),
        pltpu.VMEM((K, C, n), BF16),
        pltpu.VMEM((K, C, n), BF16),
        pltpu.VMEM((C, K * C), BF16),
        pltpu.VMEM((C, K * C), BF16),
        pltpu.VMEM((2, C, half), BF16),
        pltpu.VMEM((2, C, half), BF16),
        pltpu.VMEM((2, 2, C, half), BF16),
        pltpu.VMEM((2, 2, C, half), BF16),
        pltpu.VMEM((C, n), BF16),
        pltpu.VMEM((2, CORES, pad, TILE, 2 * C), BF16),
        pltpu.VMEM((2, pad, TILE, 2 * C), BF16),
        pltpu.VMEM((2, members * per, TILE, 2 * C), BF16),
        pltpu.VMEM((2, members, per, TILE, 2 * C), BF16),
        pltpu.VMEM((2, deep, per, TILE, 2 * C), BF16),
        pltpu.VMEM((2, CORES, members * per, TILE, 2 * C), BF16),
        pltpu.SemaphoreType.DMA((6,)),
        pltpu.SemaphoreType.DMA((4, 2)),
        pltpu.SemaphoreType.DMA((4, 2)),
        pltpu.SemaphoreType.DMA((2, 2)),
        pltpu.SemaphoreType.DMA((2, 2)),
        pltpu.SemaphoreType.DMA((2, 2, members - 1)),
        pltpu.SemaphoreType.DMA((2, 2, members - 1)),
        pltpu.SemaphoreType.DMA((2, deep - 1)),
        pltpu.SemaphoreType.DMA((2, deep - 1)),
        pltpu.SemaphoreType.REGULAR((8,)),
    ]
    outs = (
        jax.ShapeDtypeStruct((blocks, V * C), BF16),
        jax.ShapeDtypeStruct((blocks, V * C), BF16),
        jax.ShapeDtypeStruct((K, C, C), F32),
        jax.ShapeDtypeStruct((K, C, C), F32),
    )
    vmem = pl.BlockSpec(memory_space=pltpu.VMEM)
    anywhere = pl.BlockSpec(memory_space=pl.ANY)
    hbm = pl.BlockSpec(memory_space=pltpu.HBM)
    results = pl.pallas_call(
        functools.partial(step_kernel, sizes),
        out_shape=outs,
        in_specs=[hbm] * 6,
        out_specs=(vmem,) * 4,
        scratch_shapes=scratch,
        compiler_params=pltpu.CompilerParams(
            collective_id=0, has_side_effects=True, vmem_limit_bytes=32 * 1024 * 1024
        ),
        name="step",
    )(
        features[0],
        cotangent[0],
        sources[0],
        voxels[0],
        weight_one.reshape(K * C, C),
        weight_two.reshape(K * C, C),
    )
    conv, gin, grad_one, grad_two = pl.pallas_call(
        put_kernel,
        out_shape=outs,
        in_specs=[anywhere] * 4,
        out_specs=(hbm,) * 4,
        scratch_shapes=[pltpu.SemaphoreType.DMA((4, 3))],
        compiler_params=pltpu.CompilerParams(vmem_limit_bytes=1024 * 1024),
        name="put",
    )(*results)
    return conv[None], gin[None], grad_one, grad_two


def solution(mesh):
    space, dp = mesh.shape["space"], mesh.shape["dp"]
    sizes = (dp // CORES, Y, space // Y)
    wide = P("dp", "space", None)
    return jax.shard_map(
        functools.partial(per_device, sizes),
        mesh=mesh,
        in_specs=(wide, wide, wide, wide, P(), P()),
        out_specs=(wide, wide, P(), P()),
        check_vma=False,
    )
```

```python
import functools

import jax
import jax.numpy as jnp
from jax import lax
from jax.experimental import pallas as pl
from jax.experimental.pallas import tpu as pltpu
from jax.sharding import PartitionSpec as P

C = 64
V = 64
K = 27
HALO = 2
Y = 4
ZPAR = 2
CORES = 2
TILE = 16
TILES = K * C * C // (TILE * 2 * C)
MESH = pl.DeviceIdType.MESH
BF16 = jnp.bfloat16
F32 = jnp.float32


def mxu(a, b, dims=((1,), (0,))):
    return lax.dot_general(a, b, (dims, ((), ())), preferred_element_type=F32)


def step_kernel(
    sizes,
    x_hbm,
    ct_hbm,
    src_hbm,
    vox_hbm,
    w1_hbm,
    w2_hbm,
    conv_ref,
    gin_ref,
    grad1_ref,
    grad2_ref,
    x_ref,
    ct_ref,
    src_ref,
    vox_ref,
    w1_ref,
    w2_ref,
    slots,
    pair_rows,
    wide_rows,
    turn,
    flat,
    table1,
    table2,
    feat_ref,
    picked1,
    picked2,
    back,
    w1t,
    w2t,
    halo_in,
    halo_mid,
    rim_out,
    rim_in,
    hidden,
    parts,
    got1,
    mid,
    got2,
    got3,
    sums,
    load_sem,
    halo_send,
    halo_recv,
    pair_send,
    pair_recv,
    group_send,
    group_recv,
    deep_send,
    deep_recv,
    relay,
):
    n_x, n_y, n_z = sizes
    deep = n_z // ZPAR
    space = n_y * n_z
    blocks = x_ref.shape[0]
    n = feat_ref.shape[1]
    half = n // 2
    s = lax.axis_index("space")
    d = lax.axis_index("dp")
    x, core = d // CORES, d % CORES
    z, y = s // n_y, s % n_y
    z_par, depth = z % ZPAR, z // ZPAR
    pad = TILES // CORES
    per = sums.shape[2] // (n_x * n_y * ZPAR)

    def at(dx=0, dy=0, dz=0, core=core):
        return (((z + dz) % n_z) * n_y + (y + dy) % n_y, ((x + dx) % n_x) * CORES + core)

    before = ((s + space - 1) % space, d)
    after = ((s + 1) % space, d)
    twin = at(core=1 - core)
    x_pair = [at(dx=1), at(dx=n_x - 1)]
    y_pair = [at(dy=1), at(dy=n_y - 1)]

    def z_pair(step):
        return [at(dz=step), at(dz=n_z - step)]

    other_z = (((z // ZPAR) * ZPAR + 1 - z_par) * n_y + y, d)

    def signal(sem, devices):
        for device in devices:
            pl.semaphore_signal(sem, inc=1, device_id=device, device_id_type=MESH)

    barrier = pltpu.get_barrier_semaphore()
    near = [before, after, twin] + x_pair + y_pair + z_pair(1)
    signal(barrier, near)

    z_steps = []
    while 2 ** len(z_steps) < n_z // 2:
        z_steps.append(2 ** len(z_steps))

    def relay_signal(i):
        if i == 0:
            signal(relay.at[0], x_pair)
        elif i <= 2:
            signal(relay.at[i], y_pair)
        else:
            signal(relay.at[i], [other_z])
        if i < len(z_steps):
            signal(relay.at[4 + i], z_pair(z_steps[i]))

    def relay_wait(i):
        pl.semaphore_wait(relay.at[i], 2 if i <= 2 else 1)
        if i < len(z_steps) - 1:
            pl.semaphore_wait(relay.at[4 + i], 2)

    def relay_end():
        pl.semaphore_wait(relay.at[4 + len(z_steps) - 1], 2)

    def remote(src, dst, send, recv, target):
        return pltpu.make_async_remote_copy(
            src_ref=src, dst_ref=dst, send_sem=send, recv_sem=recv, device_id=target, device_id_type=MESH
        )

    loads = {}
    for i, (name, src, dst) in enumerate(
        (
            ("vox", vox_hbm, vox_ref),
            ("src", src_hbm, src_ref),
            ("x", x_hbm, x_ref),
            ("ct", ct_hbm, ct_ref),
            ("w2", w2_hbm, w2_ref),
            ("w1", w1_hbm, w1_ref),
        )
    ):
        loads[name] = pltpu.make_async_copy(src, dst, load_sem.at[i])
        loads[name].start()

    def iota(shape, dim):
        return lax.broadcasted_iota(jnp.int32, shape, dim)

    pairs = V // 2
    old = iota((n, n), 0)
    parity, rest = old // (n // 2), old % (n // 2)
    order = jnp.where(rest // pairs * V + rest % pairs * 2 + parity == iota((n, n), 1), 1.0, 0.0).astype(BF16)

    def to_channels(ref):
        wide = ref[...].astype(F32)
        for j in range(pairs):
            turn[j * blocks : (j + 1) * blocks, :] = wide[:, j * 2 * C : (j + 1) * 2 * C]
        rows = jnp.concatenate([turn[pl.ds(b, pairs, stride=blocks), :] for b in range(blocks)], axis=0)
        lanes = rows.T
        both = jnp.concatenate([lanes[:C], lanes[C:]], axis=1).astype(BF16)
        return mxu(both, order).astype(BF16)

    def from_channels(value, out_ref):
        both = mxu(value, order, ((1,), (1,)))
        rows = jnp.concatenate([both[:, : n // 2], both[:, n // 2 :]], axis=0).T
        turn[...] = rows
        for j in range(pairs):
            flat[:, j * 2 * C : (j + 1) * 2 * C] = turn[pl.ds(j, blocks, stride=pairs), :]
        out_ref[...] = flat[...].astype(BF16)

    low_row = iota((1, 2 * V), 1) < V
    shift = blocks.bit_length() - 1

    def make_rows():
        for k in range(K):
            for b in range(blocks):
                source = src_ref[b, k]
                owner, place = source >> shift, source & (blocks - 1)
                slots[k * blocks + b] = jnp.where(
                    owner == s, place, jnp.where(owner < s, place + HALO, blocks + HALO + place)
                )
            start = k // 2 * 2 * V
            if start + 2 * V <= K * V:
                here = vox_ref[:, start : start + 2 * V]
            else:
                here = jnp.concatenate([vox_ref[:, start : start + V]] * 2, axis=1)
            there = pltpu.roll(here, V, 1)
            first, second = (here, there) if k % 2 == 0 else (there, here)
            for p in range(blocks // 2):
                row = jnp.where(low_row, first[2 * p : 2 * p + 1], second[2 * p + 1 : 2 * p + 2])
                none = row >= V
                base = jnp.where(low_row, slots[k * blocks + 2 * p] * V, slots[k * blocks + 2 * p + 1] * V)
                lanes = slice(p * 2 * V, (p + 1) * 2 * V)
                pair_rows[k, :, lanes] = jnp.where(none, -1, row + jnp.where(low_row, 0, V)).astype(F32)
                wide_rows[k, :, lanes] = jnp.where(none, -1, row + base).astype(F32)

    group_of = 9
    spot = iota((n, n), 0).astype(F32).astype(BF16)
    spot_pair = iota((2 * V, 2 * V), 0).astype(F32).astype(BF16)

    def hot(where, row):
        return jnp.where(where == row.astype(BF16), jnp.ones_like(where), jnp.zeros_like(where))

    def spread(w_ref, grad):
        for g in range(0, K, group_of):
            out = mxu(w_ref[g * C : (g + group_of) * C, :], grad).astype(BF16)
            back[g : g + group_of] = out.reshape(group_of, C, n)

    def scattered(lo):
        def some(g, total):
            for i in range(group_of):
                k = g * group_of + i
                total = total + mxu(back[k], hot(spot, wide_rows[k] - lo), ((1,), (1,)))
            return total

        return lax.fori_loop(0, K // group_of, some, jnp.zeros((C, n), F32))

    low16 = iota((C, 2 * V), 1).astype(F32).astype(BF16) < V
    low32 = iota((C, 2 * V), 1) < V

    def fill(table, value, first):
        value = value.astype(F32)
        turned = pltpu.roll(value, V, 1)
        table[first] = jnp.where(low32, value, turned).astype(BF16)
        table[first + 1] = jnp.where(low32, turned, value).astype(BF16)

    def fill_own(table, value):
        for p in range(blocks // 2):
            fill(table, value[:, p * 2 * V : (p + 1) * 2 * V], 2 * p)

    def fill_halo(table, ref):
        for i in range(2):
            fill(table, ref[i], blocks + 2 * i)

    def pick(table, picked):
        def one(g, carry):
            for i in range(group_of):
                k = g * group_of + i
                for p in range(blocks // 2):
                    lanes = slice(p * 2 * V, (p + 1) * 2 * V)
                    both = jnp.where(
                        low16, table[slots[k * blocks + 2 * p]], table[slots[k * blocks + 2 * p + 1]]
                    )
                    picked[k, :, lanes] = mxu(both, hot(spot_pair, pair_rows[k, :, lanes])).astype(BF16)
            return carry

        lax.fori_loop(0, K // group_of, one, 0)

    def convolved(wt, picked):
        return mxu(wt[...], picked[...].reshape(K * C, n))

    def weight_parts(which, picked, grad):
        zero = jnp.zeros((C, n), BF16)
        pair = jnp.concatenate(
            [jnp.concatenate([grad, zero], axis=1), jnp.concatenate([zero, grad], axis=1)], axis=0
        )
        for g in range(0, K, group_of):
            both = jnp.concatenate(
                [picked[g : g + group_of, 0 : C // 2, :], picked[g : g + group_of, C // 2 : C, :]], axis=2
            ).reshape(group_of * C // 2, 2 * n)
            out = mxu(both, pair, ((1,), (1,))).astype(BF16)
            tiles = group_of * C // 2 // TILE
            out = out.reshape(tiles, TILE, 2 * C)
            first = g * C // 2 // TILE
            cut = min(max(pad - first, 0), tiles)
            if cut > 0:
                parts[which, 0, first : first + cut] = out[:cut]
            if cut < tiles:
                parts[which, 1, first + cut - pad : first + tiles - pad] = out[cut:]

    def to_neighbours(slot, low, high, into):
        copies = [
            remote(low, into.at[1], halo_send.at[slot, 0], halo_recv.at[slot, 1], before),
            remote(high, into.at[0], halo_send.at[slot, 1], halo_recv.at[slot, 0], after),
        ]
        for copy in copies:
            copy.start()
        return copies

    def arrive(copies):
        for copy in copies:
            copy.wait_recv()

    offsets = [
        (dx, dy, dz) for dx in range(n_x) for dy in range(n_y) for dz in range(ZPAR) if (dx, dy, dz) != (0, 0, 0)
    ]
    offsets.sort(key=lambda o: -(min(o[0], n_x - o[0]) + min(o[1], n_y - o[1]) + o[2]))

    def member(x, y, z):
        return (z * n_y + y) * n_x + x

    me = member(x, y, z_par)

    def to_twin(stage, which, src, dst):
        copy = remote(src, dst, pair_send.at[stage, which], pair_recv.at[stage, which], twin)
        copy.start()
        return [copy]

    def to_members(stage, which, src_of, dst):
        copies = []
        for i, (dx, dy, dz) in enumerate(offsets):
            xx, yy, zz = (x + dx) % n_x, (y + dy) % n_y, (z_par + dz) % ZPAR
            target = (((z // ZPAR) * ZPAR + zz) * n_y + yy, xx * CORES + core)
            copy = remote(
                src_of(member(xx, yy, zz)), dst, group_send.at[stage, which, i], group_recv.at[stage, which, i], target
            )
            copy.start()
            copies.append(copy)
        return copies

    def to_depths(which, src, dst):
        copies = []
        for j in [j for i in range(deep // 2, 0, -1) for j in sorted({i, deep - i})]:
            target = at(dz=j * ZPAR)
            copy = remote(src, dst, deep_send.at[which, j - 1], deep_recv.at[which, j - 1], target)
            copy.start()
            copies.append(copy)
        return copies

    for which in range(2):
        mid[which, pad:] = jnp.zeros((mid.shape[1] - pad, TILE, 2 * C), BF16)
    loads["x"].wait()
    feat = to_channels(x_ref)
    feat_ref[...] = feat
    pl.semaphore_wait(barrier, len(near))
    feat_copies = to_neighbours(0, feat_ref.at[:, 0:half], feat_ref.at[:, half:n], halo_in)
    relay_signal(0)
    sent = list(feat_copies)

    loads["vox"].wait()
    loads["src"].wait()
    make_rows()
    loads["ct"].wait()
    cot = to_channels(ct_ref)
    loads["w2"].wait()
    spread(w2_ref, cot)
    rim = scattered(n).astype(BF16)
    for i in range(2):
        rim_out[0, i] = rim[:, i * half : (i + 1) * half]
    rim_copies = to_neighbours(1, rim_out.at[0, 0], rim_out.at[0, 1], rim_in.at[0])
    sent += rim_copies
    relay_wait(0)
    relay_signal(1)
    loads["w1"].wait()
    w1t[...] = w1_ref[...].T
    fill_own(table1, feat)

    arrive(feat_copies)
    fill_halo(table1, halo_in)
    pick(table1, picked1)
    pre = convolved(w1t, picked1)
    sig = 1.0 / (1.0 + jnp.exp(-pre))
    hid = (pre * sig).astype(BF16)
    hidden[...] = hid
    hid_copies = to_neighbours(2, hidden.at[:, 0:half], hidden.at[:, half:n], halo_mid)
    sent += hid_copies
    relay_wait(1)
    relay_signal(2)

    grad_hidden = scattered(0)
    arrive(rim_copies)
    rims = jnp.concatenate([rim_in[0, 0], rim_in[0, 1]], axis=1).astype(F32)
    grad_pre = ((grad_hidden + rims) * (sig * (1.0 + pre * (1.0 - sig)))).astype(BF16)
    weight_parts(0, picked1, grad_pre)

    def mine_of(which):
        return sums.at[which, core, pl.ds(me * per, per)]

    def reduce_pair(which):
        return to_twin(0, which, parts.at[which, 1 - core], got1.at[which])

    def scatter_reduce(which, copies):
        arrive(copies)
        mid[which, 0:pad] = (parts[which, core].astype(F32) + got1[which].astype(F32)).astype(BF16)
        got2[which, me] = mid[which, pl.ds(me * per, per)]
        return to_members(0, which, lambda other: mid.at[which, pl.ds(other * per, per)], got2.at[which, me])

    def added(ref, which, count):
        totals = [ref[which, i].astype(F32) for i in range(count)]
        while len(totals) > 1:
            totals = [a + b for a, b in zip(totals[::2], totals[1::2])]
        return totals[0].astype(BF16)

    def reduce_deep(which, copies):
        arrive(copies)
        got3[which, depth] = added(got2, which, len(offsets) + 1)
        mine = got3.at[which, depth]
        return to_depths(which, mine, mine)

    def gather_members(which, copies):
        arrive(copies)
        sums[which, core, pl.ds(me * per, per)] = added(got3, which, deep)
        mine = mine_of(which)
        return to_members(1, which, lambda other: mine, mine)

    def gather_pair(which, copies):
        arrive(copies)
        mine = sums.at[which, core, 0:pad]
        return to_twin(1, which, mine, mine)

    factor = float(n_x * CORES * space * n) ** (-0.5)

    def lay_out(which, side, out):
        for i in range(pad):
            tile = side * pad + i
            k = tile // 2
            value = sums[which, side, i].astype(F32) * factor
            top = pl.multiple_of(tile % 2 * TILE, TILE)
            out[k, pl.ds(top, TILE), :] = value[:, :C]
            out[k, pl.ds(top + C // 2, TILE), :] = value[:, C:]

    def drain(copies):
        for copy in copies:
            copy.wait_send()

    one = reduce_pair(0)
    sent += one
    fill_own(table2, hid)
    relay_wait(2)
    relay_signal(3)
    w2t[...] = w2_ref[...].T
    relay_wait(3)
    one = scatter_reduce(0, one)
    sent += one
    arrive(hid_copies)
    fill_halo(table2, halo_mid)
    pick(table2, picked2)
    weight_parts(1, picked2, cot)
    two = reduce_pair(1)
    sent += two

    spread(w1_ref, grad_pre)
    two = scatter_reduce(1, two)
    sent += two
    rim = scattered(n).astype(BF16)
    for i in range(2):
        rim_out[1, i] = rim[:, i * half : (i + 1) * half]
    last_copies = to_neighbours(3, rim_out.at[1, 0], rim_out.at[1, 1], rim_in.at[1])
    sent += last_copies
    from_channels(convolved(w2t, picked2).astype(BF16), conv_ref)

    relay_end()
    one = reduce_deep(0, one)
    sent += one
    grad_in = scattered(0)
    two = reduce_deep(1, two)
    sent += two
    arrive(last_copies)
    rims = jnp.concatenate([rim_in[1, 0], rim_in[1, 1]], axis=1).astype(F32)
    from_channels((grad_in + rims).astype(BF16), gin_ref)
    drain(sent)

    one = gather_members(0, one)
    sent = list(one)
    two = gather_members(1, two)
    sent += two
    one = gather_pair(0, one)
    sent += one
    lay_out(0, core, grad1_ref)
    arrive(one)
    lay_out(0, 1 - core, grad1_ref)
    two = gather_pair(1, two)
    drain(sent)
    lay_out(1, core, grad2_ref)
    arrive(two)
    lay_out(1, 1 - core, grad2_ref)
    drain(two)


def put_kernel(*refs):
    count = len(refs) // 2
    sem = refs[-1]
    copies = []
    for i, (src, dst) in enumerate(zip(refs[:count], refs[count:-1])):
        size = src.shape[0]
        cuts = 3 if size == K else 1
        for c in range(cuts):
            part = pl.ds(c * size // cuts, size // cuts)
            copies.append(pltpu.make_async_copy(src.at[part], dst.at[part], sem.at[i, c]))
    for copy in copies:
        copy.start()
    for copy in copies:
        copy.wait()


def per_device(sizes, features, sources, voxels, cotangent, weight_one, weight_two):
    n_x, n_y, n_z = sizes
    members = n_x * n_y * ZPAR
    deep = n_z // ZPAR
    blocks = features.shape[1]
    n = blocks * V
    half = n // 2
    pad = TILES // CORES
    per = -(-pad // members)
    slots = blocks + 2 * HALO
    scratch = [
        pltpu.VMEM((blocks, V * C), BF16),
        pltpu.VMEM((blocks, V * C), BF16),
        pltpu.SMEM((blocks, K), jnp.int32),
        pltpu.VMEM((blocks, K * V), jnp.int32),
        pltpu.VMEM((K * C, C), BF16),
        pltpu.VMEM((K * C, C), BF16),
        pltpu.SMEM((K * blocks,), jnp.int32),
        pltpu.VMEM((K, 1, n), F32),
        pltpu.VMEM((K, 1, n), F32),
        pltpu.VMEM((n // 2, 2 * C), F32),
        pltpu.VMEM((blocks, V * C), F32),
        pltpu.VMEM((slots, C, 2 * V), BF16),
        pltpu.VMEM((slots, C, 2 * V), BF16),
        pltpu.VMEM((C, n), BF16),
        pltpu.VMEM((K, C, n), BF16),
        pltpu.VMEM((K, C, n), BF16),
        pltpu.VMEM((K, C, n), BF16),
        pltpu.VMEM((C, K * C), BF16),
        pltpu.VMEM((C, K * C), BF16),
        pltpu.VMEM((2, C, half), BF16),
        pltpu.VMEM((2, C, half), BF16),
        pltpu.VMEM((2, 2, C, half), BF16),
        pltpu.VMEM((2, 2, C, half), BF16),
        pltpu.VMEM((C, n), BF16),
        pltpu.VMEM((2, CORES, pad, TILE, 2 * C), BF16),
        pltpu.VMEM((2, pad, TILE, 2 * C), BF16),
        pltpu.VMEM((2, members * per, TILE, 2 * C), BF16),
        pltpu.VMEM((2, members, per, TILE, 2 * C), BF16),
        pltpu.VMEM((2, deep, per, TILE, 2 * C), BF16),
        pltpu.VMEM((2, CORES, members * per, TILE, 2 * C), BF16),
        pltpu.SemaphoreType.DMA((6,)),
        pltpu.SemaphoreType.DMA((4, 2)),
        pltpu.SemaphoreType.DMA((4, 2)),
        pltpu.SemaphoreType.DMA((2, 2)),
        pltpu.SemaphoreType.DMA((2, 2)),
        pltpu.SemaphoreType.DMA((2, 2, members - 1)),
        pltpu.SemaphoreType.DMA((2, 2, members - 1)),
        pltpu.SemaphoreType.DMA((2, deep - 1)),
        pltpu.SemaphoreType.DMA((2, deep - 1)),
        pltpu.SemaphoreType.REGULAR((8,)),
    ]
    outs = (
        jax.ShapeDtypeStruct((blocks, V * C), BF16),
        jax.ShapeDtypeStruct((blocks, V * C), BF16),
        jax.ShapeDtypeStruct((K, C, C), F32),
        jax.ShapeDtypeStruct((K, C, C), F32),
    )
    vmem = pl.BlockSpec(memory_space=pltpu.VMEM)
    anywhere = pl.BlockSpec(memory_space=pl.ANY)
    hbm = pl.BlockSpec(memory_space=pltpu.HBM)
    results = pl.pallas_call(
        functools.partial(step_kernel, sizes),
        out_shape=outs,
        in_specs=[hbm] * 6,
        out_specs=(vmem,) * 4,
        scratch_shapes=scratch,
        compiler_params=pltpu.CompilerParams(
            collective_id=0, has_side_effects=True, vmem_limit_bytes=32 * 1024 * 1024
        ),
        name="step",
    )(
        *[
            pltpu.with_memory_space_constraint(a, pltpu.HBM)
            for a in (
                features[0],
                cotangent[0],
                sources[0],
                voxels[0],
                weight_one.reshape(K * C, C),
                weight_two.reshape(K * C, C),
            )
        ]
    )
    conv, gin, grad_one, grad_two = pl.pallas_call(
        put_kernel,
        out_shape=outs,
        in_specs=[anywhere] * 4,
        out_specs=(hbm,) * 4,
        scratch_shapes=[pltpu.SemaphoreType.DMA((4, 3))],
        compiler_params=pltpu.CompilerParams(vmem_limit_bytes=1024 * 1024),
        name="put",
    )(*results)
    return conv[None], gin[None], grad_one, grad_two


def solution(mesh):
    space, dp = mesh.shape["space"], mesh.shape["dp"]
    sizes = (dp // CORES, Y, space // Y)
    wide = P("dp", "space", None)
    return jax.shard_map(
        functools.partial(per_device, sizes),
        mesh=mesh,
        in_specs=(wide, wide, wide, wide, P(), P()),
        out_specs=(wide, wide, P(), P()),
        check_vma=False,
    )
```

```python
import functools

import jax
import jax.numpy as jnp
from jax import lax
from jax.experimental import pallas as pl
from jax.experimental.pallas import tpu as pltpu
from jax.sharding import PartitionSpec as P

C = 64
V = 64
K = 27
HALO = 2
Y = 4
ZPAR = 2
CORES = 2
TILE = 16
TILES = K * C * C // (TILE * 2 * C)
MESH = pl.DeviceIdType.MESH
BF16 = jnp.bfloat16
F32 = jnp.float32


def mxu(a, b, dims=((1,), (0,))):
    return lax.dot_general(a, b, (dims, ((), ())), preferred_element_type=F32)


def step_kernel(
    sizes,
    x_hbm,
    ct_hbm,
    src_hbm,
    vox_hbm,
    w1_hbm,
    w2_hbm,
    conv_ref,
    gin_ref,
    grad1_ref,
    grad2_ref,
    x_ref,
    ct_ref,
    src_ref,
    vox_ref,
    w1_ref,
    w2_ref,
    slots,
    pair_rows,
    wide_rows,
    turn,
    flat,
    table1,
    table2,
    feat_ref,
    picked1,
    picked2,
    back,
    w1t,
    w2t,
    halo_in,
    halo_mid,
    rim_out,
    rim_in,
    hidden,
    parts,
    got1,
    mid,
    got2,
    got3,
    sums,
    load_sem,
    halo_send,
    halo_recv,
    pair_send,
    pair_recv,
    group_send,
    group_recv,
    deep_send,
    deep_recv,
    relay,
):
    n_x, n_y, n_z = sizes
    deep = n_z // ZPAR
    space = n_y * n_z
    blocks = x_ref.shape[0]
    n = feat_ref.shape[1]
    half = n // 2
    s = lax.axis_index("space")
    d = lax.axis_index("dp")
    x, core = d // CORES, d % CORES
    z, y = s // n_y, s % n_y
    z_par, depth = z % ZPAR, z // ZPAR
    pad = TILES // CORES
    per = sums.shape[2] // (n_x * n_y * ZPAR)

    def at(dx=0, dy=0, dz=0, core=core):
        return (((z + dz) % n_z) * n_y + (y + dy) % n_y, ((x + dx) % n_x) * CORES + core)

    before = ((s + space - 1) % space, d)
    after = ((s + 1) % space, d)
    twin = at(core=1 - core)
    x_pair = [at(dx=1), at(dx=n_x - 1)]
    y_pair = [at(dy=1), at(dy=n_y - 1)]

    def z_pair(step):
        return [at(dz=step), at(dz=n_z - step)]

    other_z = (((z // ZPAR) * ZPAR + 1 - z_par) * n_y + y, d)

    def signal(sem, devices):
        for device in devices:
            pl.semaphore_signal(sem, inc=1, device_id=device, device_id_type=MESH)

    barrier = pltpu.get_barrier_semaphore()
    near = [before, after, twin] + x_pair + y_pair + z_pair(1)
    signal(barrier, near)

    z_steps = []
    while 2 ** len(z_steps) < n_z // 2:
        z_steps.append(2 ** len(z_steps))

    def relay_signal(i):
        if i == 0:
            signal(relay.at[0], x_pair)
        elif i <= 2:
            signal(relay.at[i], y_pair)
        else:
            signal(relay.at[i], [other_z])
        if i < len(z_steps):
            signal(relay.at[4 + i], z_pair(z_steps[i]))

    def relay_wait(i):
        pl.semaphore_wait(relay.at[i], 2 if i <= 2 else 1)
        if i < len(z_steps) - 1:
            pl.semaphore_wait(relay.at[4 + i], 2)

    def relay_end():
        pl.semaphore_wait(relay.at[4 + len(z_steps) - 1], 2)

    def remote(src, dst, send, recv, target):
        return pltpu.make_async_remote_copy(
            src_ref=src, dst_ref=dst, send_sem=send, recv_sem=recv, device_id=target, device_id_type=MESH
        )

    loads = {}
    for i, (name, src, dst) in enumerate(
        (
            ("vox", vox_hbm, vox_ref),
            ("src", src_hbm, src_ref),
            ("x", x_hbm, x_ref),
            ("ct", ct_hbm, ct_ref),
            ("w2", w2_hbm, w2_ref),
            ("w1", w1_hbm, w1_ref),
        )
    ):
        loads[name] = pltpu.make_async_copy(src, dst, load_sem.at[i])
        loads[name].start()

    def iota(shape, dim):
        return lax.broadcasted_iota(jnp.int32, shape, dim)

    pairs = V // 2
    old = iota((n, n), 0)
    parity, rest = old // (n // 2), old % (n // 2)
    order = jnp.where(rest // pairs * V + rest % pairs * 2 + parity == iota((n, n), 1), 1.0, 0.0).astype(BF16)

    def to_channels(ref):
        wide = ref[...].astype(F32)
        for j in range(pairs):
            turn[j * blocks : (j + 1) * blocks, :] = wide[:, j * 2 * C : (j + 1) * 2 * C]
        rows = jnp.concatenate([turn[pl.ds(b, pairs, stride=blocks), :] for b in range(blocks)], axis=0)
        lanes = rows.T
        both = jnp.concatenate([lanes[:C], lanes[C:]], axis=1).astype(BF16)
        return mxu(both, order).astype(BF16)

    def from_channels(value, out_ref):
        both = mxu(value, order, ((1,), (1,)))
        rows = jnp.concatenate([both[:, : n // 2], both[:, n // 2 :]], axis=0).T
        turn[...] = rows
        for j in range(pairs):
            flat[:, j * 2 * C : (j + 1) * 2 * C] = turn[pl.ds(j, blocks, stride=pairs), :]
        out_ref[...] = flat[...].astype(BF16)

    low_row = iota((1, 2 * V), 1) < V
    shift = blocks.bit_length() - 1

    def make_rows():
        for k in range(K):
            for b in range(blocks):
                source = src_ref[b, k]
                owner, place = source >> shift, source & (blocks - 1)
                slots[k * blocks + b] = jnp.where(
                    owner == s, place, jnp.where(owner < s, place + HALO, blocks + HALO + place)
                )
            start = k // 2 * 2 * V
            if start + 2 * V <= K * V:
                here = vox_ref[:, start : start + 2 * V]
            else:
                here = jnp.concatenate([vox_ref[:, start : start + V]] * 2, axis=1)
            there = pltpu.roll(here, V, 1)
            first, second = (here, there) if k % 2 == 0 else (there, here)
            for p in range(blocks // 2):
                row = jnp.where(low_row, first[2 * p : 2 * p + 1], second[2 * p + 1 : 2 * p + 2])
                none = row >= V
                base = jnp.where(low_row, slots[k * blocks + 2 * p] * V, slots[k * blocks + 2 * p + 1] * V)
                lanes = slice(p * 2 * V, (p + 1) * 2 * V)
                pair_rows[k, :, lanes] = jnp.where(none, -1, row + jnp.where(low_row, 0, V)).astype(F32)
                wide_rows[k, :, lanes] = jnp.where(none, -1, row + base).astype(F32)

    group_of = 9
    spot = iota((n, n), 0).astype(F32).astype(BF16)
    spot_pair = iota((2 * V, 2 * V), 0).astype(F32).astype(BF16)

    def hot(where, row):
        return jnp.where(where == row.astype(BF16), jnp.ones_like(where), jnp.zeros_like(where))

    def spread(w_ref, grad):
        for g in range(0, K, group_of):
            out = mxu(w_ref[g * C : (g + group_of) * C, :], grad).astype(BF16)
            back[g : g + group_of] = out.reshape(group_of, C, n)

    def scattered(lo):
        def some(g, total):
            for i in range(group_of):
                k = g * group_of + i
                total = total + mxu(back[k], hot(spot, wide_rows[k] - lo), ((1,), (1,)))
            return total

        return lax.fori_loop(0, K // group_of, some, jnp.zeros((C, n), F32))

    low16 = iota((C, 2 * V), 1).astype(F32).astype(BF16) < V
    low32 = iota((C, 2 * V), 1) < V

    def fill(table, value, first):
        value = value.astype(F32)
        turned = pltpu.roll(value, V, 1)
        table[first] = jnp.where(low32, value, turned).astype(BF16)
        table[first + 1] = jnp.where(low32, turned, value).astype(BF16)

    def fill_own(table, value):
        for p in range(blocks // 2):
            fill(table, value[:, p * 2 * V : (p + 1) * 2 * V], 2 * p)

    def fill_halo(table, ref):
        for i in range(2):
            fill(table, ref[i], blocks + 2 * i)

    def pick(table, picked):
        def one(g, carry):
            for i in range(group_of):
                k = g * group_of + i
                for p in range(blocks // 2):
                    lanes = slice(p * 2 * V, (p + 1) * 2 * V)
                    both = jnp.where(
                        low16, table[slots[k * blocks + 2 * p]], table[slots[k * blocks + 2 * p + 1]]
                    )
                    picked[k, :, lanes] = mxu(both, hot(spot_pair, pair_rows[k, :, lanes])).astype(BF16)
            return carry

        lax.fori_loop(0, K // group_of, one, 0)

    def convolved(wt, picked):
        return mxu(wt[...], picked[...].reshape(K * C, n))

    def weight_parts(which, picked, grad):
        zero = jnp.zeros((C, n), BF16)
        pair = jnp.concatenate(
            [jnp.concatenate([grad, zero], axis=1), jnp.concatenate([zero, grad], axis=1)], axis=0
        )
        for g in range(0, K, group_of):
            both = jnp.concatenate(
                [picked[g : g + group_of, 0 : C // 2, :], picked[g : g + group_of, C // 2 : C, :]], axis=2
            ).reshape(group_of * C // 2, 2 * n)
            out = mxu(both, pair, ((1,), (1,))).astype(BF16)
            tiles = group_of * C // 2 // TILE
            out = out.reshape(tiles, TILE, 2 * C)
            first = g * C // 2 // TILE
            cut = min(max(pad - first, 0), tiles)
            if cut > 0:
                parts[which, 0, first : first + cut] = out[:cut]
            if cut < tiles:
                parts[which, 1, first + cut - pad : first + tiles - pad] = out[cut:]

    class Batch:
        def __init__(self, copies, send, recv, sent, landed):
            for copy in copies:
                copy.start()
            self.all = remote(sent, landed, send, recv, twin)

        def wait_recv(self):
            self.all.wait_recv()

        def wait_send(self):
            self.all.wait_send()

    def to_neighbours(slot, low, high, into):
        send, recv = halo_send.at[slot], halo_recv.at[slot]
        copies = [remote(low, into.at[1], send, recv, before), remote(high, into.at[0], send, recv, after)]
        return [Batch(copies, send, recv, into, into)]

    def arrive(copies):
        for copy in copies:
            copy.wait_recv()

    offsets = [
        (dx, dy, dz) for dx in range(n_x) for dy in range(n_y) for dz in range(ZPAR) if (dx, dy, dz) != (0, 0, 0)
    ]
    offsets.sort(key=lambda o: -(min(o[0], n_x - o[0]) + min(o[1], n_y - o[1]) + o[2]))

    def member(x, y, z):
        return (z * n_y + y) * n_x + x

    me = member(x, y, z_par)

    def to_twin(stage, which, src, dst):
        copy = remote(src, dst, pair_send.at[stage, which], pair_recv.at[stage, which], twin)
        copy.start()
        return [copy]

    def to_members(stage, which, src_of, dst, all_of):
        send, recv = group_send.at[stage, which], group_recv.at[stage, which]
        copies = []
        for dx, dy, dz in offsets:
            xx, yy, zz = (x + dx) % n_x, (y + dy) % n_y, (z_par + dz) % ZPAR
            target = (((z // ZPAR) * ZPAR + zz) * n_y + yy, xx * CORES + core)
            copies.append(remote(src_of(member(xx, yy, zz)), dst, send, recv, target))
        return [Batch(copies, send, recv, all_of, all_of)]

    def to_depths(which, src, dst):
        send, recv = deep_send.at[which], deep_recv.at[which]
        copies = []
        for j in [j for i in range(deep // 2, 0, -1) for j in sorted({i, deep - i})]:
            copies.append(remote(src, dst, send, recv, at(dz=j * ZPAR)))
        every = got3.at[which, 0 : deep - 1]
        return [Batch(copies, send, recv, every, every)]

    for which in range(2):
        mid[which, pad:] = jnp.zeros((mid.shape[1] - pad, TILE, 2 * C), BF16)
    loads["x"].wait()
    feat = to_channels(x_ref)
    feat_ref[...] = feat
    pl.semaphore_wait(barrier, len(near))
    feat_copies = to_neighbours(0, feat_ref.at[:, 0:half], feat_ref.at[:, half:n], halo_in)
    relay_signal(0)
    sent = list(feat_copies)

    loads["vox"].wait()
    loads["src"].wait()
    make_rows()
    loads["ct"].wait()
    cot = to_channels(ct_ref)
    loads["w2"].wait()
    spread(w2_ref, cot)
    rim = scattered(n).astype(BF16)
    for i in range(2):
        rim_out[0, i] = rim[:, i * half : (i + 1) * half]
    rim_copies = to_neighbours(1, rim_out.at[0, 0], rim_out.at[0, 1], rim_in.at[0])
    sent += rim_copies
    relay_wait(0)
    relay_signal(1)
    loads["w1"].wait()
    w1t[...] = w1_ref[...].T
    fill_own(table1, feat)

    arrive(feat_copies)
    fill_halo(table1, halo_in)
    pick(table1, picked1)
    pre = convolved(w1t, picked1)
    sig = 1.0 / (1.0 + jnp.exp(-pre))
    hid = (pre * sig).astype(BF16)
    hidden[...] = hid
    hid_copies = to_neighbours(2, hidden.at[:, 0:half], hidden.at[:, half:n], halo_mid)
    sent += hid_copies
    relay_wait(1)
    relay_signal(2)

    grad_hidden = scattered(0)
    arrive(rim_copies)
    rims = jnp.concatenate([rim_in[0, 0], rim_in[0, 1]], axis=1).astype(F32)
    grad_pre = ((grad_hidden + rims) * (sig * (1.0 + pre * (1.0 - sig)))).astype(BF16)
    weight_parts(0, picked1, grad_pre)

    def mine_of(which):
        return sums.at[which, core, pl.ds(me * per, per)]

    def reduce_pair(which):
        return to_twin(0, which, parts.at[which, 1 - core], got1.at[which])

    def scatter_reduce(which, copies):
        arrive(copies)
        mid[which, 0:pad] = (parts[which, core].astype(F32) + got1[which].astype(F32)).astype(BF16)
        got2[which, me] = mid[which, pl.ds(me * per, per)]
        every = got2.at[which, 0 : len(offsets)]
        return to_members(
            0, which, lambda other: mid.at[which, pl.ds(other * per, per)], got2.at[which, me], every
        )

    def added(ref, which, count):
        totals = [ref[which, i].astype(F32) for i in range(count)]
        while len(totals) > 1:
            totals = [a + b for a, b in zip(totals[::2], totals[1::2])]
        return totals[0].astype(BF16)

    def reduce_deep(which, copies):
        arrive(copies)
        got3[which, depth] = added(got2, which, len(offsets) + 1)
        mine = got3.at[which, depth]
        return to_depths(which, mine, mine)

    def gather_members(which, copies):
        arrive(copies)
        sums[which, core, pl.ds(me * per, per)] = added(got3, which, deep)
        mine = mine_of(which)
        every = sums.at[which, core, 0 : len(offsets) * per]
        return to_members(1, which, lambda other: mine, mine, every)

    def gather_pair(which, copies):
        arrive(copies)
        mine = sums.at[which, core, 0:pad]
        return to_twin(1, which, mine, mine)

    factor = float(n_x * CORES * space * n) ** (-0.5)

    def lay_out(which, side, out):
        for i in range(pad):
            tile = side * pad + i
            k = tile // 2
            value = sums[which, side, i].astype(F32) * factor
            top = pl.multiple_of(tile % 2 * TILE, TILE)
            out[k, pl.ds(top, TILE), :] = value[:, :C]
            out[k, pl.ds(top + C // 2, TILE), :] = value[:, C:]

    def drain(copies):
        for copy in copies:
            copy.wait_send()

    one = reduce_pair(0)
    sent += one
    fill_own(table2, hid)
    relay_wait(2)
    relay_signal(3)
    w2t[...] = w2_ref[...].T
    relay_wait(3)
    one = scatter_reduce(0, one)
    sent += one
    arrive(hid_copies)
    fill_halo(table2, halo_mid)
    pick(table2, picked2)
    weight_parts(1, picked2, cot)
    two = reduce_pair(1)
    sent += two

    spread(w1_ref, grad_pre)
    two = scatter_reduce(1, two)
    sent += two
    rim = scattered(n).astype(BF16)
    for i in range(2):
        rim_out[1, i] = rim[:, i * half : (i + 1) * half]
    last_copies = to_neighbours(3, rim_out.at[1, 0], rim_out.at[1, 1], rim_in.at[1])
    sent += last_copies
    from_channels(convolved(w2t, picked2).astype(BF16), conv_ref)

    relay_end()
    one = reduce_deep(0, one)
    sent += one
    grad_in = scattered(0)
    two = reduce_deep(1, two)
    sent += two
    one = gather_members(0, one)
    sent += one
    arrive(last_copies)
    rims = jnp.concatenate([rim_in[1, 0], rim_in[1, 1]], axis=1).astype(F32)
    grad_input = (grad_in + rims).astype(BF16)
    two = gather_members(1, two)
    sent += two
    from_channels(grad_input, gin_ref)
    one = gather_pair(0, one)
    sent += one
    lay_out(0, core, grad1_ref)
    arrive(one)
    lay_out(0, 1 - core, grad1_ref)
    two = gather_pair(1, two)
    drain(sent)
    lay_out(1, core, grad2_ref)
    arrive(two)
    lay_out(1, 1 - core, grad2_ref)
    drain(two)


def put_kernel(*refs):
    count = len(refs) // 2
    sem = refs[-1]
    copies = []
    for i, (src, dst) in enumerate(zip(refs[:count], refs[count:-1])):
        size = src.shape[0]
        cuts = 3 if size == K else 1
        for c in range(cuts):
            part = pl.ds(c * size // cuts, size // cuts)
            copies.append(pltpu.make_async_copy(src.at[part], dst.at[part], sem.at[i, c]))
    for copy in copies:
        copy.start()
    for copy in copies:
        copy.wait()


def per_device(sizes, features, sources, voxels, cotangent, weight_one, weight_two):
    n_x, n_y, n_z = sizes
    members = n_x * n_y * ZPAR
    deep = n_z // ZPAR
    blocks = features.shape[1]
    n = blocks * V
    half = n // 2
    pad = TILES // CORES
    per = -(-pad // members)
    slots = blocks + 2 * HALO
    scratch = [
        pltpu.VMEM((blocks, V * C), BF16),
        pltpu.VMEM((blocks, V * C), BF16),
        pltpu.SMEM((blocks, K), jnp.int32),
        pltpu.VMEM((blocks, K * V), jnp.int32),
        pltpu.VMEM((K * C, C), BF16),
        pltpu.VMEM((K * C, C), BF16),
        pltpu.SMEM((K * blocks,), jnp.int32),
        pltpu.VMEM((K, 1, n), F32),
        pltpu.VMEM((K, 1, n), F32),
        pltpu.VMEM((n // 2, 2 * C), F32),
        pltpu.VMEM((blocks, V * C), F32),
        pltpu.VMEM((slots, C, 2 * V), BF16),
        pltpu.VMEM((slots, C, 2 * V), BF16),
        pltpu.VMEM((C, n), BF16),
        pltpu.VMEM((K, C, n), BF16),
        pltpu.VMEM((K, C, n), BF16),
        pltpu.VMEM((K, C, n), BF16),
        pltpu.VMEM((C, K * C), BF16),
        pltpu.VMEM((C, K * C), BF16),
        pltpu.VMEM((2, C, half), BF16),
        pltpu.VMEM((2, C, half), BF16),
        pltpu.VMEM((2, 2, C, half), BF16),
        pltpu.VMEM((2, 2, C, half), BF16),
        pltpu.VMEM((C, n), BF16),
        pltpu.VMEM((2, CORES, pad, TILE, 2 * C), BF16),
        pltpu.VMEM((2, pad, TILE, 2 * C), BF16),
        pltpu.VMEM((2, members * per, TILE, 2 * C), BF16),
        pltpu.VMEM((2, members, per, TILE, 2 * C), BF16),
        pltpu.VMEM((2, deep, per, TILE, 2 * C), BF16),
        pltpu.VMEM((2, CORES, members * per, TILE, 2 * C), BF16),
        pltpu.SemaphoreType.DMA((6,)),
        pltpu.SemaphoreType.DMA((4,)),
        pltpu.SemaphoreType.DMA((4,)),
        pltpu.SemaphoreType.DMA((2, 2)),
        pltpu.SemaphoreType.DMA((2, 2)),
        pltpu.SemaphoreType.DMA((2, 2)),
        pltpu.SemaphoreType.DMA((2, 2)),
        pltpu.SemaphoreType.DMA((2,)),
        pltpu.SemaphoreType.DMA((2,)),
        pltpu.SemaphoreType.REGULAR((7,)),
    ]
    outs = (
        jax.ShapeDtypeStruct((blocks, V * C), BF16),
        jax.ShapeDtypeStruct((blocks, V * C), BF16),
        jax.ShapeDtypeStruct((K, C, C), F32),
        jax.ShapeDtypeStruct((K, C, C), F32),
    )
    vmem = pl.BlockSpec(memory_space=pltpu.VMEM)
    anywhere = pl.BlockSpec(memory_space=pl.ANY)
    hbm = pl.BlockSpec(memory_space=pltpu.HBM)
    results = pl.pallas_call(
        functools.partial(step_kernel, sizes),
        out_shape=outs,
        in_specs=[hbm] * 6,
        out_specs=(vmem,) * 4,
        scratch_shapes=scratch,
        compiler_params=pltpu.CompilerParams(
            collective_id=0, has_side_effects=True, vmem_limit_bytes=32 * 1024 * 1024
        ),
        name="step",
    )(
        *[
            pltpu.with_memory_space_constraint(a, pltpu.HBM)
            for a in (
                features[0],
                cotangent[0],
                sources[0],
                voxels[0],
                weight_one.reshape(K * C, C),
                weight_two.reshape(K * C, C),
            )
        ]
    )
    conv, gin, grad_one, grad_two = pl.pallas_call(
        put_kernel,
        out_shape=outs,
        in_specs=[anywhere] * 4,
        out_specs=(hbm,) * 4,
        scratch_shapes=[pltpu.SemaphoreType.DMA((4, 3))],
        compiler_params=pltpu.CompilerParams(vmem_limit_bytes=1024 * 1024),
        name="put",
    )(*results)
    return conv[None], gin[None], grad_one, grad_two


def solution(mesh):
    space, dp = mesh.shape["space"], mesh.shape["dp"]
    sizes = (dp // CORES, Y, space // Y)
    wide = P("dp", "space", None)
    return jax.shard_map(
        functools.partial(per_device, sizes),
        mesh=mesh,
        in_specs=(wide, wide, wide, wide, P(), P()),
        out_specs=(wide, wide, P(), P()),
        check_vma=False,
    )
```

```python
import functools

import jax
import jax.numpy as jnp
from jax import lax
from jax.experimental import pallas as pl
from jax.experimental.pallas import tpu as pltpu
from jax.sharding import PartitionSpec as P

C = 64
V = 64
K = 27
HALO = 2
Y = 4
ZPAR = 2
CORES = 2
TILE = 16
K_EVEN = K + K % 2
TILES = K_EVEN * C * C // (TILE * 2 * C)
MESH = pl.DeviceIdType.MESH
BF16 = jnp.bfloat16
F32 = jnp.float32


def mxu(a, b, dims=((1,), (0,))):
    return lax.dot_general(a, b, (dims, ((), ())), preferred_element_type=F32)


def step_kernel(
    sizes,
    x_hbm,
    ct_hbm,
    src_hbm,
    vox_hbm,
    w1_hbm,
    w2_hbm,
    conv_ref,
    gin_ref,
    grad1_ref,
    grad2_ref,
    x_ref,
    ct_ref,
    src_ref,
    vox_ref,
    w1_ref,
    w2_ref,
    slots,
    pair_rows,
    wide_rows,
    turn,
    flat,
    table1,
    table2,
    feat_ref,
    picked1,
    picked2,
    back,
    spreads,
    w2p,
    w1t,
    w2t,
    halo_in,
    halo_mid,
    rim_out,
    rim_in,
    hidden,
    parts,
    got1,
    mid,
    got2,
    got3,
    sums,
    load_sem,
    halo_send,
    halo_recv,
    pair_send,
    pair_recv,
    group_send,
    group_recv,
    deep_send,
    deep_recv,
    relay,
):
    n_x, n_y, n_z = sizes
    deep = n_z // ZPAR
    space = n_y * n_z
    blocks = x_ref.shape[0]
    n = feat_ref.shape[1]
    half = n // 2
    s = lax.axis_index("space")
    d = lax.axis_index("dp")
    x, core = d // CORES, d % CORES
    z, y = s // n_y, s % n_y
    z_par, depth = z % ZPAR, z // ZPAR
    pad = TILES // CORES
    per = sums.shape[2] // (n_x * n_y * ZPAR)

    def at(dx=0, dy=0, dz=0, core=core):
        return (((z + dz) % n_z) * n_y + (y + dy) % n_y, ((x + dx) % n_x) * CORES + core)

    before = ((s + space - 1) % space, d)
    after = ((s + 1) % space, d)
    twin = at(core=1 - core)
    x_pair = [at(dx=1), at(dx=n_x - 1)]
    y_pair = [at(dy=1), at(dy=n_y - 1)]

    def z_pair(step):
        return [at(dz=step), at(dz=n_z - step)]

    other_z = (((z // ZPAR) * ZPAR + 1 - z_par) * n_y + y, d)

    def signal(sem, devices):
        for device in devices:
            pl.semaphore_signal(sem, inc=1, device_id=device, device_id_type=MESH)

    barrier = pltpu.get_barrier_semaphore()
    near = [before, after, twin] + x_pair + y_pair + z_pair(1)
    signal(barrier, near)

    z_steps = []
    while 2 ** len(z_steps) < n_z // 2:
        z_steps.append(2 ** len(z_steps))

    def relay_signal(i):
        if i == 0:
            signal(relay.at[0], x_pair)
        elif i <= 2:
            signal(relay.at[i], y_pair)
        else:
            signal(relay.at[i], [other_z])
        if i < len(z_steps):
            signal(relay.at[4 + i], z_pair(z_steps[i]))

    def relay_wait(i):
        pl.semaphore_wait(relay.at[i], 2 if i <= 2 else 1)
        if i < len(z_steps) - 1:
            pl.semaphore_wait(relay.at[4 + i], 2)

    def relay_end():
        pl.semaphore_wait(relay.at[4 + len(z_steps) - 1], 2)

    def remote(src, dst, send, recv, target):
        return pltpu.make_async_remote_copy(
            src_ref=src, dst_ref=dst, send_sem=send, recv_sem=recv, device_id=target, device_id_type=MESH
        )

    loads = {}
    for i, (name, src, dst) in enumerate(
        (
            ("vox", vox_hbm, vox_ref),
            ("src", src_hbm, src_ref),
            ("x", x_hbm, x_ref),
            ("ct", ct_hbm, ct_ref),
            ("w2", w2_hbm, w2_ref),
            ("w1", w1_hbm, w1_ref),
        )
    ):
        loads[name] = pltpu.make_async_copy(src, dst, load_sem.at[i])
        loads[name].start()

    def iota(shape, dim):
        return lax.broadcasted_iota(jnp.int32, shape, dim)

    pairs = V // 2
    old = iota((n, n), 0)
    parity, rest = old // (n // 2), old % (n // 2)
    order = jnp.where(rest // pairs * V + rest % pairs * 2 + parity == iota((n, n), 1), 1.0, 0.0).astype(BF16)

    def to_channels(ref):
        wide = ref[...].astype(F32)
        for j in range(pairs):
            turn[j * blocks : (j + 1) * blocks, :] = wide[:, j * 2 * C : (j + 1) * 2 * C]
        rows = jnp.concatenate([turn[pl.ds(b, pairs, stride=blocks), :] for b in range(blocks)], axis=0)
        lanes = rows.T
        both = jnp.concatenate([lanes[:C], lanes[C:]], axis=1).astype(BF16)
        return mxu(both, order).astype(BF16)

    def from_channels(value, out_ref):
        both = mxu(value, order, ((1,), (1,)))
        rows = jnp.concatenate([both[:, : n // 2], both[:, n // 2 :]], axis=0).T
        turn[...] = rows
        for j in range(pairs):
            flat[:, j * 2 * C : (j + 1) * 2 * C] = turn[pl.ds(j, blocks, stride=pairs), :]
        out_ref[...] = flat[...].astype(BF16)

    low_row = iota((1, 2 * V), 1) < V
    shift = blocks.bit_length() - 1

    def make_rows():
        for k in range(K):
            for b in range(blocks):
                source = src_ref[b, k]
                owner, place = source >> shift, source & (blocks - 1)
                slots[k * blocks + b] = jnp.where(
                    owner == s, place, jnp.where(owner < s, place + HALO, blocks + HALO + place)
                )
            start = k // 2 * 2 * V
            if start + 2 * V <= K * V:
                here = vox_ref[:, start : start + 2 * V]
            else:
                here = jnp.concatenate([vox_ref[:, start : start + V]] * 2, axis=1)
            there = pltpu.roll(here, V, 1)
            first, second = (here, there) if k % 2 == 0 else (there, here)
            for p in range(blocks // 2):
                row = jnp.where(low_row, first[2 * p : 2 * p + 1], second[2 * p + 1 : 2 * p + 2])
                none = row >= V
                base = jnp.where(low_row, slots[k * blocks + 2 * p] * V, slots[k * blocks + 2 * p + 1] * V)
                lanes = slice(p * 2 * V, (p + 1) * 2 * V)
                pair_rows[k, :, lanes] = jnp.where(none, -1, row + jnp.where(low_row, 0, V)).astype(F32)
                wide_rows[k, :, lanes] = jnp.where(none, -1, row + base).astype(F32)

    group_of = 9
    spot = iota((n, n), 0).astype(F32).astype(BF16)
    spot_pair = iota((2 * V, 2 * V), 0).astype(F32).astype(BF16)

    def hot(where, row):
        return jnp.where(where == row.astype(BF16), jnp.ones_like(where), jnp.zeros_like(where))

    def spread(w_ref, grad):
        for g in range(0, K, group_of):
            out = mxu(w_ref[g * C : (g + group_of) * C, :], grad).astype(BF16)
            back[g : g + group_of] = out.reshape(group_of, C, n)

    def scattered(lo):
        def some(g, total):
            for i in range(group_of):
                k = g * group_of + i
                total = total + mxu(back[k], hot(spot, wide_rows[k] - lo), ((1,), (1,)))
            return total

        return lax.fori_loop(0, K // group_of, some, jnp.zeros((C, n), F32))

    def spread_out(grad, side):
        def some(g, carry):
            for i in range(group_of):
                k = g * group_of + i
                out = mxu(grad, hot(spot, wide_rows[k] - side * n), ((1,), (1,)))
                spreads[k, :, side * n : (side + 1) * n] = out.astype(BF16)
            return carry

        lax.fori_loop(0, K // group_of, some, 0)

    def gathered_back(side):
        return mxu(w2p[:, 0 : K * C], spreads[0:K, :, side * n : (side + 1) * n].reshape(K * C, n))

    def pair_weights():
        for k in range(0, K_EVEN, 2):
            first = w2_ref[k * C : (k + 1) * C, :]
            second = w2_ref[(k + 1) * C : (k + 2) * C, :] if k + 1 < K else jnp.zeros_like(first)
            w2p[:, k * C : (k + 2) * C] = jnp.concatenate([first, second], axis=1)

    def weight_parts_wide(which, table):
        for g in range(0, K_EVEN, 4):
            out = mxu(table, spreads[g : g + 4].reshape(4 * C, 2 * n), ((1,), (1,))).astype(BF16)
            for j in range(2):
                rows = out[:, j * 2 * C : (j + 1) * 2 * C].reshape(C // TILE, TILE, 2 * C)
                first = (g // 2 + j) * (C // TILE)
                parts[which, first // pad, first % pad : first % pad + C // TILE] = rows

    low16 = iota((C, 2 * V), 1).astype(F32).astype(BF16) < V
    low32 = iota((C, 2 * V), 1) < V

    def fill(table, value, first):
        value = value.astype(F32)
        turned = pltpu.roll(value, V, 1)
        table[first] = jnp.where(low32, value, turned).astype(BF16)
        table[first + 1] = jnp.where(low32, turned, value).astype(BF16)

    def fill_own(table, value):
        for p in range(blocks // 2):
            fill(table, value[:, p * 2 * V : (p + 1) * 2 * V], 2 * p)

    def fill_halo(table, ref):
        for i in range(2):
            fill(table, ref[i], blocks + 2 * i)

    def pick(table, picked):
        def one(g, carry):
            for i in range(group_of):
                k = g * group_of + i
                for p in range(blocks // 2):
                    lanes = slice(p * 2 * V, (p + 1) * 2 * V)
                    both = jnp.where(
                        low16, table[slots[k * blocks + 2 * p]], table[slots[k * blocks + 2 * p + 1]]
                    )
                    picked[k, :, lanes] = mxu(both, hot(spot_pair, pair_rows[k, :, lanes])).astype(BF16)
            return carry

        lax.fori_loop(0, K // group_of, one, 0)

    def convolved(wt, picked):
        return mxu(wt[...], picked[...].reshape(K * C, n))

    def weight_parts(which, picked, grad):
        zero = jnp.zeros((C, n), BF16)
        pair = jnp.concatenate(
            [jnp.concatenate([grad, zero], axis=1), jnp.concatenate([zero, grad], axis=1)], axis=0
        )
        for g in range(0, K, group_of):
            both = jnp.concatenate(
                [picked[g : g + group_of, 0 : C // 2, :], picked[g : g + group_of, C // 2 : C, :]], axis=2
            ).reshape(group_of * C // 2, 2 * n)
            out = mxu(both, pair, ((1,), (1,))).astype(BF16)
            tiles = group_of * C // 2 // TILE
            out = out.reshape(tiles, TILE, 2 * C)
            first = g * C // 2 // TILE
            cut = min(max(pad - first, 0), tiles)
            if cut > 0:
                parts[which, 0, first : first + cut] = out[:cut]
            if cut < tiles:
                parts[which, 1, first + cut - pad : first + tiles - pad] = out[cut:]

    class Batch:
        def __init__(self, copies, send, recv, sent, landed):
            for copy in copies:
                copy.start()
            self.all = remote(sent, landed, send, recv, twin)

        def wait_recv(self):
            self.all.wait_recv()

        def wait_send(self):
            self.all.wait_send()

    def to_neighbours(slot, low, high, into):
        send, recv = halo_send.at[slot], halo_recv.at[slot]
        copies = [remote(low, into.at[1], send, recv, before), remote(high, into.at[0], send, recv, after)]
        return [Batch(copies, send, recv, into, into)]

    def arrive(copies):
        for copy in copies:
            copy.wait_recv()

    offsets = [
        (dx, dy, dz) for dx in range(n_x) for dy in range(n_y) for dz in range(ZPAR) if (dx, dy, dz) != (0, 0, 0)
    ]
    offsets.sort(key=lambda o: -(min(o[0], n_x - o[0]) + min(o[1], n_y - o[1]) + o[2]))

    def member(x, y, z):
        return (z * n_y + y) * n_x + x

    me = member(x, y, z_par)

    def to_twin(stage, which, src, dst):
        copy = remote(src, dst, pair_send.at[stage, which], pair_recv.at[stage, which], twin)
        copy.start()
        return [copy]

    def to_members(stage, which, src_of, dst, all_of):
        send, recv = group_send.at[stage, which], group_recv.at[stage, which]
        copies = []
        for dx, dy, dz in offsets:
            xx, yy, zz = (x + dx) % n_x, (y + dy) % n_y, (z_par + dz) % ZPAR
            target = (((z // ZPAR) * ZPAR + zz) * n_y + yy, xx * CORES + core)
            copies.append(remote(src_of(member(xx, yy, zz)), dst, send, recv, target))
        return [Batch(copies, send, recv, all_of, all_of)]

    def to_depths(which, src, dst):
        send, recv = deep_send.at[which], deep_recv.at[which]
        copies = []
        for j in [j for i in range(deep // 2, 0, -1) for j in sorted({i, deep - i})]:
            copies.append(remote(src, dst, send, recv, at(dz=j * ZPAR)))
        every = got3.at[which, 0 : deep - 1]
        return [Batch(copies, send, recv, every, every)]

    spreads[K:] = jnp.zeros((K_EVEN - K, C, 2 * n), BF16)
    used = K * C // 2 // TILE - pad
    parts[0, 1, used:] = jnp.zeros((pad - used, TILE, 2 * C), BF16)
    for which in range(2):
        mid[which, pad:] = jnp.zeros((mid.shape[1] - pad, TILE, 2 * C), BF16)
    loads["x"].wait()
    feat = to_channels(x_ref)
    feat_ref[...] = feat
    pl.semaphore_wait(barrier, len(near))
    feat_copies = to_neighbours(0, feat_ref.at[:, 0:half], feat_ref.at[:, half:n], halo_in)
    relay_signal(0)
    sent = list(feat_copies)

    loads["vox"].wait()
    loads["src"].wait()
    make_rows()
    loads["ct"].wait()
    cot = to_channels(ct_ref)
    spread_out(cot, 1)
    loads["w2"].wait()
    pair_weights()
    rim = gathered_back(1).astype(BF16)
    for i in range(2):
        rim_out[0, i] = rim[:, i * half : (i + 1) * half]
    rim_copies = to_neighbours(1, rim_out.at[0, 0], rim_out.at[0, 1], rim_in.at[0])
    sent += rim_copies
    relay_wait(0)
    relay_signal(1)
    loads["w1"].wait()
    w1t[...] = w1_ref[...].T
    fill_own(table1, feat)

    arrive(feat_copies)
    fill_halo(table1, halo_in)
    pick(table1, picked1)
    pre = convolved(w1t, picked1)
    sig = 1.0 / (1.0 + jnp.exp(-pre))
    hid = (pre * sig).astype(BF16)
    hidden[...] = hid
    hid_copies = to_neighbours(2, hidden.at[:, 0:half], hidden.at[:, half:n], halo_mid)
    sent += hid_copies
    relay_wait(1)
    relay_signal(2)

    spread_out(cot, 0)
    grad_hidden = gathered_back(0)
    arrive(rim_copies)
    rims = jnp.concatenate([rim_in[0, 0], rim_in[0, 1]], axis=1).astype(F32)
    grad_pre = ((grad_hidden + rims) * (sig * (1.0 + pre * (1.0 - sig)))).astype(BF16)
    weight_parts(0, picked1, grad_pre)

    def mine_of(which):
        return sums.at[which, core, pl.ds(me * per, per)]

    def reduce_pair(which):
        return to_twin(0, which, parts.at[which, 1 - core], got1.at[which])

    def scatter_reduce(which, copies):
        arrive(copies)
        mid[which, 0:pad] = (parts[which, core].astype(F32) + got1[which].astype(F32)).astype(BF16)
        got2[which, me] = mid[which, pl.ds(me * per, per)]
        every = got2.at[which, 0 : len(offsets)]
        return to_members(
            0, which, lambda other: mid.at[which, pl.ds(other * per, per)], got2.at[which, me], every
        )

    def added(ref, which, count):
        totals = [ref[which, i].astype(F32) for i in range(count)]
        while len(totals) > 1:
            totals = [a + b for a, b in zip(totals[::2], totals[1::2])]
        return totals[0].astype(BF16)

    def reduce_deep(which, copies):
        arrive(copies)
        got3[which, depth] = added(got2, which, len(offsets) + 1)
        mine = got3.at[which, depth]
        return to_depths(which, mine, mine)

    def gather_members(which, copies):
        arrive(copies)
        sums[which, core, pl.ds(me * per, per)] = added(got3, which, deep)
        mine = mine_of(which)
        every = sums.at[which, core, 0 : len(offsets) * per]
        return to_members(1, which, lambda other: mine, mine, every)

    def gather_pair(which, copies):
        arrive(copies)
        mine = sums.at[which, core, 0:pad]
        return to_twin(1, which, mine, mine)

    factor = float(n_x * CORES * space * n) ** (-0.5)

    def lay_out(which, side, out):
        for i in range(pad):
            tile = side * pad + i
            value = sums[which, side, i].astype(F32) * factor
            if which == 0:
                k, top = tile // 2, pl.multiple_of(tile % 2 * TILE, TILE)
                out[k, pl.ds(top, TILE), :] = value[:, :C]
                out[k, pl.ds(top + C // 2, TILE), :] = value[:, C:]
            else:
                k, top = tile // 4 * 2, pl.multiple_of(tile % 4 * TILE, TILE)
                out[k, pl.ds(top, TILE), :] = value[:, :C]
                out[k + 1, pl.ds(top, TILE), :] = value[:, C:]

    def drain(copies):
        for copy in copies:
            copy.wait_send()

    one = reduce_pair(0)
    sent += one
    relay_wait(2)
    relay_signal(3)
    w2t[...] = w2_ref[...].T
    relay_wait(3)
    one = scatter_reduce(0, one)
    sent += one
    arrive(hid_copies)
    weight_parts_wide(1, jnp.concatenate([hid, halo_mid[0], halo_mid[1]], axis=1))
    two = reduce_pair(1)
    sent += two

    spread(w1_ref, grad_pre)
    rim = scattered(n).astype(BF16)
    for i in range(2):
        rim_out[1, i] = rim[:, i * half : (i + 1) * half]
    last_copies = to_neighbours(3, rim_out.at[1, 0], rim_out.at[1, 1], rim_in.at[1])
    sent += last_copies
    two = scatter_reduce(1, two)
    sent += two
    fill_own(table2, hid)
    fill_halo(table2, halo_mid)
    pick(table2, picked2)
    from_channels(convolved(w2t, picked2).astype(BF16), conv_ref)
    grad_in = scattered(0)

    relay_end()
    one = reduce_deep(0, one)
    sent += one
    two = reduce_deep(1, two)
    sent += two
    one = gather_members(0, one)
    sent += one
    arrive(last_copies)
    rims = jnp.concatenate([rim_in[1, 0], rim_in[1, 1]], axis=1).astype(F32)
    grad_input = (grad_in + rims).astype(BF16)
    two = gather_members(1, two)
    sent += two
    from_channels(grad_input, gin_ref)
    one = gather_pair(0, one)
    sent += one
    lay_out(0, core, grad1_ref)
    arrive(one)
    lay_out(0, 1 - core, grad1_ref)
    two = gather_pair(1, two)
    drain(sent)
    lay_out(1, core, grad2_ref)
    arrive(two)
    lay_out(1, 1 - core, grad2_ref)
    drain(two)


def put_kernel(*refs):
    count = len(refs) // 2
    sem = refs[-1]
    copies = []
    for i, (src, dst) in enumerate(zip(refs[:count], refs[count:-1])):
        size = dst.shape[0]
        cuts = 3 if size == K else 1
        for c in range(cuts):
            part = pl.ds(c * size // cuts, size // cuts)
            copies.append(pltpu.make_async_copy(src.at[part], dst.at[part], sem.at[i, c]))
    for copy in copies:
        copy.start()
    for copy in copies:
        copy.wait()


def per_device(sizes, features, sources, voxels, cotangent, weight_one, weight_two):
    n_x, n_y, n_z = sizes
    members = n_x * n_y * ZPAR
    deep = n_z // ZPAR
    blocks = features.shape[1]
    n = blocks * V
    half = n // 2
    pad = TILES // CORES
    per = -(-pad // members)
    slots = blocks + 2 * HALO
    scratch = [
        pltpu.VMEM((blocks, V * C), BF16),
        pltpu.VMEM((blocks, V * C), BF16),
        pltpu.SMEM((blocks, K), jnp.int32),
        pltpu.VMEM((blocks, K * V), jnp.int32),
        pltpu.VMEM((K * C, C), BF16),
        pltpu.VMEM((K * C, C), BF16),
        pltpu.SMEM((K * blocks,), jnp.int32),
        pltpu.VMEM((K, 1, n), F32),
        pltpu.VMEM((K, 1, n), F32),
        pltpu.VMEM((n // 2, 2 * C), F32),
        pltpu.VMEM((blocks, V * C), F32),
        pltpu.VMEM((slots, C, 2 * V), BF16),
        pltpu.VMEM((slots, C, 2 * V), BF16),
        pltpu.VMEM((C, n), BF16),
        pltpu.VMEM((K, C, n), BF16),
        pltpu.VMEM((K, C, n), BF16),
        pltpu.VMEM((K, C, n), BF16),
        pltpu.VMEM((K_EVEN, C, 2 * n), BF16),
        pltpu.VMEM((C, K_EVEN * C), BF16),
        pltpu.VMEM((C, K * C), BF16),
        pltpu.VMEM((C, K * C), BF16),
        pltpu.VMEM((2, C, half), BF16),
        pltpu.VMEM((2, C, half), BF16),
        pltpu.VMEM((2, 2, C, half), BF16),
        pltpu.VMEM((2, 2, C, half), BF16),
        pltpu.VMEM((C, n), BF16),
        pltpu.VMEM((2, CORES, pad, TILE, 2 * C), BF16),
        pltpu.VMEM((2, pad, TILE, 2 * C), BF16),
        pltpu.VMEM((2, members * per, TILE, 2 * C), BF16),
        pltpu.VMEM((2, members, per, TILE, 2 * C), BF16),
        pltpu.VMEM((2, deep, per, TILE, 2 * C), BF16),
        pltpu.VMEM((2, CORES, members * per, TILE, 2 * C), BF16),
        pltpu.SemaphoreType.DMA((6,)),
        pltpu.SemaphoreType.DMA((4,)),
        pltpu.SemaphoreType.DMA((4,)),
        pltpu.SemaphoreType.DMA((2, 2)),
        pltpu.SemaphoreType.DMA((2, 2)),
        pltpu.SemaphoreType.DMA((2, 2)),
        pltpu.SemaphoreType.DMA((2, 2)),
        pltpu.SemaphoreType.DMA((2,)),
        pltpu.SemaphoreType.DMA((2,)),
        pltpu.SemaphoreType.REGULAR((7,)),
    ]
    outs = (
        jax.ShapeDtypeStruct((blocks, V * C), BF16),
        jax.ShapeDtypeStruct((blocks, V * C), BF16),
        jax.ShapeDtypeStruct((K, C, C), F32),
        jax.ShapeDtypeStruct((K, C, C), F32),
    )
    vmem = pl.BlockSpec(memory_space=pltpu.VMEM)
    anywhere = pl.BlockSpec(memory_space=pl.ANY)
    hbm = pl.BlockSpec(memory_space=pltpu.HBM)
    even = jax.ShapeDtypeStruct((K_EVEN, C, C), F32)
    results = pl.pallas_call(
        functools.partial(step_kernel, sizes),
        out_shape=(*outs[:2], even, even),
        in_specs=[hbm] * 6,
        out_specs=(vmem,) * 4,
        scratch_shapes=scratch,
        compiler_params=pltpu.CompilerParams(
            collective_id=0, has_side_effects=True, vmem_limit_bytes=32 * 1024 * 1024
        ),
        name="step",
    )(
        *[
            pltpu.with_memory_space_constraint(a, pltpu.HBM)
            for a in (
                features[0],
                cotangent[0],
                sources[0],
                voxels[0],
                weight_one.reshape(K * C, C),
                weight_two.reshape(K * C, C),
            )
        ]
    )
    conv, gin, grad_one, grad_two = pl.pallas_call(
        put_kernel,
        out_shape=outs,
        in_specs=[anywhere] * 4,
        out_specs=(hbm,) * 4,
        scratch_shapes=[pltpu.SemaphoreType.DMA((4, 3))],
        compiler_params=pltpu.CompilerParams(vmem_limit_bytes=1024 * 1024),
        name="put",
    )(*results)
    return conv[None], gin[None], grad_one, grad_two


def solution(mesh):
    space, dp = mesh.shape["space"], mesh.shape["dp"]
    sizes = (dp // CORES, Y, space // Y)
    wide = P("dp", "space", None)
    return jax.shard_map(
        functools.partial(per_device, sizes),
        mesh=mesh,
        in_specs=(wide, wide, wide, wide, P(), P()),
        out_specs=(wide, wide, P(), P()),
        check_vma=False,
    )
```

```python
import functools

import jax
import jax.numpy as jnp
from jax import lax
from jax.experimental import pallas as pl
from jax.experimental.pallas import tpu as pltpu
from jax.sharding import PartitionSpec as P

C = 64
V = 64
K = 27
HALO = 2
Y = 4
ZPAR = 2
CORES = 2
TILE = 16
K_EVEN = K + K % 2
TILES = K_EVEN * C * C // (TILE * 2 * C)
MESH = pl.DeviceIdType.MESH
BF16 = jnp.bfloat16
F32 = jnp.float32


def mxu(a, b, dims=((1,), (0,))):
    return lax.dot_general(a, b, (dims, ((), ())), preferred_element_type=F32)


def step_kernel(
    sizes,
    x_hbm,
    ct_hbm,
    src_hbm,
    vox_hbm,
    w1_hbm,
    w2_hbm,
    conv_ref,
    gin_ref,
    grad1_ref,
    grad2_ref,
    x_ref,
    ct_ref,
    src_ref,
    vox_ref,
    w1_ref,
    w2_ref,
    slots,
    pair_rows,
    wide_rows,
    turn,
    flat,
    table1,
    table2,
    feat_ref,
    picked1,
    picked2,
    back,
    spreads,
    w2p,
    w1t,
    w2t,
    halo_in,
    halo_mid,
    rim_out,
    rim_in,
    hidden,
    parts,
    got1,
    mid,
    got2,
    got3,
    sums,
    load_sem,
    halo_send,
    halo_recv,
    pair_send,
    pair_recv,
    group_send,
    group_recv,
    deep_send,
    deep_recv,
    relay,
):
    n_x, n_y, n_z = sizes
    deep = n_z // ZPAR
    space = n_y * n_z
    blocks = x_ref.shape[0]
    n = feat_ref.shape[1]
    half = n // 2
    s = lax.axis_index("space")
    d = lax.axis_index("dp")
    x, core = d // CORES, d % CORES
    z, y = s // n_y, s % n_y
    z_par, depth = z % ZPAR, z // ZPAR
    pad = TILES // CORES
    per = sums.shape[2] // (n_x * n_y * ZPAR)

    def at(dx=0, dy=0, dz=0, core=core):
        return (((z + dz) % n_z) * n_y + (y + dy) % n_y, ((x + dx) % n_x) * CORES + core)

    before = ((s + space - 1) % space, d)
    after = ((s + 1) % space, d)
    twin = at(core=1 - core)
    x_pair = [at(dx=1), at(dx=n_x - 1)]
    y_pair = [at(dy=1), at(dy=n_y - 1)]

    def z_pair(step):
        return [at(dz=step), at(dz=n_z - step)]

    other_z = (((z // ZPAR) * ZPAR + 1 - z_par) * n_y + y, d)

    def signal(sem, devices):
        for device in devices:
            pl.semaphore_signal(sem, inc=1, device_id=device, device_id_type=MESH)

    barrier = pltpu.get_barrier_semaphore()
    near = [before, after, twin] + x_pair + y_pair + z_pair(1)
    signal(barrier, near)

    z_steps = []
    while 2 ** len(z_steps) < n_z // 2:
        z_steps.append(2 ** len(z_steps))

    def relay_signal(i):
        if i == 0:
            signal(relay.at[0], x_pair)
        elif i <= 2:
            signal(relay.at[i], y_pair)
        else:
            signal(relay.at[i], [other_z])
        if i < len(z_steps):
            signal(relay.at[4 + i], z_pair(z_steps[i]))

    def relay_wait(i):
        pl.semaphore_wait(relay.at[i], 2 if i <= 2 else 1)
        if i < len(z_steps) - 1:
            pl.semaphore_wait(relay.at[4 + i], 2)

    def relay_end():
        pl.semaphore_wait(relay.at[4 + len(z_steps) - 1], 2)

    def remote(src, dst, send, recv, target):
        return pltpu.make_async_remote_copy(
            src_ref=src, dst_ref=dst, send_sem=send, recv_sem=recv, device_id=target, device_id_type=MESH
        )

    loads = {}
    for i, (name, src, dst) in enumerate(
        (
            ("vox", vox_hbm, vox_ref),
            ("src", src_hbm, src_ref),
            ("x", x_hbm, x_ref),
            ("ct", ct_hbm, ct_ref),
            ("w2", w2_hbm, w2_ref),
            ("w1", w1_hbm, w1_ref),
        )
    ):
        loads[name] = pltpu.make_async_copy(src, dst, load_sem.at[i])
        loads[name].start()

    def iota(shape, dim):
        return lax.broadcasted_iota(jnp.int32, shape, dim)

    pairs = V // 2
    old = iota((n, n), 0)
    parity, rest = old // (n // 2), old % (n // 2)
    order = jnp.where(rest // pairs * V + rest % pairs * 2 + parity == iota((n, n), 1), 1.0, 0.0).astype(BF16)

    def to_channels(ref):
        wide = ref[...].astype(F32)
        for j in range(pairs):
            turn[j * blocks : (j + 1) * blocks, :] = wide[:, j * 2 * C : (j + 1) * 2 * C]
        rows = jnp.concatenate([turn[pl.ds(b, pairs, stride=blocks), :] for b in range(blocks)], axis=0)
        lanes = rows.T
        both = jnp.concatenate([lanes[:C], lanes[C:]], axis=1).astype(BF16)
        return mxu(both, order).astype(BF16)

    def from_channels(value, out_ref):
        both = mxu(value, order, ((1,), (1,)))
        rows = jnp.concatenate([both[:, : n // 2], both[:, n // 2 :]], axis=0).T
        turn[...] = rows
        for j in range(pairs):
            flat[:, j * 2 * C : (j + 1) * 2 * C] = turn[pl.ds(j, blocks, stride=pairs), :]
        out_ref[...] = flat[...].astype(BF16)

    low_row = iota((1, 2 * V), 1) < V
    shift = blocks.bit_length() - 1

    def make_rows():
        for k in range(K):
            for b in range(blocks):
                source = src_ref[b, k]
                owner, place = source >> shift, source & (blocks - 1)
                slots[k * blocks + b] = jnp.where(
                    owner == s, place, jnp.where(owner < s, place + HALO, blocks + HALO + place)
                )
            start = k // 2 * 2 * V
            if start + 2 * V <= K * V:
                here = vox_ref[:, start : start + 2 * V]
            else:
                here = jnp.concatenate([vox_ref[:, start : start + V]] * 2, axis=1)
            there = pltpu.roll(here, V, 1)
            first, second = (here, there) if k % 2 == 0 else (there, here)
            for p in range(blocks // 2):
                row = jnp.where(low_row, first[2 * p : 2 * p + 1], second[2 * p + 1 : 2 * p + 2])
                none = row >= V
                base = jnp.where(low_row, slots[k * blocks + 2 * p] * V, slots[k * blocks + 2 * p + 1] * V)
                lanes = slice(p * 2 * V, (p + 1) * 2 * V)
                pair_rows[k, :, lanes] = jnp.where(none, -1, row + jnp.where(low_row, 0, V)).astype(F32)
                wide_rows[k, :, lanes] = jnp.where(none, -1, row + base).astype(F32)

    group_of = 9
    spot = iota((n, n), 0).astype(F32).astype(BF16)
    spot_pair = iota((2 * V, 2 * V), 0).astype(F32).astype(BF16)

    def hot(where, row):
        return jnp.where(where == row.astype(BF16), jnp.ones_like(where), jnp.zeros_like(where))

    def spread(w_ref, grad):
        for g in range(0, K, group_of):
            out = mxu(w_ref[g * C : (g + group_of) * C, :], grad).astype(BF16)
            back[g : g + group_of] = out.reshape(group_of, C, n)

    def scattered(lo):
        def some(g, total):
            for i in range(group_of):
                k = g * group_of + i
                total = total + mxu(back[k], hot(spot, wide_rows[k] - lo), ((1,), (1,)))
            return total

        return lax.fori_loop(0, K // group_of, some, jnp.zeros((C, n), F32))

    def spread_out(grad, side):
        def some(g, carry):
            for i in range(group_of):
                k = g * group_of + i
                out = mxu(grad, hot(spot, wide_rows[k] - side * n), ((1,), (1,)))
                spreads[k, :, side * n : (side + 1) * n] = out.astype(BF16)
            return carry

        lax.fori_loop(0, K // group_of, some, 0)

    def gathered_back(side):
        return mxu(w2p[:, 0 : K * C], spreads[0:K, :, side * n : (side + 1) * n].reshape(K * C, n))

    def pair_weights():
        for k in range(0, K_EVEN, 2):
            first = w2_ref[k * C : (k + 1) * C, :]
            second = w2_ref[(k + 1) * C : (k + 2) * C, :] if k + 1 < K else jnp.zeros_like(first)
            w2p[:, k * C : (k + 2) * C] = jnp.concatenate([first, second], axis=1)

    def weight_parts_wide(which, table):
        for g in range(0, K_EVEN, 4):
            out = mxu(table, spreads[g : g + 4].reshape(4 * C, 2 * n), ((1,), (1,))).astype(BF16)
            for j in range(2):
                rows = out[:, j * 2 * C : (j + 1) * 2 * C].reshape(C // TILE, TILE, 2 * C)
                first = (g // 2 + j) * (C // TILE)
                parts[which, first // pad, first % pad : first % pad + C // TILE] = rows

    low16 = iota((C, 2 * V), 1).astype(F32).astype(BF16) < V
    low32 = iota((C, 2 * V), 1) < V

    def fill(table, value, first):
        value = value.astype(F32)
        turned = pltpu.roll(value, V, 1)
        table[first] = jnp.where(low32, value, turned).astype(BF16)
        table[first + 1] = jnp.where(low32, turned, value).astype(BF16)

    def fill_own(table, value):
        for p in range(blocks // 2):
            fill(table, value[:, p * 2 * V : (p + 1) * 2 * V], 2 * p)

    def fill_halo(table, ref):
        for i in range(2):
            fill(table, ref[i], blocks + 2 * i)

    def pick(table, picked):
        def one(g, carry):
            for i in range(group_of):
                k = g * group_of + i
                for p in range(blocks // 2):
                    lanes = slice(p * 2 * V, (p + 1) * 2 * V)
                    both = jnp.where(
                        low16, table[slots[k * blocks + 2 * p]], table[slots[k * blocks + 2 * p + 1]]
                    )
                    picked[k, :, lanes] = mxu(both, hot(spot_pair, pair_rows[k, :, lanes])).astype(BF16)
            return carry

        lax.fori_loop(0, K // group_of, one, 0)

    def convolved(wt, picked):
        return mxu(wt[...], picked[...].reshape(K * C, n))

    def weight_parts(which, picked, grad):
        zero = jnp.zeros((C, n), BF16)
        pair = jnp.concatenate(
            [jnp.concatenate([grad, zero], axis=1), jnp.concatenate([zero, grad], axis=1)], axis=0
        )
        for g in range(0, K, group_of):
            both = jnp.concatenate(
                [picked[g : g + group_of, 0 : C // 2, :], picked[g : g + group_of, C // 2 : C, :]], axis=2
            ).reshape(group_of * C // 2, 2 * n)
            out = mxu(both, pair, ((1,), (1,))).astype(BF16)
            tiles = group_of * C // 2 // TILE
            out = out.reshape(tiles, TILE, 2 * C)
            first = g * C // 2 // TILE
            cut = min(max(pad - first, 0), tiles)
            if cut > 0:
                parts[which, 0, first : first + cut] = out[:cut]
            if cut < tiles:
                parts[which, 1, first + cut - pad : first + tiles - pad] = out[cut:]

    class Batch:
        def __init__(self, copies, send, recv, sent, landed):
            for copy in copies:
                copy.start()
            self.all = remote(sent, landed, send, recv, twin)

        def wait_recv(self):
            self.all.wait_recv()

        def wait_send(self):
            self.all.wait_send()

    def to_neighbours(slot, low, high, into):
        send, recv = halo_send.at[slot], halo_recv.at[slot]
        copies = [remote(low, into.at[1], send, recv, before), remote(high, into.at[0], send, recv, after)]
        return [Batch(copies, send, recv, into, into)]

    def arrive(copies):
        for copy in copies:
            copy.wait_recv()

    offsets = [
        (dx, dy, dz) for dx in range(n_x) for dy in range(n_y) for dz in range(ZPAR) if (dx, dy, dz) != (0, 0, 0)
    ]
    offsets.sort(key=lambda o: -(min(o[0], n_x - o[0]) + min(o[1], n_y - o[1]) + o[2]))

    def member(x, y, z):
        return (z * n_y + y) * n_x + x

    me = member(x, y, z_par)

    def to_twin(stage, which, src, dst):
        copy = remote(src, dst, pair_send.at[stage, which], pair_recv.at[stage, which], twin)
        copy.start()
        return [copy]

    def to_members(stage, which, src_of, dst, all_of):
        send, recv = group_send.at[stage, which], group_recv.at[stage, which]
        copies = []
        for dx, dy, dz in offsets:
            xx, yy, zz = (x + dx) % n_x, (y + dy) % n_y, (z_par + dz) % ZPAR
            target = (((z // ZPAR) * ZPAR + zz) * n_y + yy, xx * CORES + core)
            copies.append(remote(src_of(member(xx, yy, zz)), dst, send, recv, target))
        return [Batch(copies, send, recv, all_of, all_of)]

    def to_depths(which, src, dst):
        send, recv = deep_send.at[which], deep_recv.at[which]
        copies = []
        for j in [j for i in range(deep // 2, 0, -1) for j in sorted({i, deep - i})]:
            copies.append(remote(src, dst, send, recv, at(dz=j * ZPAR)))
        every = got3.at[which, 0 : deep - 1]
        return [Batch(copies, send, recv, every, every)]

    spreads[K:] = jnp.zeros((K_EVEN - K, C, 2 * n), BF16)
    used = K * C // 2 // TILE - pad
    parts[0, 1, used:] = jnp.zeros((pad - used, TILE, 2 * C), BF16)
    for which in range(2):
        mid[which, pad:] = jnp.zeros((mid.shape[1] - pad, TILE, 2 * C), BF16)
    loads["x"].wait()
    feat = to_channels(x_ref)
    feat_ref[...] = feat
    pl.semaphore_wait(barrier, len(near))
    feat_copies = to_neighbours(0, feat_ref.at[:, 0:half], feat_ref.at[:, half:n], halo_in)
    relay_signal(0)
    sent = list(feat_copies)

    loads["vox"].wait()
    loads["src"].wait()
    make_rows()
    loads["ct"].wait()
    cot = to_channels(ct_ref)
    spread_out(cot, 1)
    loads["w2"].wait()
    pair_weights()
    rim = gathered_back(1).astype(BF16)
    for i in range(2):
        rim_out[0, i] = rim[:, i * half : (i + 1) * half]
    rim_copies = to_neighbours(1, rim_out.at[0, 0], rim_out.at[0, 1], rim_in.at[0])
    sent += rim_copies
    relay_wait(0)
    relay_signal(1)
    loads["w1"].wait()
    w1t[...] = w1_ref[...].T
    fill_own(table1, feat)

    arrive(feat_copies)
    fill_halo(table1, halo_in)
    pick(table1, picked1)
    pre = convolved(w1t, picked1)
    sig = 1.0 / (1.0 + jnp.exp(-pre))
    hid = (pre * sig).astype(BF16)
    hidden[...] = hid
    hid_copies = to_neighbours(2, hidden.at[:, 0:half], hidden.at[:, half:n], halo_mid)
    sent += hid_copies
    relay_wait(1)
    relay_signal(2)

    spread_out(cot, 0)
    grad_hidden = gathered_back(0)
    arrive(rim_copies)
    rims = jnp.concatenate([rim_in[0, 0], rim_in[0, 1]], axis=1).astype(F32)
    grad_pre = ((grad_hidden + rims) * (sig * (1.0 + pre * (1.0 - sig)))).astype(BF16)
    weight_parts(0, picked1, grad_pre)

    def mine_of(which):
        return sums.at[which, core, pl.ds(me * per, per)]

    def reduce_pair(which):
        return to_twin(0, which, parts.at[which, 1 - core], got1.at[which])

    def scatter_reduce(which, copies):
        arrive(copies)
        mid[which, 0:pad] = (parts[which, core].astype(F32) + got1[which].astype(F32)).astype(BF16)
        got2[which, me] = mid[which, pl.ds(me * per, per)]
        every = got2.at[which, 0 : len(offsets)]
        return to_members(
            0, which, lambda other: mid.at[which, pl.ds(other * per, per)], got2.at[which, me], every
        )

    def added(ref, which, count):
        totals = [ref[which, i].astype(F32) for i in range(count)]
        while len(totals) > 1:
            totals = [a + b for a, b in zip(totals[::2], totals[1::2])]
        return totals[0].astype(BF16)

    def reduce_deep(which, copies):
        arrive(copies)
        got3[which, depth] = added(got2, which, len(offsets) + 1)
        mine = got3.at[which, depth]
        return to_depths(which, mine, mine)

    def gather_members(which, copies):
        arrive(copies)
        sums[which, core, pl.ds(me * per, per)] = added(got3, which, deep)
        mine = mine_of(which)
        every = sums.at[which, core, 0 : len(offsets) * per]
        return to_members(1, which, lambda other: mine, mine, every)

    def gather_pair(which, copies):
        arrive(copies)
        mine = sums.at[which, core, 0:pad]
        return to_twin(1, which, mine, mine)

    factor = float(n_x * CORES * space * n) ** (-0.5)

    def lay_out(which, side, out):
        for i in range(pad):
            tile = side * pad + i
            value = sums[which, side, i].astype(F32) * factor
            if which == 0:
                k, top = tile // 2, pl.multiple_of(tile % 2 * TILE, TILE)
                out[k, pl.ds(top, TILE), :] = value[:, :C]
                out[k, pl.ds(top + C // 2, TILE), :] = value[:, C:]
            else:
                k, top = tile // 4 * 2, pl.multiple_of(tile % 4 * TILE, TILE)
                out[k, pl.ds(top, TILE), :] = value[:, :C]
                out[k + 1, pl.ds(top, TILE), :] = value[:, C:]

    def drain(copies):
        for copy in copies:
            copy.wait_send()

    one = reduce_pair(0)
    sent += one
    relay_wait(2)
    relay_signal(3)
    w2t[...] = w2_ref[...].T
    relay_wait(3)
    one = scatter_reduce(0, one)
    sent += one
    arrive(hid_copies)
    weight_parts_wide(1, jnp.concatenate([hid, halo_mid[0], halo_mid[1]], axis=1))
    two = reduce_pair(1)
    sent += two

    spread(w1_ref, grad_pre)
    two = scatter_reduce(1, two)
    sent += two
    rim = scattered(n).astype(BF16)
    for i in range(2):
        rim_out[1, i] = rim[:, i * half : (i + 1) * half]
    last_copies = to_neighbours(3, rim_out.at[1, 0], rim_out.at[1, 1], rim_in.at[1])
    sent += last_copies
    relay_end()
    one = reduce_deep(0, one)
    sent += one
    fill_own(table2, hid)
    fill_halo(table2, halo_mid)
    pick(table2, picked2)
    from_channels(convolved(w2t, picked2).astype(BF16), conv_ref)
    two = reduce_deep(1, two)
    sent += two
    grad_in = scattered(0)

    one = gather_members(0, one)
    sent += one
    arrive(last_copies)
    rims = jnp.concatenate([rim_in[1, 0], rim_in[1, 1]], axis=1).astype(F32)
    grad_input = (grad_in + rims).astype(BF16)
    two = gather_members(1, two)
    sent += two
    from_channels(grad_input, gin_ref)
    one = gather_pair(0, one)
    sent += one
    lay_out(0, core, grad1_ref)
    arrive(one)
    lay_out(0, 1 - core, grad1_ref)
    two = gather_pair(1, two)
    drain(sent)
    lay_out(1, core, grad2_ref)
    arrive(two)
    lay_out(1, 1 - core, grad2_ref)
    drain(two)


def put_kernel(*refs):
    count = len(refs) // 2
    sem = refs[-1]
    copies = []
    for i, (src, dst) in enumerate(zip(refs[:count], refs[count:-1])):
        size = dst.shape[0]
        cuts = 3 if size == K else 1
        for c in range(cuts):
            part = pl.ds(c * size // cuts, size // cuts)
            copies.append(pltpu.make_async_copy(src.at[part], dst.at[part], sem.at[i, c]))
    for copy in copies:
        copy.start()
    for copy in copies:
        copy.wait()


def per_device(sizes, features, sources, voxels, cotangent, weight_one, weight_two):
    n_x, n_y, n_z = sizes
    members = n_x * n_y * ZPAR
    deep = n_z // ZPAR
    blocks = features.shape[1]
    n = blocks * V
    half = n // 2
    pad = TILES // CORES
    per = -(-pad // members)
    slots = blocks + 2 * HALO
    scratch = [
        pltpu.VMEM((blocks, V * C), BF16),
        pltpu.VMEM((blocks, V * C), BF16),
        pltpu.SMEM((blocks, K), jnp.int32),
        pltpu.VMEM((blocks, K * V), jnp.int32),
        pltpu.VMEM((K * C, C), BF16),
        pltpu.VMEM((K * C, C), BF16),
        pltpu.SMEM((K * blocks,), jnp.int32),
        pltpu.VMEM((K, 1, n), F32),
        pltpu.VMEM((K, 1, n), F32),
        pltpu.VMEM((n // 2, 2 * C), F32),
        pltpu.VMEM((blocks, V * C), F32),
        pltpu.VMEM((slots, C, 2 * V), BF16),
        pltpu.VMEM((slots, C, 2 * V), BF16),
        pltpu.VMEM((C, n), BF16),
        pltpu.VMEM((K, C, n), BF16),
        pltpu.VMEM((K, C, n), BF16),
        pltpu.VMEM((K, C, n), BF16),
        pltpu.VMEM((K_EVEN, C, 2 * n), BF16),
        pltpu.VMEM((C, K_EVEN * C), BF16),
        pltpu.VMEM((C, K * C), BF16),
        pltpu.VMEM((C, K * C), BF16),
        pltpu.VMEM((2, C, half), BF16),
        pltpu.VMEM((2, C, half), BF16),
        pltpu.VMEM((2, 2, C, half), BF16),
        pltpu.VMEM((2, 2, C, half), BF16),
        pltpu.VMEM((C, n), BF16),
        pltpu.VMEM((2, CORES, pad, TILE, 2 * C), BF16),
        pltpu.VMEM((2, pad, TILE, 2 * C), BF16),
        pltpu.VMEM((2, members * per, TILE, 2 * C), BF16),
        pltpu.VMEM((2, members, per, TILE, 2 * C), BF16),
        pltpu.VMEM((2, deep, per, TILE, 2 * C), BF16),
        pltpu.VMEM((2, CORES, members * per, TILE, 2 * C), BF16),
        pltpu.SemaphoreType.DMA((6,)),
        pltpu.SemaphoreType.DMA((4,)),
        pltpu.SemaphoreType.DMA((4,)),
        pltpu.SemaphoreType.DMA((2, 2)),
        pltpu.SemaphoreType.DMA((2, 2)),
        pltpu.SemaphoreType.DMA((2, 2)),
        pltpu.SemaphoreType.DMA((2, 2)),
        pltpu.SemaphoreType.DMA((2,)),
        pltpu.SemaphoreType.DMA((2,)),
        pltpu.SemaphoreType.REGULAR((7,)),
    ]
    outs = (
        jax.ShapeDtypeStruct((blocks, V * C), BF16),
        jax.ShapeDtypeStruct((blocks, V * C), BF16),
        jax.ShapeDtypeStruct((K, C, C), F32),
        jax.ShapeDtypeStruct((K, C, C), F32),
    )
    vmem = pl.BlockSpec(memory_space=pltpu.VMEM)
    anywhere = pl.BlockSpec(memory_space=pl.ANY)
    hbm = pl.BlockSpec(memory_space=pltpu.HBM)
    even = jax.ShapeDtypeStruct((K_EVEN, C, C), F32)
    results = pl.pallas_call(
        functools.partial(step_kernel, sizes),
        out_shape=(*outs[:2], even, even),
        in_specs=[hbm] * 6,
        out_specs=(vmem,) * 4,
        scratch_shapes=scratch,
        compiler_params=pltpu.CompilerParams(
            collective_id=0, has_side_effects=True, vmem_limit_bytes=32 * 1024 * 1024
        ),
        name="step",
    )(
        *[
            pltpu.with_memory_space_constraint(a, pltpu.HBM)
            for a in (
                features[0],
                cotangent[0],
                sources[0],
                voxels[0],
                weight_one.reshape(K * C, C),
                weight_two.reshape(K * C, C),
            )
        ]
    )
    conv, gin, grad_one, grad_two = pl.pallas_call(
        put_kernel,
        out_shape=outs,
        in_specs=[anywhere] * 4,
        out_specs=(hbm,) * 4,
        scratch_shapes=[pltpu.SemaphoreType.DMA((4, 3))],
        compiler_params=pltpu.CompilerParams(vmem_limit_bytes=1024 * 1024),
        name="put",
    )(*results)
    return conv[None], gin[None], grad_one, grad_two


def solution(mesh):
    space, dp = mesh.shape["space"], mesh.shape["dp"]
    sizes = (dp // CORES, Y, space // Y)
    wide = P("dp", "space", None)
    return jax.shard_map(
        functools.partial(per_device, sizes),
        mesh=mesh,
        in_specs=(wide, wide, wide, wide, P(), P()),
        out_specs=(wide, wide, P(), P()),
        check_vma=False,
    )
```

```python
import functools

import jax
import jax.numpy as jnp
from jax import lax
from jax.experimental import pallas as pl
from jax.experimental.pallas import tpu as pltpu
from jax.sharding import PartitionSpec as P

C = 64
V = 64
K = 27
HALO = 2
Y = 4
ZPAR = 2
CORES = 2
TILE = 16
K_EVEN = K + K % 2
TILES = K_EVEN * C * C // (TILE * 2 * C)
MESH = pl.DeviceIdType.MESH
BF16 = jnp.bfloat16
F32 = jnp.float32


def mxu(a, b, dims=((1,), (0,))):
    return lax.dot_general(a, b, (dims, ((), ())), preferred_element_type=F32)


def step_kernel(
    sizes,
    x_hbm,
    ct_hbm,
    src_hbm,
    vox_hbm,
    w1_hbm,
    w2_hbm,
    conv_ref,
    gin_ref,
    grad1_ref,
    grad2_ref,
    x_ref,
    ct_ref,
    src_ref,
    vox_ref,
    w1_ref,
    w2_ref,
    slots,
    pair_rows,
    wide_rows,
    turn,
    flat,
    table1,
    table2,
    feat_ref,
    picked1,
    picked2,
    back,
    spreads,
    w2p,
    w1t,
    w2t,
    halo_in,
    halo_mid,
    rim_out,
    rim_in,
    hidden,
    parts,
    got1,
    mid,
    got2,
    got3,
    sums,
    load_sem,
    halo_send,
    halo_recv,
    pair_send,
    pair_recv,
    group_send,
    group_recv,
    deep_send,
    deep_recv,
    relay,
):
    loads = {}

    def load(name, src, dst):
        loads[name] = pltpu.make_async_copy(src, dst, load_sem.at[len(loads)])
        loads[name].start()

    load("x", x_hbm, x_ref)
    load("ct", ct_hbm, ct_ref)
    n_x, n_y, n_z = sizes
    deep = n_z // ZPAR
    space = n_y * n_z
    blocks = x_ref.shape[0]
    n = feat_ref.shape[1]
    half = n // 2
    s = lax.axis_index("space")
    d = lax.axis_index("dp")
    x, core = d // CORES, d % CORES
    z, y = s // n_y, s % n_y
    z_par, depth = z % ZPAR, z // ZPAR
    pad = TILES // CORES
    per = sums.shape[2] // (n_x * n_y * ZPAR)

    def at(dx=0, dy=0, dz=0, core=core):
        return (((z + dz) % n_z) * n_y + (y + dy) % n_y, ((x + dx) % n_x) * CORES + core)

    before = ((s + space - 1) % space, d)
    after = ((s + 1) % space, d)
    twin = at(core=1 - core)
    x_pair = [at(dx=1), at(dx=n_x - 1)]
    y_pair = [at(dy=1), at(dy=n_y - 1)]

    def z_pair(step):
        return [at(dz=step), at(dz=n_z - step)]

    other_z = (((z // ZPAR) * ZPAR + 1 - z_par) * n_y + y, d)

    def signal(sem, devices):
        for device in devices:
            pl.semaphore_signal(sem, inc=1, device_id=device, device_id_type=MESH)

    barrier = pltpu.get_barrier_semaphore()
    near = [before, after, twin] + x_pair + y_pair + z_pair(1)
    signal(barrier, near)

    z_steps = []
    while 2 ** len(z_steps) < n_z // 2:
        z_steps.append(2 ** len(z_steps))

    def relay_signal(i):
        if i == 0:
            signal(relay.at[0], x_pair)
        elif i <= 2:
            signal(relay.at[i], y_pair)
        else:
            signal(relay.at[i], [other_z])
        if i < len(z_steps):
            signal(relay.at[4 + i], z_pair(z_steps[i]))

    def relay_wait(i):
        pl.semaphore_wait(relay.at[i], 2 if i <= 2 else 1)
        if i < len(z_steps) - 1:
            pl.semaphore_wait(relay.at[4 + i], 2)

    def relay_end():
        pl.semaphore_wait(relay.at[4 + len(z_steps) - 1], 2)

    def remote(src, dst, send, recv, target):
        return pltpu.make_async_remote_copy(
            src_ref=src, dst_ref=dst, send_sem=send, recv_sem=recv, device_id=target, device_id_type=MESH
        )

    load("vox", vox_hbm, vox_ref)
    load("src", src_hbm, src_ref)
    load("w2", w2_hbm, w2_ref)
    load("w1", w1_hbm, w1_ref)

    def iota(shape, dim):
        return lax.broadcasted_iota(jnp.int32, shape, dim)

    pairs = V // 2
    old = iota((n, n), 0)
    parity, rest = old // (n // 2), old % (n // 2)
    order = jnp.where(rest // pairs * V + rest % pairs * 2 + parity == iota((n, n), 1), 1.0, 0.0).astype(BF16)

    def to_channels(ref):
        wide = ref[...].astype(F32)
        for j in range(pairs):
            turn[j * blocks : (j + 1) * blocks, :] = wide[:, j * 2 * C : (j + 1) * 2 * C]
        rows = jnp.concatenate([turn[pl.ds(b, pairs, stride=blocks), :] for b in range(blocks)], axis=0)
        lanes = rows.T
        both = jnp.concatenate([lanes[:C], lanes[C:]], axis=1).astype(BF16)
        return mxu(both, order).astype(BF16)

    def from_channels(value, out_ref):
        both = mxu(value, order, ((1,), (1,)))
        rows = jnp.concatenate([both[:, : n // 2], both[:, n // 2 :]], axis=0).T
        turn[...] = rows
        for j in range(pairs):
            flat[:, j * 2 * C : (j + 1) * 2 * C] = turn[pl.ds(j, blocks, stride=pairs), :]
        out_ref[...] = flat[...].astype(BF16)

    low_row = iota((1, 2 * V), 1) < V
    shift = blocks.bit_length() - 1

    def make_rows():
        for k in range(K):
            for b in range(blocks):
                source = src_ref[b, k]
                owner, place = source >> shift, source & (blocks - 1)
                slots[k * blocks + b] = jnp.where(
                    owner == s, place, jnp.where(owner < s, place + HALO, blocks + HALO + place)
                )
            start = k // 2 * 2 * V
            if start + 2 * V <= K * V:
                here = vox_ref[:, start : start + 2 * V]
            else:
                here = jnp.concatenate([vox_ref[:, start : start + V]] * 2, axis=1)
            there = pltpu.roll(here, V, 1)
            first, second = (here, there) if k % 2 == 0 else (there, here)
            for p in range(blocks // 2):
                row = jnp.where(low_row, first[2 * p : 2 * p + 1], second[2 * p + 1 : 2 * p + 2])
                none = row >= V
                base = jnp.where(low_row, slots[k * blocks + 2 * p] * V, slots[k * blocks + 2 * p + 1] * V)
                lanes = slice(p * 2 * V, (p + 1) * 2 * V)
                pair_rows[k, :, lanes] = jnp.where(none, -1, row + jnp.where(low_row, 0, V)).astype(F32)
                wide_rows[k, :, lanes] = jnp.where(none, -1, row + base).astype(F32)

    group_of = 9
    spot = iota((n, n), 0).astype(F32).astype(BF16)
    spot_pair = iota((2 * V, 2 * V), 0).astype(F32).astype(BF16)

    def hot(where, row):
        return jnp.where(where == row.astype(BF16), jnp.ones_like(where), jnp.zeros_like(where))

    def spread(w_ref, grad):
        for g in range(0, K, group_of):
            out = mxu(w_ref[g * C : (g + group_of) * C, :], grad).astype(BF16)
            back[g : g + group_of] = out.reshape(group_of, C, n)

    def scattered(lo):
        def some(g, total):
            for i in range(group_of):
                k = g * group_of + i
                total = total + mxu(back[k], hot(spot, wide_rows[k] - lo), ((1,), (1,)))
            return total

        return lax.fori_loop(0, K // group_of, some, jnp.zeros((C, n), F32))

    def spread_out(grad, side):
        def some(g, carry):
            for i in range(group_of):
                k = g * group_of + i
                out = mxu(grad, hot(spot, wide_rows[k] - side * n), ((1,), (1,)))
                spreads[k, :, side * n : (side + 1) * n] = out.astype(BF16)
            return carry

        lax.fori_loop(0, K // group_of, some, 0)

    def gathered_back(side):
        return mxu(w2p[:, 0 : K * C], spreads[0:K, :, side * n : (side + 1) * n].reshape(K * C, n))

    def pair_weights():
        for k in range(0, K_EVEN, 2):
            first = w2_ref[k * C : (k + 1) * C, :]
            second = w2_ref[(k + 1) * C : (k + 2) * C, :] if k + 1 < K else jnp.zeros_like(first)
            w2p[:, k * C : (k + 2) * C] = jnp.concatenate([first, second], axis=1)

    def weight_parts_wide(which, table):
        for g in range(0, K_EVEN, 4):
            out = mxu(table, spreads[g : g + 4].reshape(4 * C, 2 * n), ((1,), (1,))).astype(BF16)
            for j in range(2):
                rows = out[:, j * 2 * C : (j + 1) * 2 * C].reshape(C // TILE, TILE, 2 * C)
                first = (g // 2 + j) * (C // TILE)
                parts[which, first // pad, first % pad : first % pad + C // TILE] = rows

    low16 = iota((C, 2 * V), 1).astype(F32).astype(BF16) < V
    low32 = iota((C, 2 * V), 1) < V

    def fill(table, value, first):
        value = value.astype(F32)
        turned = pltpu.roll(value, V, 1)
        table[first] = jnp.where(low32, value, turned).astype(BF16)
        table[first + 1] = jnp.where(low32, turned, value).astype(BF16)

    def fill_own(table, value):
        for p in range(blocks // 2):
            fill(table, value[:, p * 2 * V : (p + 1) * 2 * V], 2 * p)

    def fill_halo(table, ref):
        for i in range(2):
            fill(table, ref[i], blocks + 2 * i)

    def pick(table, picked):
        for k in range(K):
            for p in range(blocks // 2):
                lanes = slice(p * 2 * V, (p + 1) * 2 * V)
                both = jnp.where(low16, table[slots[k * blocks + 2 * p]], table[slots[k * blocks + 2 * p + 1]])
                picked[k, :, lanes] = mxu(both, hot(spot_pair, pair_rows[k, :, lanes])).astype(BF16)

    def convolved(wt, picked):
        return mxu(wt[...], picked[...].reshape(K * C, n))

    def weight_parts(which, picked, grad):
        zero = jnp.zeros((C, n), BF16)
        pair = jnp.concatenate(
            [jnp.concatenate([grad, zero], axis=1), jnp.concatenate([zero, grad], axis=1)], axis=0
        )
        for g in range(0, K, group_of):
            both = jnp.concatenate(
                [picked[g : g + group_of, 0 : C // 2, :], picked[g : g + group_of, C // 2 : C, :]], axis=2
            ).reshape(group_of * C // 2, 2 * n)
            out = mxu(both, pair, ((1,), (1,))).astype(BF16)
            tiles = group_of * C // 2 // TILE
            out = out.reshape(tiles, TILE, 2 * C)
            first = g * C // 2 // TILE
            cut = min(max(pad - first, 0), tiles)
            if cut > 0:
                parts[which, 0, first : first + cut] = out[:cut]
            if cut < tiles:
                parts[which, 1, first + cut - pad : first + tiles - pad] = out[cut:]

    class Batch:
        def __init__(self, copies, send, recv, sent, landed):
            for copy in copies:
                copy.start()
            self.all = remote(sent, landed, send, recv, twin)

        def wait_recv(self):
            self.all.wait_recv()

        def wait_send(self):
            self.all.wait_send()

    def to_neighbours(slot, low, high, into):
        send, recv = halo_send.at[slot], halo_recv.at[slot]
        copies = [remote(low, into.at[1], send, recv, before), remote(high, into.at[0], send, recv, after)]
        return [Batch(copies, send, recv, into, into)]

    def arrive(copies):
        for copy in copies:
            copy.wait_recv()

    offsets = [
        (dx, dy, dz) for dx in range(n_x) for dy in range(n_y) for dz in range(ZPAR) if (dx, dy, dz) != (0, 0, 0)
    ]
    offsets.sort(key=lambda o: -(min(o[0], n_x - o[0]) + min(o[1], n_y - o[1]) + o[2]))

    def member(x, y, z):
        return (z * n_y + y) * n_x + x

    me = member(x, y, z_par)

    def to_twin(stage, which, src, dst):
        copy = remote(src, dst, pair_send.at[stage, which], pair_recv.at[stage, which], twin)
        copy.start()
        return [copy]

    def to_members(stage, which, src_of, dst, all_of):
        send, recv = group_send.at[stage, which], group_recv.at[stage, which]
        copies = []
        for dx, dy, dz in offsets:
            xx, yy, zz = (x + dx) % n_x, (y + dy) % n_y, (z_par + dz) % ZPAR
            target = (((z // ZPAR) * ZPAR + zz) * n_y + yy, xx * CORES + core)
            copies.append(remote(src_of(member(xx, yy, zz)), dst, send, recv, target))
        return [Batch(copies, send, recv, all_of, all_of)]

    def to_depths(which, src, dst):
        send, recv = deep_send.at[which], deep_recv.at[which]
        copies = []
        for j in [j for i in range(deep // 2, 0, -1) for j in sorted({i, deep - i})]:
            copies.append(remote(src, dst, send, recv, at(dz=j * ZPAR)))
        every = got3.at[which, 0 : deep - 1]
        return [Batch(copies, send, recv, every, every)]

    spreads[K:] = jnp.zeros((K_EVEN - K, C, 2 * n), BF16)
    used = K * C // 2 // TILE - pad
    parts[0, 1, used:] = jnp.zeros((pad - used, TILE, 2 * C), BF16)
    for which in range(2):
        mid[which, pad:] = jnp.zeros((mid.shape[1] - pad, TILE, 2 * C), BF16)
    loads["x"].wait()
    feat = to_channels(x_ref)
    feat_ref[...] = feat
    loads["ct"].wait()
    cot = to_channels(ct_ref)
    pl.semaphore_wait(barrier, len(near))
    feat_copies = to_neighbours(0, feat_ref.at[:, 0:half], feat_ref.at[:, half:n], halo_in)
    relay_signal(0)
    sent = list(feat_copies)

    loads["vox"].wait()
    loads["src"].wait()
    make_rows()
    spread_out(cot, 1)
    loads["w2"].wait()
    pair_weights()
    rim = gathered_back(1).astype(BF16)
    for i in range(2):
        rim_out[0, i] = rim[:, i * half : (i + 1) * half]
    rim_copies = to_neighbours(1, rim_out.at[0, 0], rim_out.at[0, 1], rim_in.at[0])
    sent += rim_copies
    relay_wait(0)
    relay_signal(1)
    loads["w1"].wait()
    w1t[...] = w1_ref[...].T
    fill_own(table1, feat)

    arrive(feat_copies)
    fill_halo(table1, halo_in)
    pick(table1, picked1)
    pre = convolved(w1t, picked1)
    sig = 1.0 / (1.0 + jnp.exp(-pre))
    hid = (pre * sig).astype(BF16)
    hidden[...] = hid
    hid_copies = to_neighbours(2, hidden.at[:, 0:half], hidden.at[:, half:n], halo_mid)
    sent += hid_copies
    relay_wait(1)
    relay_signal(2)

    spread_out(cot, 0)
    grad_hidden = gathered_back(0)
    arrive(rim_copies)
    rims = jnp.concatenate([rim_in[0, 0], rim_in[0, 1]], axis=1).astype(F32)
    grad_pre = ((grad_hidden + rims) * (sig * (1.0 + pre * (1.0 - sig)))).astype(BF16)
    weight_parts(0, picked1, grad_pre)

    def mine_of(which):
        return sums.at[which, core, pl.ds(me * per, per)]

    def reduce_pair(which):
        return to_twin(0, which, parts.at[which, 1 - core], got1.at[which])

    def scatter_reduce(which, copies):
        arrive(copies)
        mid[which, 0:pad] = (parts[which, core].astype(F32) + got1[which].astype(F32)).astype(BF16)
        got2[which, me] = mid[which, pl.ds(me * per, per)]
        every = got2.at[which, 0 : len(offsets)]
        return to_members(
            0, which, lambda other: mid.at[which, pl.ds(other * per, per)], got2.at[which, me], every
        )

    def added(ref, which, count):
        totals = [ref[which, i].astype(F32) for i in range(count)]
        while len(totals) > 1:
            totals = [a + b for a, b in zip(totals[::2], totals[1::2])]
        return totals[0].astype(BF16)

    def reduce_deep(which, copies):
        arrive(copies)
        got3[which, depth] = added(got2, which, len(offsets) + 1)
        mine = got3.at[which, depth]
        return to_depths(which, mine, mine)

    def gather_members(which, copies):
        arrive(copies)
        sums[which, core, pl.ds(me * per, per)] = added(got3, which, deep)
        mine = mine_of(which)
        every = sums.at[which, core, 0 : len(offsets) * per]
        return to_members(1, which, lambda other: mine, mine, every)

    def gather_pair(which, copies):
        arrive(copies)
        mine = sums.at[which, core, 0:pad]
        return to_twin(1, which, mine, mine)

    factor = float(n_x * CORES * space * n) ** (-0.5)

    def lay_out(which, side, out):
        for i in range(pad):
            tile = side * pad + i
            value = sums[which, side, i].astype(F32) * factor
            if which == 0:
                k, top = tile // 2, pl.multiple_of(tile % 2 * TILE, TILE)
                out[k, pl.ds(top, TILE), :] = value[:, :C]
                out[k, pl.ds(top + C // 2, TILE), :] = value[:, C:]
            else:
                k, top = tile // 4 * 2, pl.multiple_of(tile % 4 * TILE, TILE)
                out[k, pl.ds(top, TILE), :] = value[:, :C]
                out[k + 1, pl.ds(top, TILE), :] = value[:, C:]

    def drain(copies):
        for copy in copies:
            copy.wait_send()

    one = reduce_pair(0)
    sent += one
    relay_wait(2)
    relay_signal(3)
    w2t[...] = w2_ref[...].T
    relay_wait(3)
    one = scatter_reduce(0, one)
    sent += one
    arrive(hid_copies)
    weight_parts_wide(1, jnp.concatenate([hid, halo_mid[0], halo_mid[1]], axis=1))
    two = reduce_pair(1)
    sent += two

    spread(w1_ref, grad_pre)
    two = scatter_reduce(1, two)
    sent += two
    rim = scattered(n).astype(BF16)
    for i in range(2):
        rim_out[1, i] = rim[:, i * half : (i + 1) * half]
    last_copies = to_neighbours(3, rim_out.at[1, 0], rim_out.at[1, 1], rim_in.at[1])
    sent += last_copies
    relay_end()
    one = reduce_deep(0, one)
    sent += one
    fill_own(table2, hid)
    fill_halo(table2, halo_mid)
    pick(table2, picked2)
    from_channels(convolved(w2t, picked2).astype(BF16), conv_ref)
    two = reduce_deep(1, two)
    sent += two
    grad_in = scattered(0)

    one = gather_members(0, one)
    sent += one
    arrive(last_copies)
    rims = jnp.concatenate([rim_in[1, 0], rim_in[1, 1]], axis=1).astype(F32)
    grad_input = (grad_in + rims).astype(BF16)
    two = gather_members(1, two)
    sent += two
    from_channels(grad_input, gin_ref)
    one = gather_pair(0, one)
    sent += one
    lay_out(0, core, grad1_ref)
    arrive(one)
    lay_out(0, 1 - core, grad1_ref)
    two = gather_pair(1, two)
    drain(sent)
    lay_out(1, core, grad2_ref)
    arrive(two)
    lay_out(1, 1 - core, grad2_ref)
    drain(two)


def put_kernel(*refs):
    count = len(refs) // 2
    sem = refs[-1]
    copies = []
    for i, (src, dst) in enumerate(zip(refs[:count], refs[count:-1])):
        size = dst.shape[0]
        cuts = 3 if size == K else 1
        for c in range(cuts):
            part = pl.ds(c * size // cuts, size // cuts)
            copies.append(pltpu.make_async_copy(src.at[part], dst.at[part], sem.at[i, c]))
    for copy in copies:
        copy.start()
    for copy in copies:
        copy.wait()


def per_device(sizes, features, sources, voxels, cotangent, weight_one, weight_two):
    n_x, n_y, n_z = sizes
    members = n_x * n_y * ZPAR
    deep = n_z // ZPAR
    blocks = features.shape[1]
    n = blocks * V
    half = n // 2
    pad = TILES // CORES
    per = -(-pad // members)
    slots = blocks + 2 * HALO
    scratch = [
        pltpu.VMEM((blocks, V * C), BF16),
        pltpu.VMEM((blocks, V * C), BF16),
        pltpu.SMEM((blocks, K), jnp.int32),
        pltpu.VMEM((blocks, K * V), jnp.int32),
        pltpu.VMEM((K * C, C), BF16),
        pltpu.VMEM((K * C, C), BF16),
        pltpu.SMEM((K * blocks,), jnp.int32),
        pltpu.VMEM((K, 1, n), F32),
        pltpu.VMEM((K, 1, n), F32),
        pltpu.VMEM((n // 2, 2 * C), F32),
        pltpu.VMEM((blocks, V * C), F32),
        pltpu.VMEM((slots, C, 2 * V), BF16),
        pltpu.VMEM((slots, C, 2 * V), BF16),
        pltpu.VMEM((C, n), BF16),
        pltpu.VMEM((K, C, n), BF16),
        pltpu.VMEM((K, C, n), BF16),
        pltpu.VMEM((K, C, n), BF16),
        pltpu.VMEM((K_EVEN, C, 2 * n), BF16),
        pltpu.VMEM((C, K_EVEN * C), BF16),
        pltpu.VMEM((C, K * C), BF16),
        pltpu.VMEM((C, K * C), BF16),
        pltpu.VMEM((2, C, half), BF16),
        pltpu.VMEM((2, C, half), BF16),
        pltpu.VMEM((2, 2, C, half), BF16),
        pltpu.VMEM((2, 2, C, half), BF16),
        pltpu.VMEM((C, n), BF16),
        pltpu.VMEM((2, CORES, pad, TILE, 2 * C), BF16),
        pltpu.VMEM((2, pad, TILE, 2 * C), BF16),
        pltpu.VMEM((2, members * per, TILE, 2 * C), BF16),
        pltpu.VMEM((2, members, per, TILE, 2 * C), BF16),
        pltpu.VMEM((2, deep, per, TILE, 2 * C), BF16),
        pltpu.VMEM((2, CORES, members * per, TILE, 2 * C), BF16),
        pltpu.SemaphoreType.DMA((6,)),
        pltpu.SemaphoreType.DMA((4,)),
        pltpu.SemaphoreType.DMA((4,)),
        pltpu.SemaphoreType.DMA((2, 2)),
        pltpu.SemaphoreType.DMA((2, 2)),
        pltpu.SemaphoreType.DMA((2, 2)),
        pltpu.SemaphoreType.DMA((2, 2)),
        pltpu.SemaphoreType.DMA((2,)),
        pltpu.SemaphoreType.DMA((2,)),
        pltpu.SemaphoreType.REGULAR((7,)),
    ]
    outs = (
        jax.ShapeDtypeStruct((blocks, V * C), BF16),
        jax.ShapeDtypeStruct((blocks, V * C), BF16),
        jax.ShapeDtypeStruct((K, C, C), F32),
        jax.ShapeDtypeStruct((K, C, C), F32),
    )
    vmem = pl.BlockSpec(memory_space=pltpu.VMEM)
    anywhere = pl.BlockSpec(memory_space=pl.ANY)
    hbm = pl.BlockSpec(memory_space=pltpu.HBM)
    even = jax.ShapeDtypeStruct((K_EVEN, C, C), F32)
    results = pl.pallas_call(
        functools.partial(step_kernel, sizes),
        out_shape=(*outs[:2], even, even),
        in_specs=[hbm] * 6,
        out_specs=(vmem,) * 4,
        scratch_shapes=scratch,
        compiler_params=pltpu.CompilerParams(
            collective_id=0, has_side_effects=True, vmem_limit_bytes=32 * 1024 * 1024
        ),
        name="step",
    )(
        *[
            pltpu.with_memory_space_constraint(a, pltpu.HBM)
            for a in (
                features[0],
                cotangent[0],
                sources[0],
                voxels[0],
                weight_one.reshape(K * C, C),
                weight_two.reshape(K * C, C),
            )
        ]
    )
    conv, gin, grad_one, grad_two = pl.pallas_call(
        put_kernel,
        out_shape=outs,
        in_specs=[anywhere] * 4,
        out_specs=(hbm,) * 4,
        scratch_shapes=[pltpu.SemaphoreType.DMA((4, 3))],
        compiler_params=pltpu.CompilerParams(vmem_limit_bytes=1024 * 1024),
        name="put",
    )(*results)
    return conv[None], gin[None], grad_one, grad_two


def solution(mesh):
    space, dp = mesh.shape["space"], mesh.shape["dp"]
    sizes = (dp // CORES, Y, space // Y)
    wide = P("dp", "space", None)
    return jax.shard_map(
        functools.partial(per_device, sizes),
        mesh=mesh,
        in_specs=(wide, wide, wide, wide, P(), P()),
        out_specs=(wide, wide, P(), P()),
        check_vma=False,
    )
```

```python
import functools

import jax
import jax.numpy as jnp
from jax import lax
from jax.experimental import pallas as pl
from jax.experimental.pallas import tpu as pltpu
from jax.sharding import PartitionSpec as P

C = 64
V = 64
K = 27
HALO = 2
Y = 4
ZPAR = 2
CORES = 2
TILE = 16
K_EVEN = K + K % 2
TILES = K_EVEN * C * C // (TILE * 2 * C)
MESH = pl.DeviceIdType.MESH
BF16 = jnp.bfloat16
F32 = jnp.float32


def mxu(a, b, dims=((1,), (0,))):
    return lax.dot_general(a, b, (dims, ((), ())), preferred_element_type=F32)


def step_kernel(
    sizes,
    x_hbm,
    ct_hbm,
    src_hbm,
    vox_hbm,
    w1_hbm,
    w2_hbm,
    conv_ref,
    gin_ref,
    grad1_ref,
    grad2_ref,
    x_ref,
    ct_ref,
    src_ref,
    vox_ref,
    w1_ref,
    w2_ref,
    slots,
    pair_rows,
    wide_rows,
    turn,
    flat,
    table1,
    table2,
    feat_ref,
    picked1,
    picked2,
    back,
    spreads,
    w2p,
    w1t,
    w2t,
    halo_in,
    halo_mid,
    rim_out,
    rim_in,
    hidden,
    parts,
    got1,
    mid,
    got2,
    got3,
    sums,
    load_sem,
    halo_send,
    halo_recv,
    pair_send,
    pair_recv,
    group_send,
    group_recv,
    deep_send,
    deep_recv,
    relay,
):
    loads = {}

    def load(name, src, dst):
        loads[name] = pltpu.make_async_copy(src, dst, load_sem.at[len(loads)])
        loads[name].start()

    load("x", x_hbm, x_ref)
    load("ct", ct_hbm, ct_ref)
    n_x, n_y, n_z = sizes
    deep = n_z // ZPAR
    space = n_y * n_z
    blocks = x_ref.shape[0]
    n = feat_ref.shape[1]
    half = n // 2
    s = lax.axis_index("space")
    d = lax.axis_index("dp")
    x, core = d // CORES, d % CORES
    z, y = s // n_y, s % n_y
    z_par, depth = z % ZPAR, z // ZPAR
    pad = TILES // CORES
    per = sums.shape[2] // (n_x * n_y * ZPAR)

    def at(dx=0, dy=0, dz=0, core=core):
        return (((z + dz) % n_z) * n_y + (y + dy) % n_y, ((x + dx) % n_x) * CORES + core)

    before = ((s + space - 1) % space, d)
    after = ((s + 1) % space, d)
    twin = at(core=1 - core)
    x_pair = [at(dx=1), at(dx=n_x - 1)]
    y_pair = [at(dy=1), at(dy=n_y - 1)]

    def z_pair(step):
        return [at(dz=step), at(dz=n_z - step)]

    other_z = (((z // ZPAR) * ZPAR + 1 - z_par) * n_y + y, d)

    def signal(sem, devices):
        for device in devices:
            pl.semaphore_signal(sem, inc=1, device_id=device, device_id_type=MESH)

    barrier = pltpu.get_barrier_semaphore()
    near = [before, after, twin] + x_pair + y_pair + z_pair(1)
    signal(barrier, near)

    z_steps = []
    while 2 ** len(z_steps) < n_z // 2:
        z_steps.append(2 ** len(z_steps))

    def relay_signal(i):
        if i == 0:
            signal(relay.at[0], x_pair)
        elif i <= 2:
            signal(relay.at[i], y_pair)
        else:
            signal(relay.at[i], [other_z])
        if i < len(z_steps):
            signal(relay.at[4 + i], z_pair(z_steps[i]))

    def relay_wait(i):
        pl.semaphore_wait(relay.at[i], 2 if i <= 2 else 1)
        if i < len(z_steps) - 1:
            pl.semaphore_wait(relay.at[4 + i], 2)

    def relay_end():
        pl.semaphore_wait(relay.at[4 + len(z_steps) - 1], 2)

    def remote(src, dst, send, recv, target):
        return pltpu.make_async_remote_copy(
            src_ref=src, dst_ref=dst, send_sem=send, recv_sem=recv, device_id=target, device_id_type=MESH
        )

    load("vox", vox_hbm, vox_ref)
    load("src", src_hbm, src_ref)
    load("w2", w2_hbm, w2_ref)
    load("w1", w1_hbm, w1_ref)

    def iota(shape, dim):
        return lax.broadcasted_iota(jnp.int32, shape, dim)

    pairs = V // 2
    old = iota((n, n), 0)
    parity, rest = old // (n // 2), old % (n // 2)
    order = jnp.where(rest // pairs * V + rest % pairs * 2 + parity == iota((n, n), 1), 1.0, 0.0).astype(BF16)

    def to_channels(ref):
        wide = ref[...].astype(F32)
        for j in range(pairs):
            turn[j * blocks : (j + 1) * blocks, :] = wide[:, j * 2 * C : (j + 1) * 2 * C]
        rows = jnp.concatenate([turn[pl.ds(b, pairs, stride=blocks), :] for b in range(blocks)], axis=0)
        lanes = rows.T
        both = jnp.concatenate([lanes[:C], lanes[C:]], axis=1).astype(BF16)
        return mxu(both, order).astype(BF16)

    def from_channels(value, out_ref):
        both = mxu(value, order, ((1,), (1,)))
        rows = jnp.concatenate([both[:, : n // 2], both[:, n // 2 :]], axis=0).T
        turn[...] = rows
        for j in range(pairs):
            flat[:, j * 2 * C : (j + 1) * 2 * C] = turn[pl.ds(j, blocks, stride=pairs), :]
        out_ref[...] = flat[...].astype(BF16)

    low_row = iota((1, 2 * V), 1) < V
    shift = blocks.bit_length() - 1

    def make_rows():
        for k in range(K):
            for b in range(blocks):
                source = src_ref[b, k]
                owner, place = source >> shift, source & (blocks - 1)
                slots[k * blocks + b] = jnp.where(
                    owner == s, place, jnp.where(owner < s, place + HALO, blocks + HALO + place)
                )
            start = k // 2 * 2 * V
            if start + 2 * V <= K * V:
                here = vox_ref[:, start : start + 2 * V]
            else:
                here = jnp.concatenate([vox_ref[:, start : start + V]] * 2, axis=1)
            there = pltpu.roll(here, V, 1)
            first, second = (here, there) if k % 2 == 0 else (there, here)
            for p in range(blocks // 2):
                row = jnp.where(low_row, first[2 * p : 2 * p + 1], second[2 * p + 1 : 2 * p + 2])
                none = row >= V
                base = jnp.where(low_row, slots[k * blocks + 2 * p] * V, slots[k * blocks + 2 * p + 1] * V)
                lanes = slice(p * 2 * V, (p + 1) * 2 * V)
                pair_rows[k, :, lanes] = jnp.where(none, -1, row + jnp.where(low_row, 0, V)).astype(F32)
                wide_rows[k, :, lanes] = jnp.where(none, -1, row + base).astype(F32)

    group_of = 9
    spot = iota((n, n), 0).astype(F32).astype(BF16)
    spot_pair = iota((2 * V, 2 * V), 0).astype(F32).astype(BF16)

    def hot(where, row):
        return jnp.where(where == row.astype(BF16), jnp.ones_like(where), jnp.zeros_like(where))

    def spread(w_ref, grad):
        for g in range(0, K, group_of):
            out = mxu(w_ref[g * C : (g + group_of) * C, :], grad).astype(BF16)
            back[g : g + group_of] = out.reshape(group_of, C, n)

    def scattered(lo):
        def some(g, total):
            for i in range(group_of):
                k = g * group_of + i
                total = total + mxu(back[k], hot(spot, wide_rows[k] - lo), ((1,), (1,)))
            return total

        return lax.fori_loop(0, K // group_of, some, jnp.zeros((C, n), F32))

    def spread_out(grad, side):
        def some(g, carry):
            for i in range(group_of):
                k = g * group_of + i
                out = mxu(grad, hot(spot, wide_rows[k] - side * n), ((1,), (1,)))
                spreads[k, :, side * n : (side + 1) * n] = out.astype(BF16)
            return carry

        lax.fori_loop(0, K // group_of, some, 0)

    def gathered_back(side):
        return mxu(w2p[:, 0 : K * C], spreads[0:K, :, side * n : (side + 1) * n].reshape(K * C, n))

    def pair_weights():
        for k in range(0, K_EVEN, 2):
            first = w2_ref[k * C : (k + 1) * C, :]
            second = w2_ref[(k + 1) * C : (k + 2) * C, :] if k + 1 < K else jnp.zeros_like(first)
            w2p[:, k * C : (k + 2) * C] = jnp.concatenate([first, second], axis=1)

    def weight_parts_wide(which, table):
        for g in range(0, K_EVEN, 4):
            out = mxu(table, spreads[g : g + 4].reshape(4 * C, 2 * n), ((1,), (1,))).astype(BF16)
            for j in range(2):
                rows = out[:, j * 2 * C : (j + 1) * 2 * C].reshape(C // TILE, TILE, 2 * C)
                first = (g // 2 + j) * (C // TILE)
                parts[which, first // pad, first % pad : first % pad + C // TILE] = rows

    low16 = iota((C, 2 * V), 1).astype(F32).astype(BF16) < V
    low32 = iota((C, 2 * V), 1) < V

    def fill(table, value, first):
        value = value.astype(F32)
        turned = pltpu.roll(value, V, 1)
        table[first] = jnp.where(low32, value, turned).astype(BF16)
        table[first + 1] = jnp.where(low32, turned, value).astype(BF16)

    def fill_own(table, value):
        for p in range(blocks // 2):
            fill(table, value[:, p * 2 * V : (p + 1) * 2 * V], 2 * p)

    def fill_halo(table, ref):
        for i in range(2):
            fill(table, ref[i], blocks + 2 * i)

    def pick(table, picked):
        for k in range(K):
            for p in range(blocks // 2):
                lanes = slice(p * 2 * V, (p + 1) * 2 * V)
                both = jnp.where(low16, table[slots[k * blocks + 2 * p]], table[slots[k * blocks + 2 * p + 1]])
                picked[k, :, lanes] = mxu(both, hot(spot_pair, pair_rows[k, :, lanes])).astype(BF16)

    def convolved(wt, picked):
        return mxu(wt[...], picked[...].reshape(K * C, n))

    def weight_parts(which, picked, grad):
        zero = jnp.zeros((C, n), BF16)
        pair = jnp.concatenate(
            [jnp.concatenate([grad, zero], axis=1), jnp.concatenate([zero, grad], axis=1)], axis=0
        )
        for g in range(0, K, group_of):
            both = jnp.concatenate(
                [picked[g : g + group_of, 0 : C // 2, :], picked[g : g + group_of, C // 2 : C, :]], axis=2
            ).reshape(group_of * C // 2, 2 * n)
            out = mxu(both, pair, ((1,), (1,))).astype(BF16)
            tiles = group_of * C // 2 // TILE
            out = out.reshape(tiles, TILE, 2 * C)
            first = g * C // 2 // TILE
            cut = min(max(pad - first, 0), tiles)
            if cut > 0:
                parts[which, 0, first : first + cut] = out[:cut]
            if cut < tiles:
                parts[which, 1, first + cut - pad : first + tiles - pad] = out[cut:]

    class Batch:
        def __init__(self, copies, send, recv, sent, landed):
            for copy in copies:
                copy.start()
            self.all = remote(sent, landed, send, recv, twin)

        def wait_recv(self):
            self.all.wait_recv()

        def wait_send(self):
            self.all.wait_send()

    def to_neighbours(slot, low, high, into):
        send, recv = halo_send.at[slot], halo_recv.at[slot]
        copies = [remote(low, into.at[1], send, recv, before), remote(high, into.at[0], send, recv, after)]
        return [Batch(copies, send, recv, into, into)]

    def arrive(copies):
        for copy in copies:
            copy.wait_recv()

    offsets = [
        (dx, dy, dz) for dx in range(n_x) for dy in range(n_y) for dz in range(ZPAR) if (dx, dy, dz) != (0, 0, 0)
    ]
    offsets.sort(key=lambda o: -(min(o[0], n_x - o[0]) + min(o[1], n_y - o[1]) + o[2]))

    def member(x, y, z):
        return (z * n_y + y) * n_x + x

    me = member(x, y, z_par)

    def to_twin(stage, which, src, dst):
        copy = remote(src, dst, pair_send.at[stage, which], pair_recv.at[stage, which], twin)
        copy.start()
        return [copy]

    def to_members(stage, which, src_of, dst, all_of):
        send, recv = group_send.at[stage, which], group_recv.at[stage, which]
        copies = []
        for dx, dy, dz in offsets:
            xx, yy, zz = (x + dx) % n_x, (y + dy) % n_y, (z_par + dz) % ZPAR
            target = (((z // ZPAR) * ZPAR + zz) * n_y + yy, xx * CORES + core)
            copies.append(remote(src_of(member(xx, yy, zz)), dst, send, recv, target))
        return [Batch(copies, send, recv, all_of, all_of)]

    owners = -(-pad // per)

    class Gather:
        def __init__(self, which, mine):
            send, recv = group_send.at[1, which], group_recv.at[1, which]

            def some(count):
                ref = sums.at[which, core, 0 : count * per]
                return remote(ref, ref, send, recv, twin)

            self.out, self.few, self.many = some(len(offsets)), some(owners - 1), some(owners)
            copies = []
            for dx, dy, dz in offsets:
                xx, yy, zz = (x + dx) % n_x, (y + dy) % n_y, (z_par + dz) % ZPAR
                target = (((z // ZPAR) * ZPAR + zz) * n_y + yy, xx * CORES + core)
                copies.append(remote(mine, mine, send, recv, target))

            @pl.when(me < owners)
            def _():
                for copy in copies:
                    copy.start()

        def wait_recv(self):
            @pl.when(me < owners)
            def _():
                self.few.wait_recv()

            @pl.when(me >= owners)
            def _():
                self.many.wait_recv()

        def wait_send(self):
            @pl.when(me < owners)
            def _():
                self.out.wait_send()

    def to_depths(which, src, dst):
        send, recv = deep_send.at[which], deep_recv.at[which]
        copies = []
        for j in [j for i in range(deep // 2, 0, -1) for j in sorted({i, deep - i})]:
            copies.append(remote(src, dst, send, recv, at(dz=j * ZPAR)))
        every = got3.at[which, 0 : deep - 1]
        return [Batch(copies, send, recv, every, every)]

    spreads[K:] = jnp.zeros((K_EVEN - K, C, 2 * n), BF16)
    used = K * C // 2 // TILE - pad
    parts[0, 1, used:] = jnp.zeros((pad - used, TILE, 2 * C), BF16)
    for which in range(2):
        mid[which, pad:] = jnp.zeros((mid.shape[1] - pad, TILE, 2 * C), BF16)
    loads["x"].wait()
    feat = to_channels(x_ref)
    feat_ref[...] = feat
    loads["ct"].wait()
    cot = to_channels(ct_ref)
    pl.semaphore_wait(barrier, len(near))
    feat_copies = to_neighbours(0, feat_ref.at[:, 0:half], feat_ref.at[:, half:n], halo_in)
    relay_signal(0)
    sent = list(feat_copies)

    loads["vox"].wait()
    loads["src"].wait()
    make_rows()
    spread_out(cot, 1)
    loads["w2"].wait()
    pair_weights()
    rim = gathered_back(1).astype(BF16)
    for i in range(2):
        rim_out[0, i] = rim[:, i * half : (i + 1) * half]
    rim_copies = to_neighbours(1, rim_out.at[0, 0], rim_out.at[0, 1], rim_in.at[0])
    sent += rim_copies
    relay_wait(0)
    relay_signal(1)
    loads["w1"].wait()
    w1t[...] = w1_ref[...].T
    fill_own(table1, feat)

    arrive(feat_copies)
    fill_halo(table1, halo_in)
    pick(table1, picked1)
    pre = convolved(w1t, picked1)
    sig = 1.0 / (1.0 + jnp.exp(-pre))
    hid = (pre * sig).astype(BF16)
    hidden[...] = hid
    hid_copies = to_neighbours(2, hidden.at[:, 0:half], hidden.at[:, half:n], halo_mid)
    sent += hid_copies
    relay_wait(1)
    relay_signal(2)

    spread_out(cot, 0)
    grad_hidden = gathered_back(0)
    arrive(rim_copies)
    rims = jnp.concatenate([rim_in[0, 0], rim_in[0, 1]], axis=1).astype(F32)
    grad_pre = ((grad_hidden + rims) * (sig * (1.0 + pre * (1.0 - sig)))).astype(BF16)
    weight_parts(0, picked1, grad_pre)

    def mine_of(which):
        return sums.at[which, core, pl.ds(me * per, per)]

    def reduce_pair(which):
        return to_twin(0, which, parts.at[which, 1 - core], got1.at[which])

    def scatter_reduce(which, copies):
        arrive(copies)
        mid[which, 0:pad] = (parts[which, core].astype(F32) + got1[which].astype(F32)).astype(BF16)
        got2[which, me] = mid[which, pl.ds(me * per, per)]
        every = got2.at[which, 0 : len(offsets)]
        return to_members(
            0, which, lambda other: mid.at[which, pl.ds(other * per, per)], got2.at[which, me], every
        )

    def added(ref, which, count):
        totals = [ref[which, i].astype(F32) for i in range(count)]
        while len(totals) > 1:
            totals = [a + b for a, b in zip(totals[::2], totals[1::2])]
        return totals[0].astype(BF16)

    def reduce_deep(which, copies):
        arrive(copies)
        got3[which, depth] = added(got2, which, len(offsets) + 1)
        mine = got3.at[which, depth]
        return to_depths(which, mine, mine)

    def gather_members(which, copies):
        arrive(copies)
        sums[which, core, pl.ds(me * per, per)] = added(got3, which, deep)
        mine = mine_of(which)
        return [Gather(which, mine)]

    def gather_pair(which, copies):
        arrive(copies)
        mine = sums.at[which, core, 0:pad]
        return to_twin(1, which, mine, mine)

    factor = float(n_x * CORES * space * n) ** (-0.5)

    def lay_out(which, side, out):
        for i in range(pad):
            tile = side * pad + i
            value = sums[which, side, i].astype(F32) * factor
            if which == 0:
                k, top = tile // 2, pl.multiple_of(tile % 2 * TILE, TILE)
                out[k, pl.ds(top, TILE), :] = value[:, :C]
                out[k, pl.ds(top + C // 2, TILE), :] = value[:, C:]
            else:
                k, top = tile // 4 * 2, pl.multiple_of(tile % 4 * TILE, TILE)
                out[k, pl.ds(top, TILE), :] = value[:, :C]
                out[k + 1, pl.ds(top, TILE), :] = value[:, C:]

    def drain(copies):
        for copy in copies:
            copy.wait_send()

    one = reduce_pair(0)
    sent += one
    relay_wait(2)
    relay_signal(3)
    w2t[...] = w2_ref[...].T
    relay_wait(3)
    one = scatter_reduce(0, one)
    sent += one
    arrive(hid_copies)
    weight_parts_wide(1, jnp.concatenate([hid, halo_mid[0], halo_mid[1]], axis=1))
    two = reduce_pair(1)
    sent += two

    spread(w1_ref, grad_pre)
    two = scatter_reduce(1, two)
    sent += two
    rim = scattered(n).astype(BF16)
    for i in range(2):
        rim_out[1, i] = rim[:, i * half : (i + 1) * half]
    last_copies = to_neighbours(3, rim_out.at[1, 0], rim_out.at[1, 1], rim_in.at[1])
    sent += last_copies
    relay_end()
    one = reduce_deep(0, one)
    sent += one
    fill_own(table2, hid)
    fill_halo(table2, halo_mid)
    pick(table2, picked2)
    from_channels(convolved(w2t, picked2).astype(BF16), conv_ref)
    two = reduce_deep(1, two)
    sent += two
    grad_in = scattered(0)

    one = gather_members(0, one)
    sent += one
    arrive(last_copies)
    rims = jnp.concatenate([rim_in[1, 0], rim_in[1, 1]], axis=1).astype(F32)
    grad_input = (grad_in + rims).astype(BF16)
    two = gather_members(1, two)
    sent += two
    from_channels(grad_input, gin_ref)
    one = gather_pair(0, one)
    sent += one
    lay_out(0, core, grad1_ref)
    arrive(one)
    lay_out(0, 1 - core, grad1_ref)
    two = gather_pair(1, two)
    drain(sent)
    lay_out(1, core, grad2_ref)
    arrive(two)
    lay_out(1, 1 - core, grad2_ref)
    drain(two)


def put_kernel(*refs):
    count = len(refs) // 2
    sem = refs[-1]
    copies = []
    for i, (src, dst) in enumerate(zip(refs[:count], refs[count:-1])):
        size = dst.shape[0]
        cuts = 3 if size == K else 1
        for c in range(cuts):
            part = pl.ds(c * size // cuts, size // cuts)
            copies.append(pltpu.make_async_copy(src.at[part], dst.at[part], sem.at[i, c]))
    for copy in copies:
        copy.start()
    for copy in copies:
        copy.wait()


def per_device(sizes, features, sources, voxels, cotangent, weight_one, weight_two):
    n_x, n_y, n_z = sizes
    members = n_x * n_y * ZPAR
    deep = n_z // ZPAR
    blocks = features.shape[1]
    n = blocks * V
    half = n // 2
    pad = TILES // CORES
    per = -(-pad // members)
    slots = blocks + 2 * HALO
    scratch = [
        pltpu.VMEM((blocks, V * C), BF16),
        pltpu.VMEM((blocks, V * C), BF16),
        pltpu.SMEM((blocks, K), jnp.int32),
        pltpu.VMEM((blocks, K * V), jnp.int32),
        pltpu.VMEM((K * C, C), BF16),
        pltpu.VMEM((K * C, C), BF16),
        pltpu.SMEM((K * blocks,), jnp.int32),
        pltpu.VMEM((K, 1, n), F32),
        pltpu.VMEM((K, 1, n), F32),
        pltpu.VMEM((n // 2, 2 * C), F32),
        pltpu.VMEM((blocks, V * C), F32),
        pltpu.VMEM((slots, C, 2 * V), BF16),
        pltpu.VMEM((slots, C, 2 * V), BF16),
        pltpu.VMEM((C, n), BF16),
        pltpu.VMEM((K, C, n), BF16),
        pltpu.VMEM((K, C, n), BF16),
        pltpu.VMEM((K, C, n), BF16),
        pltpu.VMEM((K_EVEN, C, 2 * n), BF16),
        pltpu.VMEM((C, K_EVEN * C), BF16),
        pltpu.VMEM((C, K * C), BF16),
        pltpu.VMEM((C, K * C), BF16),
        pltpu.VMEM((2, C, half), BF16),
        pltpu.VMEM((2, C, half), BF16),
        pltpu.VMEM((2, 2, C, half), BF16),
        pltpu.VMEM((2, 2, C, half), BF16),
        pltpu.VMEM((C, n), BF16),
        pltpu.VMEM((2, CORES, pad, TILE, 2 * C), BF16),
        pltpu.VMEM((2, pad, TILE, 2 * C), BF16),
        pltpu.VMEM((2, members * per, TILE, 2 * C), BF16),
        pltpu.VMEM((2, members, per, TILE, 2 * C), BF16),
        pltpu.VMEM((2, deep, per, TILE, 2 * C), BF16),
        pltpu.VMEM((2, CORES, members * per, TILE, 2 * C), BF16),
        pltpu.SemaphoreType.DMA((6,)),
        pltpu.SemaphoreType.DMA((4,)),
        pltpu.SemaphoreType.DMA((4,)),
        pltpu.SemaphoreType.DMA((2, 2)),
        pltpu.SemaphoreType.DMA((2, 2)),
        pltpu.SemaphoreType.DMA((2, 2)),
        pltpu.SemaphoreType.DMA((2, 2)),
        pltpu.SemaphoreType.DMA((2,)),
        pltpu.SemaphoreType.DMA((2,)),
        pltpu.SemaphoreType.REGULAR((7,)),
    ]
    outs = (
        jax.ShapeDtypeStruct((blocks, V * C), BF16),
        jax.ShapeDtypeStruct((blocks, V * C), BF16),
        jax.ShapeDtypeStruct((K, C, C), F32),
        jax.ShapeDtypeStruct((K, C, C), F32),
    )
    vmem = pl.BlockSpec(memory_space=pltpu.VMEM)
    anywhere = pl.BlockSpec(memory_space=pl.ANY)
    hbm = pl.BlockSpec(memory_space=pltpu.HBM)
    even = jax.ShapeDtypeStruct((K_EVEN, C, C), F32)
    results = pl.pallas_call(
        functools.partial(step_kernel, sizes),
        out_shape=(*outs[:2], even, even),
        in_specs=[hbm] * 6,
        out_specs=(vmem,) * 4,
        scratch_shapes=scratch,
        compiler_params=pltpu.CompilerParams(
            collective_id=0, has_side_effects=True, vmem_limit_bytes=32 * 1024 * 1024
        ),
        name="step",
    )(
        *[
            pltpu.with_memory_space_constraint(a, pltpu.HBM)
            for a in (
                features[0],
                cotangent[0],
                sources[0],
                voxels[0],
                weight_one.reshape(K * C, C),
                weight_two.reshape(K * C, C),
            )
        ]
    )
    conv, gin, grad_one, grad_two = pl.pallas_call(
        put_kernel,
        out_shape=outs,
        in_specs=[anywhere] * 4,
        out_specs=(hbm,) * 4,
        scratch_shapes=[pltpu.SemaphoreType.DMA((4, 3))],
        compiler_params=pltpu.CompilerParams(vmem_limit_bytes=1024 * 1024),
        name="put",
    )(*results)
    return conv[None], gin[None], grad_one, grad_two


def solution(mesh):
    space, dp = mesh.shape["space"], mesh.shape["dp"]
    sizes = (dp // CORES, Y, space // Y)
    wide = P("dp", "space", None)
    return jax.shard_map(
        functools.partial(per_device, sizes),
        mesh=mesh,
        in_specs=(wide, wide, wide, wide, P(), P()),
        out_specs=(wide, wide, P(), P()),
        check_vma=False,
    )
```

```python
import functools

import jax
import jax.numpy as jnp
from jax import lax
from jax.experimental import pallas as pl
from jax.experimental.pallas import tpu as pltpu
from jax.sharding import PartitionSpec as P

C = 64
V = 64
K = 27
HALO = 2
Y = 4
ZPAR = 2
CORES = 2
TILE = 16
K_EVEN = K + K % 2
TILES = K_EVEN * C * C // (TILE * 2 * C)
MESH = pl.DeviceIdType.MESH
BF16 = jnp.bfloat16
F32 = jnp.float32


def mxu(a, b, dims=((1,), (0,))):
    return lax.dot_general(a, b, (dims, ((), ())), preferred_element_type=F32)


def step_kernel(
    sizes,
    x_hbm,
    ct_hbm,
    src_hbm,
    vox_hbm,
    w1_hbm,
    w2_hbm,
    conv_ref,
    gin_ref,
    grad1_ref,
    grad2_ref,
    x_ref,
    ct_ref,
    src_ref,
    vox_ref,
    w1_ref,
    w2_ref,
    slots,
    pair_rows,
    wide_rows,
    turn,
    flat,
    table1,
    table2,
    feat_ref,
    picked1,
    picked2,
    back,
    spreads,
    w2p,
    w1t,
    w2t,
    halo_in,
    halo_mid,
    rim_out,
    rim_in,
    hidden,
    parts,
    got1,
    mid,
    got2,
    got3,
    sums,
    load_sem,
    halo_send,
    halo_recv,
    pair_send,
    pair_recv,
    group_send,
    group_recv,
    deep_send,
    deep_recv,
    relay,
):
    loads = {}

    def load(name, src, dst):
        loads[name] = pltpu.make_async_copy(src, dst, load_sem.at[len(loads)])
        loads[name].start()

    load("x", x_hbm, x_ref)
    load("ct", ct_hbm, ct_ref)
    n_x, n_y, n_z = sizes
    deep = n_z // ZPAR
    space = n_y * n_z
    blocks = x_ref.shape[0]
    n = feat_ref.shape[1]
    half = n // 2
    s = lax.axis_index("space")
    d = lax.axis_index("dp")
    x, core = d // CORES, d % CORES
    z, y = s // n_y, s % n_y
    z_par, depth = z % ZPAR, z // ZPAR
    pad = TILES // CORES
    per = sums.shape[2] // (n_x * n_y * ZPAR)

    def at(dx=0, dy=0, dz=0, core=core):
        return (((z + dz) % n_z) * n_y + (y + dy) % n_y, ((x + dx) % n_x) * CORES + core)

    before = ((s + space - 1) % space, d)
    after = ((s + 1) % space, d)
    twin = at(core=1 - core)
    x_pair = [at(dx=1), at(dx=n_x - 1)]
    y_pair = [at(dy=1), at(dy=n_y - 1)]

    def z_pair(step):
        return [at(dz=step), at(dz=n_z - step)]

    other_z = (((z // ZPAR) * ZPAR + 1 - z_par) * n_y + y, d)

    def signal(sem, devices):
        for device in devices:
            pl.semaphore_signal(sem, inc=1, device_id=device, device_id_type=MESH)

    barrier = pltpu.get_barrier_semaphore()
    near = [before, after, twin] + x_pair + y_pair + z_pair(1)
    signal(barrier, near)

    z_steps = []
    while 2 ** len(z_steps) < n_z // 2:
        z_steps.append(2 ** len(z_steps))

    def relay_signal(i):
        if i == 0:
            signal(relay.at[0], x_pair)
        elif i <= 2:
            signal(relay.at[i], y_pair)
        else:
            signal(relay.at[i], [other_z])
        if i < len(z_steps):
            signal(relay.at[4 + i], z_pair(z_steps[i]))

    def relay_wait(i):
        pl.semaphore_wait(relay.at[i], 2 if i <= 2 else 1)
        if i < len(z_steps) - 1:
            pl.semaphore_wait(relay.at[4 + i], 2)

    def relay_end():
        pl.semaphore_wait(relay.at[4 + len(z_steps) - 1], 2)

    def remote(src, dst, send, recv, target):
        return pltpu.make_async_remote_copy(
            src_ref=src, dst_ref=dst, send_sem=send, recv_sem=recv, device_id=target, device_id_type=MESH
        )

    load("vox", vox_hbm, vox_ref)
    load("src", src_hbm, src_ref)
    load("w2", w2_hbm, w2_ref)
    load("w1", w1_hbm, w1_ref)

    def iota(shape, dim):
        return lax.broadcasted_iota(jnp.int32, shape, dim)

    pairs = V // 2
    old = iota((n, n), 0)
    parity, rest = old // (n // 2), old % (n // 2)
    order = jnp.where(rest // pairs * V + rest % pairs * 2 + parity == iota((n, n), 1), 1.0, 0.0).astype(BF16)

    def to_channels(ref):
        wide = ref[...].astype(F32)
        for j in range(pairs):
            turn[j * blocks : (j + 1) * blocks, :] = wide[:, j * 2 * C : (j + 1) * 2 * C]
        rows = jnp.concatenate([turn[pl.ds(b, pairs, stride=blocks), :] for b in range(blocks)], axis=0)
        lanes = rows.T
        both = jnp.concatenate([lanes[:C], lanes[C:]], axis=1).astype(BF16)
        return mxu(both, order).astype(BF16)

    def from_channels(value, out_ref):
        both = mxu(value, order, ((1,), (1,)))
        rows = jnp.concatenate([both[:, : n // 2], both[:, n // 2 :]], axis=0).T
        turn[...] = rows
        for j in range(pairs):
            flat[:, j * 2 * C : (j + 1) * 2 * C] = turn[pl.ds(j, blocks, stride=pairs), :]
        out_ref[...] = flat[...].astype(BF16)

    low_row = iota((1, 2 * V), 1) < V
    shift = blocks.bit_length() - 1

    def make_rows():
        for k in range(K):
            for b in range(blocks):
                source = src_ref[b, k]
                owner, place = source >> shift, source & (blocks - 1)
                slots[k * blocks + b] = jnp.where(
                    owner == s, place, jnp.where(owner < s, place + HALO, blocks + HALO + place)
                )
            start = k // 2 * 2 * V
            if start + 2 * V <= K * V:
                here = vox_ref[:, start : start + 2 * V]
            else:
                here = jnp.concatenate([vox_ref[:, start : start + V]] * 2, axis=1)
            there = pltpu.roll(here, V, 1)
            first, second = (here, there) if k % 2 == 0 else (there, here)
            for p in range(blocks // 2):
                row = jnp.where(low_row, first[2 * p : 2 * p + 1], second[2 * p + 1 : 2 * p + 2])
                none = row >= V
                base = jnp.where(low_row, slots[k * blocks + 2 * p] * V, slots[k * blocks + 2 * p + 1] * V)
                lanes = slice(p * 2 * V, (p + 1) * 2 * V)
                pair_rows[k, :, lanes] = jnp.where(none, -1, row + jnp.where(low_row, 0, V)).astype(F32)
                wide_rows[k, :, lanes] = jnp.where(none, -1, row + base).astype(F32)

    group_of = 9
    spot = iota((n, n), 0).astype(F32).astype(BF16)
    spot_pair = iota((2 * V, 2 * V), 0).astype(F32).astype(BF16)

    def hot(where, row):
        return jnp.where(where == row.astype(BF16), jnp.ones_like(where), jnp.zeros_like(where))

    def spread(w_ref, grad):
        for g in range(0, K, group_of):
            out = mxu(w_ref[g * C : (g + group_of) * C, :], grad).astype(BF16)
            back[g : g + group_of] = out.reshape(group_of, C, n)

    def scattered(lo):
        def some(g, total):
            for i in range(group_of):
                k = g * group_of + i
                total = total + mxu(back[k], hot(spot, wide_rows[k] - lo), ((1,), (1,)))
            return total

        return lax.fori_loop(0, K // group_of, some, jnp.zeros((C, n), F32))

    def spread_out(grad, side):
        def some(g, carry):
            for i in range(group_of):
                k = g * group_of + i
                out = mxu(grad, hot(spot, wide_rows[k] - side * n), ((1,), (1,)))
                spreads[k, :, side * n : (side + 1) * n] = out.astype(BF16)
            return carry

        lax.fori_loop(0, K // group_of, some, 0)

    def gathered_back(side):
        return mxu(w2p[:, 0 : K * C], spreads[0:K, :, side * n : (side + 1) * n].reshape(K * C, n))

    def pair_weights():
        for k in range(0, K_EVEN, 2):
            first = w2_ref[k * C : (k + 1) * C, :]
            second = w2_ref[(k + 1) * C : (k + 2) * C, :] if k + 1 < K else jnp.zeros_like(first)
            w2p[:, k * C : (k + 2) * C] = jnp.concatenate([first, second], axis=1)

    def weight_parts_wide(which, table):
        for g in range(0, K_EVEN, 4):
            out = mxu(table, spreads[g : g + 4].reshape(4 * C, 2 * n), ((1,), (1,))).astype(BF16)
            for j in range(2):
                rows = out[:, j * 2 * C : (j + 1) * 2 * C].reshape(C // TILE, TILE, 2 * C)
                first = (g // 2 + j) * (C // TILE)
                parts[which, first // pad, first % pad : first % pad + C // TILE] = rows

    low16 = iota((C, 2 * V), 1).astype(F32).astype(BF16) < V
    low32 = iota((C, 2 * V), 1) < V

    def fill(table, value, first):
        value = value.astype(F32)
        turned = pltpu.roll(value, V, 1)
        table[first] = jnp.where(low32, value, turned).astype(BF16)
        table[first + 1] = jnp.where(low32, turned, value).astype(BF16)

    def fill_own(table, value):
        for p in range(blocks // 2):
            fill(table, value[:, p * 2 * V : (p + 1) * 2 * V], 2 * p)

    def fill_halo(table, ref):
        for i in range(2):
            fill(table, ref[i], blocks + 2 * i)

    def pick(table, picked):
        for k in range(K):
            for p in range(blocks // 2):
                lanes = slice(p * 2 * V, (p + 1) * 2 * V)
                both = jnp.where(low16, table[slots[k * blocks + 2 * p]], table[slots[k * blocks + 2 * p + 1]])
                picked[k, :, lanes] = mxu(both, hot(spot_pair, pair_rows[k, :, lanes])).astype(BF16)

    def convolved(wt, picked):
        return mxu(wt[...], picked[...].reshape(K * C, n))

    def weight_parts(which, picked, grad):
        zero = jnp.zeros((C, n), BF16)
        pair = jnp.concatenate(
            [jnp.concatenate([grad, zero], axis=1), jnp.concatenate([zero, grad], axis=1)], axis=0
        )
        for g in range(0, K, group_of):
            both = jnp.concatenate(
                [picked[g : g + group_of, 0 : C // 2, :], picked[g : g + group_of, C // 2 : C, :]], axis=2
            ).reshape(group_of * C // 2, 2 * n)
            out = mxu(both, pair, ((1,), (1,))).astype(BF16)
            tiles = group_of * C // 2 // TILE
            out = out.reshape(tiles, TILE, 2 * C)
            first = g * C // 2 // TILE
            cut = min(max(pad - first, 0), tiles)
            if cut > 0:
                parts[which, 0, first : first + cut] = out[:cut]
            if cut < tiles:
                parts[which, 1, first + cut - pad : first + tiles - pad] = out[cut:]

    class Batch:
        def __init__(self, copies, send, recv, sent, landed):
            for copy in copies:
                copy.start()
            self.all = remote(sent, landed, send, recv, twin)

        def wait_recv(self):
            self.all.wait_recv()

        def wait_send(self):
            self.all.wait_send()

    def to_neighbours(slot, low, high, into):
        send, recv = halo_send.at[slot], halo_recv.at[slot]
        copies = [remote(low, into.at[1], send, recv, before), remote(high, into.at[0], send, recv, after)]
        return [Batch(copies, send, recv, into, into)]

    def arrive(copies):
        for copy in copies:
            copy.wait_recv()

    offsets = [
        (dx, dy, dz) for dx in range(n_x) for dy in range(n_y) for dz in range(ZPAR) if (dx, dy, dz) != (0, 0, 0)
    ]
    offsets.sort(key=lambda o: -(min(o[0], n_x - o[0]) + min(o[1], n_y - o[1]) + o[2]))

    def member(x, y, z):
        return (z * n_y + y) * n_x + x

    me = member(x, y, z_par)

    def to_twin(stage, which, src, dst):
        copy = remote(src, dst, pair_send.at[stage, which], pair_recv.at[stage, which], twin)
        copy.start()
        return [copy]

    def to_members(stage, which, src_of, dst, all_of):
        send, recv = group_send.at[stage, which], group_recv.at[stage, which]
        copies = []
        for dx, dy, dz in offsets:
            xx, yy, zz = (x + dx) % n_x, (y + dy) % n_y, (z_par + dz) % ZPAR
            target = (((z // ZPAR) * ZPAR + zz) * n_y + yy, xx * CORES + core)
            copies.append(remote(src_of(member(xx, yy, zz)), dst, send, recv, target))
        return [Batch(copies, send, recv, all_of, all_of)]

    owners = -(-pad // per)

    class Gather:
        def __init__(self, which, mine):
            send, recv = group_send.at[1, which], group_recv.at[1, which]

            def some(count):
                ref = sums.at[which, core, 0 : count * per]
                return remote(ref, ref, send, recv, twin)

            self.out, self.few, self.many = some(len(offsets)), some(owners - 1), some(owners)
            copies = []
            for dx, dy, dz in offsets:
                xx, yy, zz = (x + dx) % n_x, (y + dy) % n_y, (z_par + dz) % ZPAR
                target = (((z // ZPAR) * ZPAR + zz) * n_y + yy, xx * CORES + core)
                copies.append(remote(mine, mine, send, recv, target))

            @pl.when(me < owners)
            def _():
                for copy in copies:
                    copy.start()

        def wait_recv(self):
            @pl.when(me < owners)
            def _():
                self.few.wait_recv()

            @pl.when(me >= owners)
            def _():
                self.many.wait_recv()

        def wait_send(self):
            @pl.when(me < owners)
            def _():
                self.out.wait_send()

    def to_depths(which, src, dst):
        send, recv = deep_send.at[which], deep_recv.at[which]
        copies = []
        for j in [j for i in range(deep // 2, 0, -1) for j in sorted({i, deep - i})]:
            copies.append(remote(src, dst, send, recv, at(dz=j * ZPAR)))
        every = got3.at[which, 0 : deep - 1]
        return [Batch(copies, send, recv, every, every)]

    spreads[K:] = jnp.zeros((K_EVEN - K, C, 2 * n), BF16)
    used = K * C // 2 // TILE - pad
    parts[0, 1, used:] = jnp.zeros((pad - used, TILE, 2 * C), BF16)
    for which in range(2):
        mid[which, pad:] = jnp.zeros((mid.shape[1] - pad, TILE, 2 * C), BF16)
    loads["x"].wait()
    feat = to_channels(x_ref)
    feat_ref[...] = feat
    loads["ct"].wait()
    cot = to_channels(ct_ref)
    pl.semaphore_wait(barrier, len(near))
    feat_copies = to_neighbours(0, feat_ref.at[:, 0:half], feat_ref.at[:, half:n], halo_in)
    relay_signal(0)
    sent = list(feat_copies)

    loads["vox"].wait()
    loads["src"].wait()
    make_rows()
    spread_out(cot, 1)
    loads["w2"].wait()
    pair_weights()
    rim = gathered_back(1).astype(BF16)
    for i in range(2):
        rim_out[0, i] = rim[:, i * half : (i + 1) * half]
    rim_copies = to_neighbours(1, rim_out.at[0, 0], rim_out.at[0, 1], rim_in.at[0])
    sent += rim_copies
    relay_wait(0)
    relay_signal(1)
    loads["w1"].wait()
    w1t[...] = w1_ref[...].T
    fill_own(table1, feat)

    arrive(feat_copies)
    fill_halo(table1, halo_in)
    pick(table1, picked1)
    pre = convolved(w1t, picked1)
    sig = 1.0 / (1.0 + jnp.exp(-pre))
    hid = (pre * sig).astype(BF16)
    hidden[...] = hid
    hid_copies = to_neighbours(2, hidden.at[:, 0:half], hidden.at[:, half:n], halo_mid)
    sent += hid_copies
    relay_wait(1)
    relay_signal(2)

    spread_out(cot, 0)
    grad_hidden = gathered_back(0)
    arrive(rim_copies)
    rims = jnp.concatenate([rim_in[0, 0], rim_in[0, 1]], axis=1).astype(F32)
    grad_pre = ((grad_hidden + rims) * (sig * (1.0 + pre * (1.0 - sig)))).astype(BF16)
    weight_parts(0, picked1, grad_pre)

    def mine_of(which):
        return sums.at[which, core, pl.ds(me * per, per)]

    def reduce_pair(which):
        return to_twin(0, which, parts.at[which, 1 - core], got1.at[which])

    def scatter_reduce(which, copies):
        arrive(copies)
        mid[which, 0:pad] = (parts[which, core].astype(F32) + got1[which].astype(F32)).astype(BF16)
        got2[which, me] = mid[which, pl.ds(me * per, per)]
        every = got2.at[which, 0 : len(offsets)]
        return to_members(
            0, which, lambda other: mid.at[which, pl.ds(other * per, per)], got2.at[which, me], every
        )

    def added(ref, which, count):
        totals = [ref[which, i].astype(F32) for i in range(count)]
        while len(totals) > 1:
            totals = [a + b for a, b in zip(totals[::2], totals[1::2])]
        return totals[0].astype(BF16)

    def reduce_deep(which, copies):
        arrive(copies)
        got3[which, depth] = added(got2, which, len(offsets) + 1)
        mine = got3.at[which, depth]
        return to_depths(which, mine, mine)

    def gather_members(which, copies):
        arrive(copies)
        sums[which, core, pl.ds(me * per, per)] = added(got3, which, deep)
        mine = mine_of(which)
        return [Gather(which, mine)]

    def gather_pair(which, copies):
        arrive(copies)
        mine = sums.at[which, core, 0:pad]
        return to_twin(1, which, mine, mine)

    factor = float(n_x * CORES * space * n) ** (-0.5)

    def lay_out(which, side, out):
        for i in range(pad):
            tile = side * pad + i
            value = sums[which, side, i].astype(F32) * factor
            if which == 0:
                k, top = tile // 2, pl.multiple_of(tile % 2 * TILE, TILE)
                out[k, pl.ds(top, TILE), :] = value[:, :C]
                out[k, pl.ds(top + C // 2, TILE), :] = value[:, C:]
            else:
                k, top = tile // 4 * 2, pl.multiple_of(tile % 4 * TILE, TILE)
                out[k, pl.ds(top, TILE), :] = value[:, :C]
                out[k + 1, pl.ds(top, TILE), :] = value[:, C:]

    def drain(copies):
        for copy in copies:
            copy.wait_send()

    one = reduce_pair(0)
    sent += one
    spread(w1_ref, grad_pre)
    relay_wait(2)
    relay_signal(3)
    w2t[...] = w2_ref[...].T
    relay_wait(3)
    one = scatter_reduce(0, one)
    sent += one
    arrive(hid_copies)
    weight_parts_wide(1, jnp.concatenate([hid, halo_mid[0], halo_mid[1]], axis=1))
    two = reduce_pair(1)
    sent += two

    two = scatter_reduce(1, two)
    sent += two
    rim = scattered(n).astype(BF16)
    for i in range(2):
        rim_out[1, i] = rim[:, i * half : (i + 1) * half]
    last_copies = to_neighbours(3, rim_out.at[1, 0], rim_out.at[1, 1], rim_in.at[1])
    sent += last_copies
    relay_end()
    one = reduce_deep(0, one)
    sent += one
    fill_own(table2, hid)
    fill_halo(table2, halo_mid)
    pick(table2, picked2)
    from_channels(convolved(w2t, picked2).astype(BF16), conv_ref)
    two = reduce_deep(1, two)
    sent += two
    grad_in = scattered(0)

    one = gather_members(0, one)
    sent += one
    arrive(last_copies)
    rims = jnp.concatenate([rim_in[1, 0], rim_in[1, 1]], axis=1).astype(F32)
    grad_input = (grad_in + rims).astype(BF16)
    two = gather_members(1, two)
    sent += two
    from_channels(grad_input, gin_ref)
    one = gather_pair(0, one)
    sent += one
    lay_out(0, core, grad1_ref)
    arrive(one)
    lay_out(0, 1 - core, grad1_ref)
    two = gather_pair(1, two)
    drain(sent)
    lay_out(1, core, grad2_ref)
    arrive(two)
    lay_out(1, 1 - core, grad2_ref)
    drain(two)


def put_kernel(*refs):
    count = len(refs) // 2
    sem = refs[-1]
    copies = []
    for i, (src, dst) in enumerate(zip(refs[:count], refs[count:-1])):
        size = dst.shape[0]
        cuts = 3 if size == K else 1
        for c in range(cuts):
            part = pl.ds(c * size // cuts, size // cuts)
            copies.append(pltpu.make_async_copy(src.at[part], dst.at[part], sem.at[i, c]))
    for copy in copies:
        copy.start()
    for copy in copies:
        copy.wait()


def per_device(sizes, features, sources, voxels, cotangent, weight_one, weight_two):
    n_x, n_y, n_z = sizes
    members = n_x * n_y * ZPAR
    deep = n_z // ZPAR
    blocks = features.shape[1]
    n = blocks * V
    half = n // 2
    pad = TILES // CORES
    per = -(-pad // members)
    slots = blocks + 2 * HALO
    scratch = [
        pltpu.VMEM((blocks, V * C), BF16),
        pltpu.VMEM((blocks, V * C), BF16),
        pltpu.SMEM((blocks, K), jnp.int32),
        pltpu.VMEM((blocks, K * V), jnp.int32),
        pltpu.VMEM((K * C, C), BF16),
        pltpu.VMEM((K * C, C), BF16),
        pltpu.SMEM((K * blocks,), jnp.int32),
        pltpu.VMEM((K, 1, n), F32),
        pltpu.VMEM((K, 1, n), F32),
        pltpu.VMEM((n // 2, 2 * C), F32),
        pltpu.VMEM((blocks, V * C), F32),
        pltpu.VMEM((slots, C, 2 * V), BF16),
        pltpu.VMEM((slots, C, 2 * V), BF16),
        pltpu.VMEM((C, n), BF16),
        pltpu.VMEM((K, C, n), BF16),
        pltpu.VMEM((K, C, n), BF16),
        pltpu.VMEM((K, C, n), BF16),
        pltpu.VMEM((K_EVEN, C, 2 * n), BF16),
        pltpu.VMEM((C, K_EVEN * C), BF16),
        pltpu.VMEM((C, K * C), BF16),
        pltpu.VMEM((C, K * C), BF16),
        pltpu.VMEM((2, C, half), BF16),
        pltpu.VMEM((2, C, half), BF16),
        pltpu.VMEM((2, 2, C, half), BF16),
        pltpu.VMEM((2, 2, C, half), BF16),
        pltpu.VMEM((C, n), BF16),
        pltpu.VMEM((2, CORES, pad, TILE, 2 * C), BF16),
        pltpu.VMEM((2, pad, TILE, 2 * C), BF16),
        pltpu.VMEM((2, members * per, TILE, 2 * C), BF16),
        pltpu.VMEM((2, members, per, TILE, 2 * C), BF16),
        pltpu.VMEM((2, deep, per, TILE, 2 * C), BF16),
        pltpu.VMEM((2, CORES, members * per, TILE, 2 * C), BF16),
        pltpu.SemaphoreType.DMA((6,)),
        pltpu.SemaphoreType.DMA((4,)),
        pltpu.SemaphoreType.DMA((4,)),
        pltpu.SemaphoreType.DMA((2, 2)),
        pltpu.SemaphoreType.DMA((2, 2)),
        pltpu.SemaphoreType.DMA((2, 2)),
        pltpu.SemaphoreType.DMA((2, 2)),
        pltpu.SemaphoreType.DMA((2,)),
        pltpu.SemaphoreType.DMA((2,)),
        pltpu.SemaphoreType.REGULAR((7,)),
    ]
    outs = (
        jax.ShapeDtypeStruct((blocks, V * C), BF16),
        jax.ShapeDtypeStruct((blocks, V * C), BF16),
        jax.ShapeDtypeStruct((K, C, C), F32),
        jax.ShapeDtypeStruct((K, C, C), F32),
    )
    vmem = pl.BlockSpec(memory_space=pltpu.VMEM)
    anywhere = pl.BlockSpec(memory_space=pl.ANY)
    hbm = pl.BlockSpec(memory_space=pltpu.HBM)
    even = jax.ShapeDtypeStruct((K_EVEN, C, C), F32)
    results = pl.pallas_call(
        functools.partial(step_kernel, sizes),
        out_shape=(*outs[:2], even, even),
        in_specs=[hbm] * 6,
        out_specs=(vmem,) * 4,
        scratch_shapes=scratch,
        compiler_params=pltpu.CompilerParams(
            collective_id=0, has_side_effects=True, vmem_limit_bytes=32 * 1024 * 1024
        ),
        name="step",
    )(
        *[
            pltpu.with_memory_space_constraint(a, pltpu.HBM)
            for a in (
                features[0],
                cotangent[0],
                sources[0],
                voxels[0],
                weight_one.reshape(K * C, C),
                weight_two.reshape(K * C, C),
            )
        ]
    )
    conv, gin, grad_one, grad_two = pl.pallas_call(
        put_kernel,
        out_shape=outs,
        in_specs=[anywhere] * 4,
        out_specs=(hbm,) * 4,
        scratch_shapes=[pltpu.SemaphoreType.DMA((4, 3))],
        compiler_params=pltpu.CompilerParams(vmem_limit_bytes=1024 * 1024),
        name="put",
    )(*results)
    return conv[None], gin[None], grad_one, grad_two


def solution(mesh):
    space, dp = mesh.shape["space"], mesh.shape["dp"]
    sizes = (dp // CORES, Y, space // Y)
    wide = P("dp", "space", None)
    return jax.shard_map(
        functools.partial(per_device, sizes),
        mesh=mesh,
        in_specs=(wide, wide, wide, wide, P(), P()),
        out_specs=(wide, wide, P(), P()),
        check_vma=False,
    )
```
